128 devices in a mesh: tm: 8 (over x, y_hi), space: 16 (over z, y_lo, core).
Axes of the slice: x: 4, y: 4 (y_hi: 2, y_lo: 2; y = y_hi * 2 + y_lo), z: 4, core: 2. Of those that a mesh axis runs over, the one named last changes fastest.
Arguments:
- potential: float32 [64, 64, 128, 128], P('tm', 'space'), may hold values from -6 to 6
- multiplier: float32 [4, 64, 64, 128, 128], P(None, 'tm', 'space'), may hold values from -12 to 12
- start_density: float32 [64, 128, 128], P('space'), may hold values from 0.1 to 1
- final_density: float32 [64, 128, 128], P('space'), may hold values from 0.1 to 1
Outputs:
- next_potential: float32 [64, 64, 128, 128], P('tm', 'space')
- next_multiplier: float32 [4, 64, 64, 128, 128], P(None, 'tm', 'space')
The draws below stay inside these ranges and needn't reach their ends.
All inputs are finite; a program needn't handle non-finite values.
Results may differ from the reference program's by a relative error of at most 0.0003.
Values sent between devices are 32-bit elements; how exact they have to be, the bound alone decides.
A program may use at most 128 MiB of HBM per device.

```python
import math
import jax
import jax.numpy as jnp
from jax import lax

NT = 64
NX = 64
NY = 128
NZ = 128
NEWTON = 10


def level_of(stream_key, extent, shards, smallest, top_value):
    def one(position, blocks):
        steps = jax.random.uniform(jax.random.fold_in(jax.random.fold_in(stream_key, 6), position), (blocks,), jnp.float32, smallest / len(shards), top_value / len(shards))
        return jnp.repeat(jnp.exp(steps), extent[position] // blocks).reshape((-1,) + (1,) * (len(extent) - position - 1))

    level = one(*shards[0])
    for cut in shards[1:]:
        level = level * one(*cut)
    return level


def normal_values(rng, extent, scale, reach, shards=(), kind=jnp.bfloat16):
    drawn = scale * jax.random.normal(rng, extent, jnp.float32)
    if shards:
        drawn = drawn * level_of(rng, extent, shards, -0.22, 0.18)
    return jnp.clip(drawn, -reach, reach).astype(kind)


def setup_inputs(seed: int = 0) -> dict:
    keys = jax.random.split(jax.random.key(seed), 5)
    potential = normal_values(keys[0], (NT, NX, NY, NZ), 1.0, 6.0, ((0, 8), (1, 16)), jnp.float32)
    multiplier = normal_values(keys[1], (4, NT, NX, NY, NZ), 2.0, 12.0, ((1, 8), (2, 16)), jnp.float32)
    start_density = jnp.clip(jnp.exp(math.log(1.0) - 2.3025851 * jax.random.uniform(keys[2], (NX, NY, NZ), jnp.float32) ** level_of(keys[2], (NX, NY, NZ), ((0, 16),), -0.2, 0.2)), 0.1, 1.0)
    final_density = jnp.clip(jnp.exp(math.log(1.0) - 2.3025851 * jax.random.uniform(keys[3], (NX, NY, NZ), jnp.float32) ** level_of(keys[3], (NX, NY, NZ), ((0, 16),), -0.2, 0.2)), 0.1, 1.0)
    return dict(potential=potential, multiplier=multiplier, start_density=start_density, final_density=final_density)


RATE = 4.0
PROX = 0.01

def cosine_table(length):
    freq = jnp.arange(length, dtype=jnp.float32)[:, None]
    place = jnp.arange(length, dtype=jnp.float32)[None, :]
    weight = jnp.where(freq == 0.0, jnp.sqrt(jnp.float32(0.5)), jnp.float32(1.0))
    return jnp.sqrt(jnp.float32(2.0) / length) * weight * jnp.cos(jnp.pi * freq * (place + 0.5) / length)

def eigen(length):
    freq = jnp.arange(length, dtype=jnp.float32)
    return 4.0 * jnp.square(jnp.sin(jnp.pi * freq / (2.0 * length)))

def forward_diff(field, axis):
    size = field.shape[axis]
    upper = lax.slice_in_dim(field, 1, size, axis=axis)
    lower = lax.slice_in_dim(field, 0, size - 1, axis=axis)
    edge = jnp.zeros_like(lax.slice_in_dim(field, 0, 1, axis=axis))
    return jnp.concatenate([upper - lower, edge], axis=axis)

def adjoint(face, axis):
    size = face.shape[axis]
    inner = lax.slice_in_dim(face, 0, size - 1, axis=axis)
    edge = jnp.zeros_like(lax.slice_in_dim(face, 0, 1, axis=axis))
    return jnp.concatenate([edge, inner], axis=axis) - jnp.concatenate([inner, edge], axis=axis)

def project(target):
    lead = target[0]
    side = target[1:]
    wsq = lax.optimization_barrier(jnp.sum(side * side, axis=0))
    excess = lead + 0.5 * wsq
    stretch = jnp.maximum(1.0, lead + 1.0)
    for step in range(NEWTON):
        resid = stretch - (lead + 1.0) - 0.5 * wsq / (stretch * stretch)
        slope = 1.0 + wsq / (stretch * stretch * stretch)
        stretch = jnp.maximum(1.0, stretch - resid / slope)
    inside = excess <= 0.0
    new_lead = jnp.where(inside, lead, lead - (stretch - 1.0))
    new_side = jnp.where(inside[None], side, side / stretch[None])
    return jnp.concatenate([new_lead[None], new_side], axis=0)

def reference(potential, multiplier, start_density, final_density):
    high = lax.Precision.HIGHEST
    gradient = jnp.stack([forward_diff(potential, axis) for axis in range(4)])
    projected = project(gradient + multiplier / RATE)
    next_multiplier = multiplier + RATE * (gradient - projected)
    flux = next_multiplier - RATE * projected
    right_side = -(adjoint(flux[0], 0) + adjoint(flux[1], 1) + adjoint(flux[2], 2) + adjoint(flux[3], 3))
    right_side = right_side + PROX * potential
    right_side = right_side.at[0].add(start_density)
    right_side = right_side.at[NT - 1].add(-final_density)
    cos_t = cosine_table(NT)
    cos_x = cosine_table(NX)
    cos_y = cosine_table(NY)
    cos_z = cosine_table(NZ)
    hat = jnp.einsum('ki,ixyz->kxyz', cos_t, right_side, precision=high)
    hat = jnp.einsum('ki,tiyz->tkyz', cos_x, hat, precision=high)
    hat = jnp.einsum('ki,txiz->txkz', cos_y, hat, precision=high)
    hat = jnp.einsum('ki,txyi->txyk', cos_z, hat, precision=high)
    denom = eigen(NT)[:, None, None, None] + eigen(NX)[None, :, None, None]
    denom = denom + eigen(NY)[None, None, :, None] + eigen(NZ)[None, None, None, :]
    hat = hat / (RATE * denom + PROX)
    hat = jnp.einsum('ik,kxyz->ixyz', cos_t, hat, precision=high)
    hat = jnp.einsum('ik,tkyz->tiyz', cos_x, hat, precision=high)
    hat = jnp.einsum('ik,txkz->txiz', cos_y, hat, precision=high)
    next_potential = jnp.einsum('ik,txyk->txyi', cos_z, hat, precision=high)
    return (next_potential, next_multiplier)
```

```python
import jax
import jax.numpy as jnp
from jax import lax
from jax.sharding import PartitionSpec as P

NEWTON = 10


RATE = 4.0
PROX = 0.01


def from_behind(block, axis, distance):
    devices = range(lax.axis_size(axis))
    route = [(i - distance, i) for i in devices if i - distance in devices]
    return lax.ppermute(block, axis, route)


def cosine_table(length):
    freq = jnp.arange(length, dtype=jnp.float32)[:, None]
    place = jnp.arange(length, dtype=jnp.float32)[None, :]
    weight = jnp.where(freq == 0.0, jnp.sqrt(jnp.float32(0.5)), jnp.float32(1.0))
    return (
        jnp.sqrt(jnp.float32(2.0) / length)
        * weight
        * jnp.cos(jnp.pi * freq * (place + 0.5) / length)
    )


def eigen_at(length, freq):
    return 4.0 * jnp.square(jnp.sin(jnp.pi * freq / (2.0 * length)))


def adjoint(face, axis):
    size = face.shape[axis]
    inner = lax.slice_in_dim(face, 0, size - 1, axis=axis)
    edge = jnp.zeros_like(lax.slice_in_dim(face, 0, 1, axis=axis))
    return jnp.concatenate([edge, inner], axis=axis) - jnp.concatenate([inner, edge], axis=axis)


def local_diff(field, axis):
    size = field.shape[axis]
    upper = lax.slice_in_dim(field, 1, size, axis=axis)
    lower = lax.slice_in_dim(field, 0, size - 1, axis=axis)
    edge = jnp.zeros_like(lax.slice_in_dim(field, 0, 1, axis=axis))
    return jnp.concatenate([upper - lower, edge], axis=axis)


def project(target):
    lead = target[0]
    side = target[1:]
    wsq = jnp.sum(side * side, axis=0)
    excess = lead + 0.5 * wsq
    stretch = jnp.maximum(1.0, lead + 1.0)
    shifted = lead + 1.0
    half_again = 1.5 * wsq
    for step in range(NEWTON):
        square = stretch * stretch
        cube = square * stretch
        stretch = jnp.maximum(1.0, stretch * (shifted * square + half_again) / (cube + wsq))
    inside = excess <= 0.0
    new_lead = jnp.where(inside, lead, lead - (stretch - 1.0))
    shrink = 1.0 / stretch
    new_side = jnp.where(inside[None], side, side * shrink[None])
    return jnp.concatenate([new_lead[None], new_side], axis=0)


def body(potential, multiplier, start_density, final_density):
    high = lax.Precision.HIGHEST
    steps_t, rows_x, width_y, width_z = potential.shape
    n_tm = lax.axis_size("tm")
    n_sp = lax.axis_size("space")
    total_t = steps_t * n_tm
    total_x = rows_x * n_sp
    block_y = width_y // (n_tm * n_sp)
    time_at = lax.axis_index("tm") * steps_t + jnp.arange(steps_t)
    row_at = lax.axis_index("space") * rows_x + jnp.arange(rows_x)
    not_last_t = (time_at < total_t - 1)[:, None, None, None]
    not_last_x = (row_at < total_x - 1)[None, :, None, None]
    ahead_t = from_behind(potential[:1], "tm", -1)
    ahead_x = from_behind(potential[:, :1], "space", -1)
    later = jnp.concatenate([potential[1:], ahead_t], axis=0)
    beside = jnp.concatenate([potential[:, 1:], ahead_x], axis=1)
    grad_t = jnp.where(not_last_t, later - potential, 0.0)
    grad_x = jnp.where(not_last_x, beside - potential, 0.0)
    gradient = jnp.stack([grad_t, grad_x, local_diff(potential, 2), local_diff(potential, 3)])
    projected = project(gradient + multiplier / RATE)
    next_multiplier = multiplier + RATE * (gradient - projected)
    flux = next_multiplier - RATE * projected
    rest = -(adjoint(flux[2], 2) + adjoint(flux[3], 3)) + PROX * potential
    first_step = (time_at == 0)[:, None, None, None]
    last_step = (time_at == total_t - 1)[:, None, None, None]
    rest = (
        rest
        + jnp.where(first_step, start_density[None], 0.0)
        - jnp.where(last_step, final_density[None], 0.0)
    )
    behind_t = from_behind(flux[0][-1:], "tm", 1)
    behind_x = from_behind(flux[1][:, -1:], "space", 1)
    flow_t = jnp.where(not_last_t, flux[0], 0.0)
    flow_x = jnp.where(not_last_x, flux[1], 0.0)
    div_t = jnp.concatenate([behind_t, flux[0][:-1]], axis=0) - flow_t
    div_x = jnp.concatenate([behind_x, flux[1][:, :-1]], axis=1) - flow_x
    payload = (rest - div_t - div_x)[None]
    cos_y = cosine_table(width_y)
    cos_z = cosine_table(width_z)
    payload = jnp.einsum("ctxyi,ki->ctxyk", payload, cos_z, precision=high)
    payload = jnp.einsum("ctxiz,ki->ctxkz", payload, cos_y, precision=high)
    both = ("tm", "space")
    middle = lax.all_to_all(payload[0], both, split_axis=2, concat_axis=0, tiled=True)
    middle = middle.reshape(n_tm, n_sp, steps_t, rows_x, block_y, width_z)
    cos_t = cosine_table(total_t).reshape(total_t, n_tm, steps_t)
    cos_x = cosine_table(total_x).reshape(total_x, n_sp, rows_x)
    hat = jnp.einsum("kat,abtxyz->kbxyz", cos_t, middle, precision=high)
    hat = jnp.einsum("jbx,kbxyz->kjyz", cos_x, hat, precision=high)
    freq_y = (
        (lax.axis_index("tm") * n_sp + lax.axis_index("space")) * block_y + jnp.arange(block_y)
    ).astype(jnp.float32)
    eig_t = eigen_at(total_t, jnp.arange(total_t, dtype=jnp.float32))
    eig_x = eigen_at(total_x, jnp.arange(total_x, dtype=jnp.float32))
    eig_y = eigen_at(width_y, freq_y)
    eig_z = eigen_at(width_z, jnp.arange(width_z, dtype=jnp.float32))
    denom = eig_t[:, None, None, None] + eig_x[None, :, None, None]
    denom = denom + eig_y[None, None, :, None] + eig_z[None, None, None, :]
    hat = hat / (RATE * denom + PROX)
    hat = jnp.einsum("atk,kjyz->atjyz", cos_t.reshape(n_tm, steps_t, total_t), hat, precision=high)
    solved = jnp.einsum("bxj,atjyz->abtxyz", cos_x.reshape(n_sp, rows_x, total_x), hat, precision=high)
    solved = solved.reshape(n_tm * n_sp * steps_t, rows_x, block_y, width_z)
    local = lax.all_to_all(solved, both, split_axis=0, concat_axis=2, tiled=True)
    local = jnp.einsum("ik,txkz->txiz", cos_y, local, precision=high)
    next_potential = jnp.einsum("ik,txyk->txyi", cos_z, local, precision=high)
    return (next_potential, next_multiplier)


def solution(mesh):
    in_specs = (
        P("tm", "space", None, None),
        P(None, "tm", "space", None, None),
        P("space", None, None),
        P("space", None, None),
    )
    out_specs = (P("tm", "space", None, None), P(None, "tm", "space", None, None))
    return jax.shard_map(body, mesh=mesh, in_specs=in_specs, out_specs=out_specs, check_vma=False)
```

```python
import functools

import jax
import jax.numpy as jnp
from jax import lax
from jax.sharding import PartitionSpec as P
from jax.experimental import pallas as pl
from jax.experimental.pallas import tpu as pltpu

NEWTON = 10


RATE = 4.0
PROX = 0.01


def from_behind(block, axis, distance):
    devices = range(lax.axis_size(axis))
    route = [(i - distance, i) for i in devices if i - distance in devices]
    return lax.ppermute(block, axis, route)


def cosine_table(length):
    freq = jnp.arange(length, dtype=jnp.float32)[:, None]
    place = jnp.arange(length, dtype=jnp.float32)[None, :]
    weight = jnp.where(freq == 0.0, jnp.sqrt(jnp.float32(0.5)), jnp.float32(1.0))
    return (
        jnp.sqrt(jnp.float32(2.0) / length)
        * weight
        * jnp.cos(jnp.pi * freq * (place + 0.5) / length)
    )


def eigen_at(length, freq):
    return 4.0 * jnp.square(jnp.sin(jnp.pi * freq / (2.0 * length)))


def adjoint(face, axis):
    size = face.shape[axis]
    inner = lax.slice_in_dim(face, 0, size - 1, axis=axis)
    edge = jnp.zeros_like(lax.slice_in_dim(face, 0, 1, axis=axis))
    return jnp.concatenate([edge, inner], axis=axis) - jnp.concatenate([inner, edge], axis=axis)


def local_diff(field, axis):
    size = field.shape[axis]
    upper = lax.slice_in_dim(field, 1, size, axis=axis)
    lower = lax.slice_in_dim(field, 0, size - 1, axis=axis)
    edge = jnp.zeros_like(lax.slice_in_dim(field, 0, 1, axis=axis))
    return jnp.concatenate([upper - lower, edge], axis=axis)


def project(target):
    lead = target[0]
    side = target[1:]
    wsq = jnp.sum(side * side, axis=0)
    excess = lead + 0.5 * wsq
    stretch = jnp.maximum(1.0, lead + 1.0)
    shifted = lead + 1.0
    half_again = 1.5 * wsq
    for step in range(NEWTON):
        square = stretch * stretch
        cube = square * stretch
        stretch = jnp.maximum(1.0, stretch * (shifted * square + half_again) / (cube + wsq))
    inside = excess <= 0.0
    new_lead = jnp.where(inside, lead, lead - (stretch - 1.0))
    shrink = 1.0 / stretch
    new_side = jnp.where(inside[None], side, side * shrink[None])
    return jnp.concatenate([new_lead[None], new_side], axis=0)


def cell_kernel(n_tm, n_sp, idx_ref, pc, pn, at, ax, m, sd, fd, nm_out, pay_out, ft_out, fx_out, ft_carry):
    t = pl.program_id(0)
    steps_t = pl.num_programs(0)
    rows_x, width_y, width_z = pc.shape[1], pc.shape[2], pc.shape[3]
    t_glob = idx_ref[0] * steps_t + t
    last_t = t_glob == n_tm * steps_t - 1
    last_x_dev = idx_ref[1] == n_sp - 1
    row = lax.broadcasted_iota(jnp.int32, (width_y, width_z), 0)
    col = lax.broadcasted_iota(jnp.int32, (width_y, width_z), 1)
    first_row = row == 0
    last_row = row == width_y - 1
    last_col = col == width_z - 1
    first_col = col == 0
    fx_prev = None
    for x in range(rows_x):
        p = pc[0, x]
        nxt = jnp.where(t == steps_t - 1, at[0, x], pn[0, x])
        grad_t = jnp.where(last_t, 0.0, nxt - p)
        if x < rows_x - 1:
            grad_x = pc[0, x + 1] - p
        else:
            grad_x = jnp.where(last_x_dev, 0.0, ax[0, 0] - p)
        grad_y = jnp.where(last_row, 0.0, pltpu.roll(p, width_y - 1, 0) - p)
        grad_z = jnp.where(last_col, 0.0, pltpu.roll(p, width_z - 1, 1) - p)
        grads = (grad_t, grad_x, grad_y, grad_z)
        mults = tuple(m[c, 0, x] for c in range(4))
        target = tuple(g + mu * (1.0 / RATE) for g, mu in zip(grads, mults))
        lead = target[0]
        wsq = target[1] * target[1] + target[2] * target[2] + target[3] * target[3]
        excess = lead + 0.5 * wsq
        shifted = lead + 1.0
        half_again = 1.5 * wsq
        stretch = jnp.maximum(1.0, shifted)
        for step in range(NEWTON):
            square = stretch * stretch
            cube = square * stretch
            stretch = jnp.maximum(1.0, stretch * (shifted * square + half_again) / (cube + wsq))
        inside = excess <= 0.0
        shrink = 1.0 / stretch
        proj = (jnp.where(inside, lead, lead - (stretch - 1.0)),) + tuple(
            jnp.where(inside, target[c], target[c] * shrink) for c in (1, 2, 3)
        )
        flux = []
        for c in range(4):
            nm = mults[c] + RATE * (grads[c] - proj[c])
            nm_out[c, 0, x] = nm
            flux.append(nm - RATE * proj[c])
        flow_y = jnp.where(first_row, 0.0, pltpu.roll(flux[2], 1, 0)) - jnp.where(last_row, 0.0, flux[2])
        flow_z = jnp.where(first_col, 0.0, pltpu.roll(flux[3], 1, 1)) - jnp.where(last_col, 0.0, flux[3])
        rest = PROX * p - (flow_y + flow_z)
        rest = rest + jnp.where(t_glob == 0, sd[x], 0.0) - jnp.where(last_t, fd[x], 0.0)
        ft_prev = jnp.where(t == 0, 0.0, ft_carry[x])
        div_t = ft_prev - jnp.where(last_t, 0.0, flux[0])
        ft_carry[x] = flux[0]
        ft_out[0, x] = flux[0]
        if x < rows_x - 1:
            fx_cur = flux[1]
        else:
            fx_cur = jnp.where(last_x_dev, 0.0, flux[1])
            fx_out[0, 0] = flux[1]
        div_x = -fx_cur if fx_prev is None else fx_prev - fx_cur
        fx_prev = flux[1]
        pay_out[0, x] = rest - div_t - div_x


def cells(potential, ahead_t, ahead_x, multiplier, start_density, final_density, n_tm, n_sp):
    steps_t, rows_x, width_y, width_z = potential.shape
    idx = jnp.stack([lax.axis_index("tm"), lax.axis_index("space")]).astype(jnp.int32)
    slab = (1, rows_x, width_y, width_z)
    f32 = jnp.float32
    grid_spec = pltpu.PrefetchScalarGridSpec(
        num_scalar_prefetch=1,
        grid=(steps_t,),
        in_specs=[
            pl.BlockSpec(slab, lambda t, s: (t, 0, 0, 0)),
            pl.BlockSpec(slab, lambda t, s: (jnp.minimum(t + 1, steps_t - 1), 0, 0, 0)),
            pl.BlockSpec(slab, lambda t, s: (0, 0, 0, 0)),
            pl.BlockSpec((1, 1, width_y, width_z), lambda t, s: (t, 0, 0, 0)),
            pl.BlockSpec((4, 1, rows_x, width_y, width_z), lambda t, s: (0, t, 0, 0, 0)),
            pl.BlockSpec((rows_x, width_y, width_z), lambda t, s: (0, 0, 0)),
            pl.BlockSpec((rows_x, width_y, width_z), lambda t, s: (0, 0, 0)),
        ],
        out_specs=[
            pl.BlockSpec((4, 1, rows_x, width_y, width_z), lambda t, s: (0, t, 0, 0, 0)),
            pl.BlockSpec(slab, lambda t, s: (t, 0, 0, 0)),
            pl.BlockSpec(slab, lambda t, s: (0, 0, 0, 0)),
            pl.BlockSpec((1, 1, width_y, width_z), lambda t, s: (t, 0, 0, 0)),
        ],
        scratch_shapes=[pltpu.VMEM((rows_x, width_y, width_z), f32)],
    )
    cells_n = potential.size
    return pl.pallas_call(
        functools.partial(cell_kernel, n_tm, n_sp),
        grid_spec=grid_spec,
        out_shape=[
            jax.ShapeDtypeStruct(multiplier.shape, f32),
            jax.ShapeDtypeStruct(potential.shape, f32),
            jax.ShapeDtypeStruct(slab, f32),
            jax.ShapeDtypeStruct((steps_t, 1, width_y, width_z), f32),
        ],
        compiler_params=pltpu.CompilerParams(dimension_semantics=("arbitrary",)),
        cost_estimate=pl.CostEstimate(
            flops=cells_n * 200, transcendentals=cells_n * 11, bytes_accessed=cells_n * 4 * 12
        ),
    )(idx, potential, potential, ahead_t, ahead_x, multiplier, start_density, final_density)


def body(potential, multiplier, start_density, final_density):
    high = lax.Precision.HIGHEST
    steps_t, rows_x, width_y, width_z = potential.shape
    n_tm = lax.axis_size("tm")
    n_sp = lax.axis_size("space")
    total_t = steps_t * n_tm
    total_x = rows_x * n_sp
    block_y = width_y // (n_tm * n_sp)
    time_at = lax.axis_index("tm") * steps_t + jnp.arange(steps_t)
    row_at = lax.axis_index("space") * rows_x + jnp.arange(rows_x)
    ahead_t = from_behind(potential[:1], "tm", -1)
    ahead_x = from_behind(potential[:, :1], "space", -1)
    next_multiplier, partial, flux_t_last, flux_x_last = cells(
        potential, ahead_t, ahead_x, multiplier, start_density, final_density, n_tm, n_sp
    )
    behind_t = from_behind(flux_t_last, "tm", 1)
    behind_x = from_behind(flux_x_last, "space", 1)
    cos_y = cosine_table(width_y)
    cos_z = cosine_table(width_z)
    payload = jnp.einsum("txyi,ki->txyk", partial, cos_z, precision=high)
    payload = jnp.einsum("txiz,ki->txkz", payload, cos_y, precision=high)
    edge_t = jnp.einsum("txyi,ki->txyk", behind_t, cos_z, precision=high)
    edge_t = jnp.einsum("txiz,ki->txkz", edge_t, cos_y, precision=high)
    edge_x = jnp.einsum("txyi,ki->txyk", behind_x, cos_z, precision=high)
    edge_x = jnp.einsum("txiz,ki->txkz", edge_x, cos_y, precision=high)
    payload = payload.at[:, :1].add(-edge_x)
    payload = payload.at[:1].add(-edge_t)
    both = ("tm", "space")
    middle = lax.all_to_all(payload, both, split_axis=2, concat_axis=0, tiled=True)
    middle = middle.reshape(n_tm, n_sp, steps_t, rows_x, block_y, width_z)
    cos_t = cosine_table(total_t).reshape(total_t, n_tm, steps_t)
    cos_x = cosine_table(total_x).reshape(total_x, n_sp, rows_x)
    hat = jnp.einsum("kat,abtxyz->kbxyz", cos_t, middle, precision=high)
    hat = jnp.einsum("jbx,kbxyz->kjyz", cos_x, hat, precision=high)
    freq_y = (
        (lax.axis_index("tm") * n_sp + lax.axis_index("space")) * block_y + jnp.arange(block_y)
    ).astype(jnp.float32)
    eig_t = eigen_at(total_t, jnp.arange(total_t, dtype=jnp.float32))
    eig_x = eigen_at(total_x, jnp.arange(total_x, dtype=jnp.float32))
    eig_y = eigen_at(width_y, freq_y)
    eig_z = eigen_at(width_z, jnp.arange(width_z, dtype=jnp.float32))
    denom = eig_t[:, None, None, None] + eig_x[None, :, None, None]
    denom = denom + eig_y[None, None, :, None] + eig_z[None, None, None, :]
    hat = hat / (RATE * denom + PROX)
    hat = jnp.einsum("atk,kjyz->atjyz", cos_t.reshape(n_tm, steps_t, total_t), hat, precision=high)
    solved = jnp.einsum("bxj,atjyz->abtxyz", cos_x.reshape(n_sp, rows_x, total_x), hat, precision=high)
    solved = solved.reshape(n_tm * n_sp * steps_t, rows_x, block_y, width_z)
    local = lax.all_to_all(solved, both, split_axis=0, concat_axis=2, tiled=True)
    local = jnp.einsum("ik,txkz->txiz", cos_y, local, precision=high)
    next_potential = jnp.einsum("ik,txyk->txyi", cos_z, local, precision=high)
    return (next_potential, next_multiplier)


def solution(mesh):
    in_specs = (
        P("tm", "space", None, None),
        P(None, "tm", "space", None, None),
        P("space", None, None),
        P("space", None, None),
    )
    out_specs = (P("tm", "space", None, None), P(None, "tm", "space", None, None))
    return jax.shard_map(body, mesh=mesh, in_specs=in_specs, out_specs=out_specs, check_vma=False)
```

```python
import functools

import jax
import jax.numpy as jnp
from jax import lax
from jax.sharding import PartitionSpec as P
from jax.experimental import pallas as pl
from jax.experimental.pallas import tpu as pltpu

NEWTON = 10


RATE = 4.0
PROX = 0.01


def from_behind(block, axis, distance):
    devices = range(lax.axis_size(axis))
    route = [(i - distance, i) for i in devices if i - distance in devices]
    return lax.ppermute(block, axis, route)


def cosine_table(length):
    freq = jnp.arange(length, dtype=jnp.float32)[:, None]
    place = jnp.arange(length, dtype=jnp.float32)[None, :]
    weight = jnp.where(freq == 0.0, jnp.sqrt(jnp.float32(0.5)), jnp.float32(1.0))
    return (
        jnp.sqrt(jnp.float32(2.0) / length)
        * weight
        * jnp.cos(jnp.pi * freq * (place + 0.5) / length)
    )


def eigen_at(length, freq):
    return 4.0 * jnp.square(jnp.sin(jnp.pi * freq / (2.0 * length)))


def adjoint(face, axis):
    size = face.shape[axis]
    inner = lax.slice_in_dim(face, 0, size - 1, axis=axis)
    edge = jnp.zeros_like(lax.slice_in_dim(face, 0, 1, axis=axis))
    return jnp.concatenate([edge, inner], axis=axis) - jnp.concatenate([inner, edge], axis=axis)


def local_diff(field, axis):
    size = field.shape[axis]
    upper = lax.slice_in_dim(field, 1, size, axis=axis)
    lower = lax.slice_in_dim(field, 0, size - 1, axis=axis)
    edge = jnp.zeros_like(lax.slice_in_dim(field, 0, 1, axis=axis))
    return jnp.concatenate([upper - lower, edge], axis=axis)


def project(target):
    lead = target[0]
    side = target[1:]
    wsq = jnp.sum(side * side, axis=0)
    excess = lead + 0.5 * wsq
    stretch = jnp.maximum(1.0, lead + 1.0)
    shifted = lead + 1.0
    half_again = 1.5 * wsq
    for step in range(NEWTON):
        square = stretch * stretch
        cube = square * stretch
        stretch = jnp.maximum(1.0, stretch * (shifted * square + half_again) / (cube + wsq))
    inside = excess <= 0.0
    new_lead = jnp.where(inside, lead, lead - (stretch - 1.0))
    shrink = 1.0 / stretch
    new_side = jnp.where(inside[None], side, side * shrink[None])
    return jnp.concatenate([new_lead[None], new_side], axis=0)


def cell_kernel(n_tm, n_sp, idx_ref, pc, pn, at, ax, m, sd, fd, nm_out, pay_out, ft_out, fx_out, ft_carry):
    t = pl.program_id(0)
    steps_t = pl.num_programs(0)
    rows_x, width_y, width_z = pc.shape[1], pc.shape[2], pc.shape[3]
    t_glob = idx_ref[0] * steps_t + t
    last_t = t_glob == n_tm * steps_t - 1
    last_x_dev = idx_ref[1] == n_sp - 1
    row = lax.broadcasted_iota(jnp.int32, (width_y, width_z), 0)
    col = lax.broadcasted_iota(jnp.int32, (width_y, width_z), 1)
    first_row = row == 0
    last_row = row == width_y - 1
    last_col = col == width_z - 1
    first_col = col == 0
    fx_prev = None
    for x in range(rows_x):
        p = pc[0, x]
        nxt = jnp.where(t == steps_t - 1, at[0, x], pn[0, x])
        grad_t = jnp.where(last_t, 0.0, nxt - p)
        if x < rows_x - 1:
            grad_x = pc[0, x + 1] - p
        else:
            grad_x = jnp.where(last_x_dev, 0.0, ax[0, 0] - p)
        grad_y = jnp.where(last_row, 0.0, pltpu.roll(p, width_y - 1, 0) - p)
        grad_z = jnp.where(last_col, 0.0, pltpu.roll(p, width_z - 1, 1) - p)
        grads = (grad_t, grad_x, grad_y, grad_z)
        mults = tuple(m[c, 0, x] for c in range(4))
        target = tuple(g + mu * (1.0 / RATE) for g, mu in zip(grads, mults))
        lead = target[0]
        wsq = target[1] * target[1] + target[2] * target[2] + target[3] * target[3]
        excess = lead + 0.5 * wsq
        shifted = lead + 1.0
        half_again = 1.5 * wsq
        stretch = jnp.maximum(1.0, shifted)
        for step in range(NEWTON):
            square = stretch * stretch
            cube = square * stretch
            stretch = jnp.maximum(1.0, stretch * (shifted * square + half_again) / (cube + wsq))
        inside = excess <= 0.0
        shrink = 1.0 / stretch
        proj = (jnp.where(inside, lead, lead - (stretch - 1.0)),) + tuple(
            jnp.where(inside, target[c], target[c] * shrink) for c in (1, 2, 3)
        )
        flux = []
        for c in range(4):
            nm = mults[c] + RATE * (grads[c] - proj[c])
            nm_out[c, 0, x] = nm
            flux.append(nm - RATE * proj[c])
        flow_y = jnp.where(first_row, 0.0, pltpu.roll(flux[2], 1, 0)) - jnp.where(last_row, 0.0, flux[2])
        flow_z = jnp.where(first_col, 0.0, pltpu.roll(flux[3], 1, 1)) - jnp.where(last_col, 0.0, flux[3])
        rest = PROX * p - (flow_y + flow_z)
        rest = rest + jnp.where(t_glob == 0, sd[x], 0.0) - jnp.where(last_t, fd[x], 0.0)
        ft_prev = jnp.where(t == 0, 0.0, ft_carry[x])
        div_t = ft_prev - jnp.where(last_t, 0.0, flux[0])
        ft_carry[x] = flux[0]
        ft_out[0, x] = flux[0]
        if x < rows_x - 1:
            fx_cur = flux[1]
        else:
            fx_cur = jnp.where(last_x_dev, 0.0, flux[1])
            fx_out[0, 0] = flux[1]
        div_x = -fx_cur if fx_prev is None else fx_prev - fx_cur
        fx_prev = flux[1]
        pay_out[0, x] = rest - div_t - div_x


def cells(potential, ahead_t, ahead_x, multiplier, start_density, final_density, n_tm, n_sp):
    steps_t, rows_x, width_y, width_z = potential.shape
    idx = jnp.stack([lax.axis_index("tm"), lax.axis_index("space")]).astype(jnp.int32)
    slab = (1, rows_x, width_y, width_z)
    f32 = jnp.float32
    grid_spec = pltpu.PrefetchScalarGridSpec(
        num_scalar_prefetch=1,
        grid=(steps_t,),
        in_specs=[
            pl.BlockSpec(slab, lambda t, s: (t, 0, 0, 0)),
            pl.BlockSpec(slab, lambda t, s: (jnp.minimum(t + 1, steps_t - 1), 0, 0, 0)),
            pl.BlockSpec(slab, lambda t, s: (0, 0, 0, 0)),
            pl.BlockSpec((1, 1, width_y, width_z), lambda t, s: (t, 0, 0, 0)),
            pl.BlockSpec((4, 1, rows_x, width_y, width_z), lambda t, s: (0, t, 0, 0, 0)),
            pl.BlockSpec((rows_x, width_y, width_z), lambda t, s: (0, 0, 0)),
            pl.BlockSpec((rows_x, width_y, width_z), lambda t, s: (0, 0, 0)),
        ],
        out_specs=[
            pl.BlockSpec((4, 1, rows_x, width_y, width_z), lambda t, s: (0, t, 0, 0, 0)),
            pl.BlockSpec(slab, lambda t, s: (t, 0, 0, 0)),
            pl.BlockSpec(slab, lambda t, s: (0, 0, 0, 0)),
            pl.BlockSpec((1, 1, width_y, width_z), lambda t, s: (t, 0, 0, 0)),
        ],
        scratch_shapes=[pltpu.VMEM((rows_x, width_y, width_z), f32)],
    )
    cells_n = potential.size
    return pl.pallas_call(
        functools.partial(cell_kernel, n_tm, n_sp),
        grid_spec=grid_spec,
        out_shape=[
            jax.ShapeDtypeStruct(multiplier.shape, f32),
            jax.ShapeDtypeStruct(potential.shape, f32),
            jax.ShapeDtypeStruct(slab, f32),
            jax.ShapeDtypeStruct((steps_t, 1, width_y, width_z), f32),
        ],
        compiler_params=pltpu.CompilerParams(dimension_semantics=("arbitrary",)),
        cost_estimate=pl.CostEstimate(
            flops=cells_n * 200, transcendentals=cells_n * 11, bytes_accessed=cells_n * 4 * 12
        ),
    )(idx, potential, potential, ahead_t, ahead_x, multiplier, start_density, final_density)


def exchange_kernel(n_sp, src_ref, out_ref, send_sem, recv_sem, own_sem):
    n_dev = src_ref.shape[0]
    me = lax.axis_index("tm") * n_sp + lax.axis_index("space")

    def peer_copy(peer, source):
        return pltpu.make_async_remote_copy(
            src_ref.at[peer],
            out_ref.at[source],
            send_sem.at[peer],
            recv_sem.at[source],
            device_id=(peer // n_sp, peer % n_sp),
            device_id_type=pl.DeviceIdType.MESH,
        )

    def start(k, carry):
        peer = lax.rem(me + k, n_dev)
        peer_copy(peer, me).start()
        return carry

    lax.fori_loop(1, n_dev, start, 0)
    own = pltpu.make_async_copy(src_ref.at[me], out_ref.at[me], own_sem)
    own.start()

    def finish(k, carry):
        peer = lax.rem(me + k, n_dev)
        peer_copy(peer, me).wait_send()
        source = lax.rem(me + n_dev - k, n_dev)
        peer_copy(me, source).wait_recv()
        return carry

    lax.fori_loop(1, n_dev, finish, 0)
    own.wait()


def exchange(blocks, n_sp):
    n_dev = blocks.shape[0]
    any_space = pl.BlockSpec(memory_space=pl.ANY)
    return pl.pallas_call(
        functools.partial(exchange_kernel, n_sp),
        out_shape=jax.ShapeDtypeStruct(blocks.shape, blocks.dtype),
        in_specs=[any_space],
        out_specs=any_space,
        scratch_shapes=[
            pltpu.SemaphoreType.DMA((n_dev,)),
            pltpu.SemaphoreType.DMA((n_dev,)),
            pltpu.SemaphoreType.DMA(()),
        ],
        compiler_params=pltpu.CompilerParams(has_side_effects=True),
        cost_estimate=pl.CostEstimate(flops=0, transcendentals=0, bytes_accessed=2 * blocks.size * 4),
    )(blocks)


def body(potential, multiplier, start_density, final_density):
    high = lax.Precision.HIGHEST
    steps_t, rows_x, width_y, width_z = potential.shape
    n_tm = lax.axis_size("tm")
    n_sp = lax.axis_size("space")
    total_t = steps_t * n_tm
    total_x = rows_x * n_sp
    block_y = width_y // (n_tm * n_sp)
    time_at = lax.axis_index("tm") * steps_t + jnp.arange(steps_t)
    row_at = lax.axis_index("space") * rows_x + jnp.arange(rows_x)
    ahead_t = from_behind(potential[:1], "tm", -1)
    ahead_x = from_behind(potential[:, :1], "space", -1)
    next_multiplier, partial, flux_t_last, flux_x_last = cells(
        potential, ahead_t, ahead_x, multiplier, start_density, final_density, n_tm, n_sp
    )
    behind_t = from_behind(flux_t_last, "tm", 1)
    behind_x = from_behind(flux_x_last, "space", 1)
    cos_y = cosine_table(width_y)
    cos_z = cosine_table(width_z)
    payload = jnp.einsum("txyi,ki->txyk", partial, cos_z, precision=high)
    payload = jnp.einsum("txiz,ki->txkz", payload, cos_y, precision=high)
    edge_t = jnp.einsum("txyi,ki->txyk", behind_t, cos_z, precision=high)
    edge_t = jnp.einsum("txiz,ki->txkz", edge_t, cos_y, precision=high)
    edge_x = jnp.einsum("txyi,ki->txyk", behind_x, cos_z, precision=high)
    edge_x = jnp.einsum("txiz,ki->txkz", edge_x, cos_y, precision=high)
    payload = payload.at[:, :1].add(-edge_x)
    payload = payload.at[:1].add(-edge_t)
    n_dev = n_tm * n_sp
    blocks = payload.reshape(steps_t, rows_x, n_dev, block_y, width_z).transpose(2, 3, 0, 1, 4)
    blocks = blocks.reshape(n_dev, block_y * steps_t * rows_x, width_z)
    middle = exchange(blocks, n_sp)
    middle = middle.reshape(n_tm, n_sp, block_y, steps_t, rows_x, width_z).transpose(0, 1, 3, 4, 2, 5)
    cos_t = cosine_table(total_t).reshape(total_t, n_tm, steps_t)
    cos_x = cosine_table(total_x).reshape(total_x, n_sp, rows_x)
    hat = jnp.einsum("kat,abtxyz->kbxyz", cos_t, middle, precision=high)
    hat = jnp.einsum("jbx,kbxyz->kjyz", cos_x, hat, precision=high)
    freq_y = (
        (lax.axis_index("tm") * n_sp + lax.axis_index("space")) * block_y + jnp.arange(block_y)
    ).astype(jnp.float32)
    eig_t = eigen_at(total_t, jnp.arange(total_t, dtype=jnp.float32))
    eig_x = eigen_at(total_x, jnp.arange(total_x, dtype=jnp.float32))
    eig_y = eigen_at(width_y, freq_y)
    eig_z = eigen_at(width_z, jnp.arange(width_z, dtype=jnp.float32))
    denom = eig_t[:, None, None, None] + eig_x[None, :, None, None]
    denom = denom + eig_y[None, None, :, None] + eig_z[None, None, None, :]
    hat = hat / (RATE * denom + PROX)
    hat = jnp.einsum("atk,kjyz->atjyz", cos_t.reshape(n_tm, steps_t, total_t), hat, precision=high)
    solved = jnp.einsum("bxj,atjyz->abtxyz", cos_x.reshape(n_sp, rows_x, total_x), hat, precision=high)
    solved = solved.transpose(0, 1, 4, 2, 3, 5).reshape(n_dev, block_y * steps_t * rows_x, width_z)
    local = exchange(solved, n_sp)
    local = local.reshape(n_dev * block_y, steps_t, rows_x, width_z)
    local = jnp.einsum("ik,ktxz->txiz", cos_y, local, precision=high)
    next_potential = jnp.einsum("ik,txyk->txyi", cos_z, local, precision=high)
    return (next_potential, next_multiplier)


def solution(mesh):
    in_specs = (
        P("tm", "space", None, None),
        P(None, "tm", "space", None, None),
        P("space", None, None),
        P("space", None, None),
    )
    out_specs = (P("tm", "space", None, None), P(None, "tm", "space", None, None))
    return jax.shard_map(body, mesh=mesh, in_specs=in_specs, out_specs=out_specs, check_vma=False)
```

```python
import functools

import jax
import jax.numpy as jnp
from jax import lax
from jax.sharding import PartitionSpec as P
from jax.experimental import pallas as pl
from jax.experimental.pallas import tpu as pltpu

NEWTON = 10


RATE = 4.0
PROX = 0.01


def from_behind(block, axis, distance):
    devices = range(lax.axis_size(axis))
    route = [(i - distance, i) for i in devices if i - distance in devices]
    return lax.ppermute(block, axis, route)


def cosine_table(length):
    freq = jnp.arange(length, dtype=jnp.float32)[:, None]
    place = jnp.arange(length, dtype=jnp.float32)[None, :]
    weight = jnp.where(freq == 0.0, jnp.sqrt(jnp.float32(0.5)), jnp.float32(1.0))
    return (
        jnp.sqrt(jnp.float32(2.0) / length)
        * weight
        * jnp.cos(jnp.pi * freq * (place + 0.5) / length)
    )


def eigen_at(length, freq):
    return 4.0 * jnp.square(jnp.sin(jnp.pi * freq / (2.0 * length)))


def adjoint(face, axis):
    size = face.shape[axis]
    inner = lax.slice_in_dim(face, 0, size - 1, axis=axis)
    edge = jnp.zeros_like(lax.slice_in_dim(face, 0, 1, axis=axis))
    return jnp.concatenate([edge, inner], axis=axis) - jnp.concatenate([inner, edge], axis=axis)


def local_diff(field, axis):
    size = field.shape[axis]
    upper = lax.slice_in_dim(field, 1, size, axis=axis)
    lower = lax.slice_in_dim(field, 0, size - 1, axis=axis)
    edge = jnp.zeros_like(lax.slice_in_dim(field, 0, 1, axis=axis))
    return jnp.concatenate([upper - lower, edge], axis=axis)


def project(target):
    lead = target[0]
    side = target[1:]
    wsq = jnp.sum(side * side, axis=0)
    excess = lead + 0.5 * wsq
    stretch = jnp.maximum(1.0, lead + 1.0)
    shifted = lead + 1.0
    half_again = 1.5 * wsq
    for step in range(NEWTON):
        square = stretch * stretch
        cube = square * stretch
        stretch = jnp.maximum(1.0, stretch * (shifted * square + half_again) / (cube + wsq))
    inside = excess <= 0.0
    new_lead = jnp.where(inside, lead, lead - (stretch - 1.0))
    shrink = 1.0 / stretch
    new_side = jnp.where(inside[None], side, side * shrink[None])
    return jnp.concatenate([new_lead[None], new_side], axis=0)


def cell_kernel(n_tm, n_sp, idx_ref, pc, pn, p_any, m, sd, fd, nm_out, pay_out,
                ft_carry, ahead_t, ahead_x, send_x, send_t, behind_t, behind_x,
                at_sems, ax_sems, bt_sems, bx_sems):
    t = pl.program_id(0)
    steps_t = pl.num_programs(0)
    rows_x, width_y, width_z = pc.shape[1], pc.shape[2], pc.shape[3]
    tm = lax.axis_index("tm")
    sp = lax.axis_index("space")
    t_glob = tm * steps_t + t
    last_t = t_glob == n_tm * steps_t - 1
    has_later_t = tm < n_tm - 1
    has_earlier_t = tm > 0
    has_later_x = sp < n_sp - 1
    has_earlier_x = sp > 0
    mesh_id = pl.DeviceIdType.MESH

    def ahead_t_copy():
        return pltpu.make_async_remote_copy(
            p_any.at[0], ahead_t, at_sems.at[0], at_sems.at[1],
            device_id=(tm - 1, sp), device_id_type=mesh_id)

    def ahead_x_copy(row):
        return pltpu.make_async_remote_copy(
            p_any.at[row, 0], ahead_x.at[row], ax_sems.at[0, row], ax_sems.at[1, row],
            device_id=(tm, sp - 1), device_id_type=mesh_id)

    def behind_t_copy():
        return pltpu.make_async_remote_copy(
            send_t, behind_t, bt_sems.at[0], bt_sems.at[1],
            device_id=(tm + 1, sp), device_id_type=mesh_id)

    def behind_x_copy(row):
        return pltpu.make_async_remote_copy(
            send_x.at[row], behind_x.at[row], bx_sems.at[0, row], bx_sems.at[1, row],
            device_id=(tm, sp + 1), device_id_type=mesh_id)

    @pl.when(t == 0)
    def _():
        barrier = pltpu.get_barrier_semaphore()
        for cond, dev in ((has_earlier_t, (tm - 1, sp)), (has_later_t, (tm + 1, sp)),
                          (has_earlier_x, (tm, sp - 1)), (has_later_x, (tm, sp + 1))):
            @pl.when(cond)
            def _():
                pl.semaphore_signal(barrier, 1, device_id=dev, device_id_type=mesh_id)
        peers = (has_earlier_t.astype(jnp.int32) + has_later_t.astype(jnp.int32)
                 + has_earlier_x.astype(jnp.int32) + has_later_x.astype(jnp.int32))
        pl.semaphore_wait(barrier, peers)

        @pl.when(has_earlier_t)
        def _():
            ahead_t_copy().start()

        @pl.when(has_earlier_x)
        def _():
            for row in range(steps_t):
                ahead_x_copy(row).start()

    row = lax.broadcasted_iota(jnp.int32, (width_y, width_z), 0)
    col = lax.broadcasted_iota(jnp.int32, (width_y, width_z), 1)
    first_row = row == 0
    last_row = row == width_y - 1
    last_col = col == width_z - 1
    first_col = col == 0
    fx_prev = None
    for x in range(rows_x):
        p = pc[0, x]
        if x == 0:
            @pl.when(jnp.logical_and(t == steps_t - 1, has_later_t))
            def _():
                ahead_t_copy().wait_recv()
        nxt = lax.cond(t == steps_t - 1, lambda: ahead_t[x], lambda: pn[0, x])
        grad_t = jnp.where(last_t, 0.0, nxt - p)
        if x < rows_x - 1:
            grad_x = pc[0, x + 1] - p
        else:
            @pl.when(has_later_x)
            def _():
                ahead_x_copy(t).wait_recv()
            grad_x = lax.cond(has_later_x, lambda: ahead_x[t] - p, lambda: jnp.zeros_like(p))
        grad_y = jnp.where(last_row, 0.0, pltpu.roll(p, width_y - 1, 0) - p)
        grad_z = jnp.where(last_col, 0.0, pltpu.roll(p, width_z - 1, 1) - p)
        grads = (grad_t, grad_x, grad_y, grad_z)
        mults = tuple(m[c, 0, x] for c in range(4))
        target = tuple(g + mu * (1.0 / RATE) for g, mu in zip(grads, mults))
        lead = target[0]
        wsq = target[1] * target[1] + target[2] * target[2] + target[3] * target[3]
        excess = lead + 0.5 * wsq
        shifted = lead + 1.0
        half_again = 1.5 * wsq
        stretch = jnp.maximum(1.0, shifted)
        for step in range(NEWTON):
            square = stretch * stretch
            cube = square * stretch
            stretch = jnp.maximum(1.0, stretch * (shifted * square + half_again) / (cube + wsq))
        inside = excess <= 0.0
        shrink = 1.0 / stretch
        proj = (jnp.where(inside, lead, lead - (stretch - 1.0)),) + tuple(
            jnp.where(inside, target[c], target[c] * shrink) for c in (1, 2, 3)
        )
        flux = []
        for c in range(4):
            nm = mults[c] + RATE * (grads[c] - proj[c])
            nm_out[c, 0, x] = nm
            flux.append(nm - RATE * proj[c])
        flow_y = jnp.where(first_row, 0.0, pltpu.roll(flux[2], 1, 0)) - jnp.where(last_row, 0.0, flux[2])
        flow_z = jnp.where(first_col, 0.0, pltpu.roll(flux[3], 1, 1)) - jnp.where(last_col, 0.0, flux[3])
        rest = PROX * p - (flow_y + flow_z)
        rest = rest + jnp.where(t_glob == 0, sd[x], 0.0) - jnp.where(last_t, fd[x], 0.0)
        ft_prev = jnp.where(t == 0, 0.0, ft_carry[x])
        div_t = ft_prev - jnp.where(last_t, 0.0, flux[0])
        ft_carry[x] = flux[0]
        send_t[x] = flux[0]
        if x < rows_x - 1:
            fx_cur = flux[1]
        else:
            fx_cur = jnp.where(has_later_x, flux[1], 0.0)
            send_x[t] = flux[1]

            @pl.when(has_later_x)
            def _():
                behind_x_copy(t).start()
        div_x = -fx_cur if fx_prev is None else fx_prev - fx_cur
        fx_prev = flux[1]
        pay_out[t, x] = rest - div_t - div_x

    @pl.when(t == steps_t - 1)
    def _():
        @pl.when(has_later_t)
        def _():
            behind_t_copy().start()

        @pl.when(has_earlier_t)
        def _():
            ahead_t_copy().wait_send()
            behind_t_copy().wait_recv()
            for x in range(rows_x):
                pay_out[0, x] = pay_out[0, x] - behind_t[x]

        @pl.when(has_earlier_x)
        def _():
            for r in range(steps_t):
                ahead_x_copy(r).wait_send()
                behind_x_copy(r).wait_recv()
                pay_out[r, 0] = pay_out[r, 0] - behind_x[r]

        @pl.when(has_later_x)
        def _():
            for r in range(steps_t):
                behind_x_copy(r).wait_send()

        @pl.when(has_later_t)
        def _():
            behind_t_copy().wait_send()


def cells(potential, multiplier, start_density, final_density, n_tm, n_sp):
    steps_t, rows_x, width_y, width_z = potential.shape
    idx = jnp.stack([lax.axis_index("tm"), lax.axis_index("space")]).astype(jnp.int32)
    slab = (1, rows_x, width_y, width_z)
    plane = (rows_x, width_y, width_z)
    f32 = jnp.float32
    grid_spec = pltpu.PrefetchScalarGridSpec(
        num_scalar_prefetch=1,
        grid=(steps_t,),
        in_specs=[
            pl.BlockSpec(slab, lambda t, s: (t, 0, 0, 0)),
            pl.BlockSpec(slab, lambda t, s: (jnp.minimum(t + 1, steps_t - 1), 0, 0, 0)),
            pl.BlockSpec(memory_space=pl.ANY),
            pl.BlockSpec((4, 1, rows_x, width_y, width_z), lambda t, s: (0, t, 0, 0, 0)),
            pl.BlockSpec(plane, lambda t, s: (0, 0, 0)),
            pl.BlockSpec(plane, lambda t, s: (0, 0, 0)),
        ],
        out_specs=[
            pl.BlockSpec((4, 1, rows_x, width_y, width_z), lambda t, s: (0, t, 0, 0, 0)),
            pl.BlockSpec(potential.shape, lambda t, s: (0, 0, 0, 0)),
        ],
        scratch_shapes=[
            pltpu.VMEM(plane, f32),
            pltpu.VMEM(plane, f32),
            pltpu.VMEM((steps_t, width_y, width_z), f32),
            pltpu.VMEM((steps_t, width_y, width_z), f32),
            pltpu.VMEM(plane, f32),
            pltpu.VMEM(plane, f32),
            pltpu.VMEM((steps_t, width_y, width_z), f32),
            pltpu.SemaphoreType.DMA((2,)),
            pltpu.SemaphoreType.DMA((2, steps_t)),
            pltpu.SemaphoreType.DMA((2,)),
            pltpu.SemaphoreType.DMA((2, steps_t)),
        ],
    )
    cells_n = potential.size
    return pl.pallas_call(
        functools.partial(cell_kernel, n_tm, n_sp),
        grid_spec=grid_spec,
        out_shape=[
            jax.ShapeDtypeStruct(multiplier.shape, f32),
            jax.ShapeDtypeStruct(potential.shape, f32),
        ],
        compiler_params=pltpu.CompilerParams(
            dimension_semantics=("arbitrary",), collective_id=0, has_side_effects=True
        ),
        cost_estimate=pl.CostEstimate(
            flops=cells_n * 200, transcendentals=cells_n * 11, bytes_accessed=cells_n * 4 * 12
        ),
    )(idx, potential, potential, potential, multiplier, start_density, final_density)

def body(potential, multiplier, start_density, final_density):
    high = lax.Precision.HIGHEST
    steps_t, rows_x, width_y, width_z = potential.shape
    n_tm = lax.axis_size("tm")
    n_sp = lax.axis_size("space")
    total_t = steps_t * n_tm
    total_x = rows_x * n_sp
    block_y = width_y // (n_tm * n_sp)
    time_at = lax.axis_index("tm") * steps_t + jnp.arange(steps_t)
    row_at = lax.axis_index("space") * rows_x + jnp.arange(rows_x)
    next_multiplier, partial = cells(
        potential, multiplier, start_density, final_density, n_tm, n_sp
    )
    cos_y = cosine_table(width_y)
    cos_z = cosine_table(width_z)
    payload = jnp.einsum("txyi,ki->txyk", partial, cos_z, precision=high)
    payload = jnp.einsum("txiz,ki->txkz", payload, cos_y, precision=high)
    both = ("tm", "space")
    middle = lax.all_to_all(payload, both, split_axis=2, concat_axis=0, tiled=True)
    middle = middle.reshape(n_tm, n_sp, steps_t, rows_x, block_y, width_z)
    cos_t = cosine_table(total_t).reshape(total_t, n_tm, steps_t)
    cos_x = cosine_table(total_x).reshape(total_x, n_sp, rows_x)
    hat = jnp.einsum("kat,abtxyz->kbxyz", cos_t, middle, precision=high)
    hat = jnp.einsum("jbx,kbxyz->kjyz", cos_x, hat, precision=high)
    freq_y = (
        (lax.axis_index("tm") * n_sp + lax.axis_index("space")) * block_y + jnp.arange(block_y)
    ).astype(jnp.float32)
    eig_t = eigen_at(total_t, jnp.arange(total_t, dtype=jnp.float32))
    eig_x = eigen_at(total_x, jnp.arange(total_x, dtype=jnp.float32))
    eig_y = eigen_at(width_y, freq_y)
    eig_z = eigen_at(width_z, jnp.arange(width_z, dtype=jnp.float32))
    denom = eig_t[:, None, None, None] + eig_x[None, :, None, None]
    denom = denom + eig_y[None, None, :, None] + eig_z[None, None, None, :]
    hat = hat / (RATE * denom + PROX)
    hat = jnp.einsum("atk,kjyz->atjyz", cos_t.reshape(n_tm, steps_t, total_t), hat, precision=high)
    solved = jnp.einsum("bxj,atjyz->abtxyz", cos_x.reshape(n_sp, rows_x, total_x), hat, precision=high)
    solved = solved.reshape(n_tm * n_sp * steps_t, rows_x, block_y, width_z)
    local = lax.all_to_all(solved, both, split_axis=0, concat_axis=2, tiled=True)
    local = jnp.einsum("ik,txkz->txiz", cos_y, local, precision=high)
    next_potential = jnp.einsum("ik,txyk->txyi", cos_z, local, precision=high)
    return (next_potential, next_multiplier)


def solution(mesh):
    in_specs = (
        P("tm", "space", None, None),
        P(None, "tm", "space", None, None),
        P("space", None, None),
        P("space", None, None),
    )
    out_specs = (P("tm", "space", None, None), P(None, "tm", "space", None, None))
    return jax.shard_map(body, mesh=mesh, in_specs=in_specs, out_specs=out_specs, check_vma=False)
```

```python
import functools

import jax
import jax.numpy as jnp
from jax import lax
from jax.sharding import PartitionSpec as P
from jax.experimental import pallas as pl
from jax.experimental.pallas import tpu as pltpu

NEWTON = 10


RATE = 4.0
PROX = 0.01


def from_behind(block, axis, distance):
    devices = range(lax.axis_size(axis))
    route = [(i - distance, i) for i in devices if i - distance in devices]
    return lax.ppermute(block, axis, route)


def cosine_table(length):
    freq = jnp.arange(length, dtype=jnp.float32)[:, None]
    place = jnp.arange(length, dtype=jnp.float32)[None, :]
    weight = jnp.where(freq == 0.0, jnp.sqrt(jnp.float32(0.5)), jnp.float32(1.0))
    return (
        jnp.sqrt(jnp.float32(2.0) / length)
        * weight
        * jnp.cos(jnp.pi * freq * (place + 0.5) / length)
    )


def eigen_at(length, freq):
    return 4.0 * jnp.square(jnp.sin(jnp.pi * freq / (2.0 * length)))


def adjoint(face, axis):
    size = face.shape[axis]
    inner = lax.slice_in_dim(face, 0, size - 1, axis=axis)
    edge = jnp.zeros_like(lax.slice_in_dim(face, 0, 1, axis=axis))
    return jnp.concatenate([edge, inner], axis=axis) - jnp.concatenate([inner, edge], axis=axis)


def local_diff(field, axis):
    size = field.shape[axis]
    upper = lax.slice_in_dim(field, 1, size, axis=axis)
    lower = lax.slice_in_dim(field, 0, size - 1, axis=axis)
    edge = jnp.zeros_like(lax.slice_in_dim(field, 0, 1, axis=axis))
    return jnp.concatenate([upper - lower, edge], axis=axis)


def project(target):
    lead = target[0]
    side = target[1:]
    wsq = jnp.sum(side * side, axis=0)
    excess = lead + 0.5 * wsq
    stretch = jnp.maximum(1.0, lead + 1.0)
    shifted = lead + 1.0
    half_again = 1.5 * wsq
    for step in range(NEWTON):
        square = stretch * stretch
        cube = square * stretch
        stretch = jnp.maximum(1.0, stretch * (shifted * square + half_again) / (cube + wsq))
    inside = excess <= 0.0
    new_lead = jnp.where(inside, lead, lead - (stretch - 1.0))
    shrink = 1.0 / stretch
    new_side = jnp.where(inside[None], side, side * shrink[None])
    return jnp.concatenate([new_lead[None], new_side], axis=0)


def cell_kernel(n_tm, n_sp, idx_ref, pc, pn, p_any, m, sd, fd, nm_out, pay_out,
                ft_carry, ahead_t, ahead_x, send_x, send_t, behind_t, behind_x,
                at_sems, ax_sems, bt_sems, bx_sems):
    t = pl.program_id(0)
    steps_t = pl.num_programs(0)
    rows_x, width_y, width_z = pc.shape[1], pc.shape[2], pc.shape[3]
    tm = lax.axis_index("tm")
    sp = lax.axis_index("space")
    t_glob = tm * steps_t + t
    last_t = t_glob == n_tm * steps_t - 1
    has_later_t = tm < n_tm - 1
    has_earlier_t = tm > 0
    has_later_x = sp < n_sp - 1
    has_earlier_x = sp > 0
    mesh_id = pl.DeviceIdType.MESH

    def ahead_t_copy():
        return pltpu.make_async_remote_copy(
            p_any.at[0], ahead_t, at_sems.at[0], at_sems.at[1],
            device_id=(tm - 1, sp), device_id_type=mesh_id)

    def ahead_x_copy(row):
        return pltpu.make_async_remote_copy(
            p_any.at[row, 0], ahead_x.at[row], ax_sems.at[0, row], ax_sems.at[1, row],
            device_id=(tm, sp - 1), device_id_type=mesh_id)

    def behind_t_copy():
        return pltpu.make_async_remote_copy(
            send_t, behind_t, bt_sems.at[0], bt_sems.at[1],
            device_id=(tm + 1, sp), device_id_type=mesh_id)

    def behind_x_copy(row):
        return pltpu.make_async_remote_copy(
            send_x.at[row], behind_x.at[row], bx_sems.at[0, row], bx_sems.at[1, row],
            device_id=(tm, sp + 1), device_id_type=mesh_id)

    @pl.when(t == 0)
    def _():
        barrier = pltpu.get_barrier_semaphore()
        for cond, dev in ((has_earlier_t, (tm - 1, sp)), (has_later_t, (tm + 1, sp)),
                          (has_earlier_x, (tm, sp - 1)), (has_later_x, (tm, sp + 1))):
            @pl.when(cond)
            def _():
                pl.semaphore_signal(barrier, 1, device_id=dev, device_id_type=mesh_id)
        peers = (has_earlier_t.astype(jnp.int32) + has_later_t.astype(jnp.int32)
                 + has_earlier_x.astype(jnp.int32) + has_later_x.astype(jnp.int32))
        pl.semaphore_wait(barrier, peers)

        @pl.when(has_earlier_t)
        def _():
            ahead_t_copy().start()

        @pl.when(has_earlier_x)
        def _():
            for row in range(steps_t):
                ahead_x_copy(row).start()

    row = lax.broadcasted_iota(jnp.int32, (width_y, width_z), 0)
    col = lax.broadcasted_iota(jnp.int32, (width_y, width_z), 1)
    first_row = row == 0
    last_row = row == width_y - 1
    last_col = col == width_z - 1
    first_col = col == 0
    fx_prev = None
    for x in range(rows_x):
        p = pc[0, x]
        if x == 0:
            @pl.when(jnp.logical_and(t == steps_t - 1, has_later_t))
            def _():
                ahead_t_copy().wait_recv()
        nxt = lax.cond(t == steps_t - 1, lambda: ahead_t[x], lambda: pn[0, x])
        grad_t = jnp.where(last_t, 0.0, nxt - p)
        if x < rows_x - 1:
            grad_x = pc[0, x + 1] - p
        else:
            @pl.when(has_later_x)
            def _():
                ahead_x_copy(t).wait_recv()
            grad_x = lax.cond(has_later_x, lambda: ahead_x[t] - p, lambda: jnp.zeros_like(p))
        grad_y = jnp.where(last_row, 0.0, pltpu.roll(p, width_y - 1, 0) - p)
        grad_z = jnp.where(last_col, 0.0, pltpu.roll(p, width_z - 1, 1) - p)
        grads = (grad_t, grad_x, grad_y, grad_z)
        mults = tuple(m[c, 0, x] for c in range(4))
        target = tuple(g + mu * (1.0 / RATE) for g, mu in zip(grads, mults))
        lead = target[0]
        wsq = target[1] * target[1] + target[2] * target[2] + target[3] * target[3]
        excess = lead + 0.5 * wsq
        shifted = lead + 1.0
        half_again = 1.5 * wsq
        stretch = jnp.maximum(1.0, shifted)
        for step in range(NEWTON):
            square = stretch * stretch
            cube = square * stretch
            stretch = jnp.maximum(1.0, stretch * (shifted * square + half_again) / (cube + wsq))
        inside = excess <= 0.0
        shrink = 1.0 / stretch
        proj = (jnp.where(inside, lead, lead - (stretch - 1.0)),) + tuple(
            jnp.where(inside, target[c], target[c] * shrink) for c in (1, 2, 3)
        )
        flux = []
        for c in range(4):
            nm = mults[c] + RATE * (grads[c] - proj[c])
            nm_out[c, 0, x] = nm
            flux.append(nm - RATE * proj[c])
        flow_y = jnp.where(first_row, 0.0, pltpu.roll(flux[2], 1, 0)) - jnp.where(last_row, 0.0, flux[2])
        flow_z = jnp.where(first_col, 0.0, pltpu.roll(flux[3], 1, 1)) - jnp.where(last_col, 0.0, flux[3])
        rest = PROX * p - (flow_y + flow_z)
        rest = rest + jnp.where(t_glob == 0, sd[x], 0.0) - jnp.where(last_t, fd[x], 0.0)
        ft_prev = jnp.where(t == 0, 0.0, ft_carry[x])
        div_t = ft_prev - jnp.where(last_t, 0.0, flux[0])
        ft_carry[x] = flux[0]
        send_t[x] = flux[0]
        if x < rows_x - 1:
            fx_cur = flux[1]
        else:
            fx_cur = jnp.where(has_later_x, flux[1], 0.0)
            send_x[t] = flux[1]

            @pl.when(has_later_x)
            def _():
                behind_x_copy(t).start()
        div_x = -fx_cur if fx_prev is None else fx_prev - fx_cur
        fx_prev = flux[1]
        pay_out[t, x] = rest - div_t - div_x

    @pl.when(t == steps_t - 1)
    def _():
        @pl.when(has_later_t)
        def _():
            behind_t_copy().start()

        @pl.when(has_earlier_t)
        def _():
            ahead_t_copy().wait_send()
            behind_t_copy().wait_recv()
            for x in range(rows_x):
                pay_out[0, x] = pay_out[0, x] - behind_t[x]

        @pl.when(has_earlier_x)
        def _():
            for r in range(steps_t):
                ahead_x_copy(r).wait_send()
                behind_x_copy(r).wait_recv()
                pay_out[r, 0] = pay_out[r, 0] - behind_x[r]

        @pl.when(has_later_x)
        def _():
            for r in range(steps_t):
                behind_x_copy(r).wait_send()

        @pl.when(has_later_t)
        def _():
            behind_t_copy().wait_send()


def cells(potential, multiplier, start_density, final_density, n_tm, n_sp):
    steps_t, rows_x, width_y, width_z = potential.shape
    idx = jnp.stack([lax.axis_index("tm"), lax.axis_index("space")]).astype(jnp.int32)
    slab = (1, rows_x, width_y, width_z)
    plane = (rows_x, width_y, width_z)
    f32 = jnp.float32
    grid_spec = pltpu.PrefetchScalarGridSpec(
        num_scalar_prefetch=1,
        grid=(steps_t,),
        in_specs=[
            pl.BlockSpec(slab, lambda t, s: (t, 0, 0, 0)),
            pl.BlockSpec(slab, lambda t, s: (jnp.minimum(t + 1, steps_t - 1), 0, 0, 0)),
            pl.BlockSpec(memory_space=pl.ANY),
            pl.BlockSpec((4, 1, rows_x, width_y, width_z), lambda t, s: (0, t, 0, 0, 0)),
            pl.BlockSpec(plane, lambda t, s: (0, 0, 0)),
            pl.BlockSpec(plane, lambda t, s: (0, 0, 0)),
        ],
        out_specs=[
            pl.BlockSpec((4, 1, rows_x, width_y, width_z), lambda t, s: (0, t, 0, 0, 0)),
            pl.BlockSpec(potential.shape, lambda t, s: (0, 0, 0, 0)),
        ],
        scratch_shapes=[
            pltpu.VMEM(plane, f32),
            pltpu.VMEM(plane, f32),
            pltpu.VMEM((steps_t, width_y, width_z), f32),
            pltpu.VMEM((steps_t, width_y, width_z), f32),
            pltpu.VMEM(plane, f32),
            pltpu.VMEM(plane, f32),
            pltpu.VMEM((steps_t, width_y, width_z), f32),
            pltpu.SemaphoreType.DMA((2,)),
            pltpu.SemaphoreType.DMA((2, steps_t)),
            pltpu.SemaphoreType.DMA((2,)),
            pltpu.SemaphoreType.DMA((2, steps_t)),
        ],
    )
    cells_n = potential.size
    return pl.pallas_call(
        functools.partial(cell_kernel, n_tm, n_sp),
        grid_spec=grid_spec,
        out_shape=[
            jax.ShapeDtypeStruct(multiplier.shape, f32),
            jax.ShapeDtypeStruct(potential.shape, f32),
        ],
        compiler_params=pltpu.CompilerParams(
            dimension_semantics=("arbitrary",), collective_id=0, has_side_effects=True
        ),
        cost_estimate=pl.CostEstimate(
            flops=cells_n * 200, transcendentals=cells_n * 11, bytes_accessed=cells_n * 4 * 12
        ),
    )(idx, potential, potential, potential, multiplier, start_density, final_density)

def body(potential, multiplier, start_density, final_density):
    high = lax.Precision.HIGHEST
    steps_t, rows_x, width_y, width_z = potential.shape
    n_tm = lax.axis_size("tm")
    n_sp = lax.axis_size("space")
    total_t = steps_t * n_tm
    total_x = rows_x * n_sp
    block_y = width_y // (n_tm * n_sp)
    time_at = lax.axis_index("tm") * steps_t + jnp.arange(steps_t)
    row_at = lax.axis_index("space") * rows_x + jnp.arange(rows_x)
    next_multiplier, partial = cells(
        potential, multiplier, start_density, final_density, n_tm, n_sp
    )
    cos_y = cosine_table(width_y)
    cos_z = cosine_table(width_z)
    payload = jnp.einsum("txyi,ki->txyk", partial, cos_z, precision=high)
    payload = jnp.einsum("txiz,ki->txkz", payload, cos_y, precision=high)
    both = ("tm", "space")
    middle = lax.all_to_all(payload, both, split_axis=2, concat_axis=0, tiled=True)
    next_multiplier = jnp.where(next_multiplier == next_multiplier, next_multiplier, 0.0)
    middle, next_multiplier = lax.optimization_barrier((middle, next_multiplier))
    middle = middle.reshape(n_tm, n_sp, steps_t, rows_x, block_y, width_z)
    cos_t = cosine_table(total_t).reshape(total_t, n_tm, steps_t)
    cos_x = cosine_table(total_x).reshape(total_x, n_sp, rows_x)
    hat = jnp.einsum("kat,abtxyz->kbxyz", cos_t, middle, precision=high)
    hat = jnp.einsum("jbx,kbxyz->kjyz", cos_x, hat, precision=high)
    freq_y = (
        (lax.axis_index("tm") * n_sp + lax.axis_index("space")) * block_y + jnp.arange(block_y)
    ).astype(jnp.float32)
    eig_t = eigen_at(total_t, jnp.arange(total_t, dtype=jnp.float32))
    eig_x = eigen_at(total_x, jnp.arange(total_x, dtype=jnp.float32))
    eig_y = eigen_at(width_y, freq_y)
    eig_z = eigen_at(width_z, jnp.arange(width_z, dtype=jnp.float32))
    denom = eig_t[:, None, None, None] + eig_x[None, :, None, None]
    denom = denom + eig_y[None, None, :, None] + eig_z[None, None, None, :]
    hat = hat / (RATE * denom + PROX)
    hat = jnp.einsum("atk,kjyz->atjyz", cos_t.reshape(n_tm, steps_t, total_t), hat, precision=high)
    solved = jnp.einsum("bxj,atjyz->abtxyz", cos_x.reshape(n_sp, rows_x, total_x), hat, precision=high)
    solved = solved.reshape(n_tm * n_sp * steps_t, rows_x, block_y, width_z)
    local = lax.all_to_all(solved, both, split_axis=0, concat_axis=2, tiled=True)
    local = jnp.einsum("ik,txkz->txiz", cos_y, local, precision=high)
    next_potential = jnp.einsum("ik,txyk->txyi", cos_z, local, precision=high)
    return (next_potential, next_multiplier)


def solution(mesh):
    in_specs = (
        P("tm", "space", None, None),
        P(None, "tm", "space", None, None),
        P("space", None, None),
        P("space", None, None),
    )
    out_specs = (P("tm", "space", None, None), P(None, "tm", "space", None, None))
    return jax.shard_map(body, mesh=mesh, in_specs=in_specs, out_specs=out_specs, check_vma=False)
```

```python
import functools

import jax
import jax.numpy as jnp
from jax import lax
from jax.sharding import PartitionSpec as P
from jax.experimental import pallas as pl
from jax.experimental.pallas import tpu as pltpu

NEWTON = 10


RATE = 4.0
PROX = 0.01


def from_behind(block, axis, distance):
    devices = range(lax.axis_size(axis))
    route = [(i - distance, i) for i in devices if i - distance in devices]
    return lax.ppermute(block, axis, route)


def cosine_table(length):
    freq = jnp.arange(length, dtype=jnp.float32)[:, None]
    place = jnp.arange(length, dtype=jnp.float32)[None, :]
    weight = jnp.where(freq == 0.0, jnp.sqrt(jnp.float32(0.5)), jnp.float32(1.0))
    return (
        jnp.sqrt(jnp.float32(2.0) / length)
        * weight
        * jnp.cos(jnp.pi * freq * (place + 0.5) / length)
    )


def eigen_at(length, freq):
    return 4.0 * jnp.square(jnp.sin(jnp.pi * freq / (2.0 * length)))


def adjoint(face, axis):
    size = face.shape[axis]
    inner = lax.slice_in_dim(face, 0, size - 1, axis=axis)
    edge = jnp.zeros_like(lax.slice_in_dim(face, 0, 1, axis=axis))
    return jnp.concatenate([edge, inner], axis=axis) - jnp.concatenate([inner, edge], axis=axis)


def local_diff(field, axis):
    size = field.shape[axis]
    upper = lax.slice_in_dim(field, 1, size, axis=axis)
    lower = lax.slice_in_dim(field, 0, size - 1, axis=axis)
    edge = jnp.zeros_like(lax.slice_in_dim(field, 0, 1, axis=axis))
    return jnp.concatenate([upper - lower, edge], axis=axis)


def project(target):
    lead = target[0]
    side = target[1:]
    wsq = jnp.sum(side * side, axis=0)
    excess = lead + 0.5 * wsq
    stretch = jnp.maximum(1.0, lead + 1.0)
    shifted = lead + 1.0
    half_again = 1.5 * wsq
    for step in range(NEWTON):
        square = stretch * stretch
        cube = square * stretch
        stretch = jnp.maximum(1.0, stretch * (shifted * square + half_again) / (cube + wsq))
    inside = excess <= 0.0
    new_lead = jnp.where(inside, lead, lead - (stretch - 1.0))
    shrink = 1.0 / stretch
    new_side = jnp.where(inside[None], side, side * shrink[None])
    return jnp.concatenate([new_lead[None], new_side], axis=0)


def cell_kernel(n_tm, n_sp, idx_ref, pc, pn, p_any, m, sd, fd, nm_out, pay_out,
                ft_carry, ahead_t, ahead_x, send_x, send_t, behind_t, behind_x,
                at_sems, ax_sems, bt_sems, bx_sems):
    t = pl.program_id(0)
    steps_t = pl.num_programs(0)
    rows_x, width_y, width_z = pc.shape[1], pc.shape[2], pc.shape[3]
    tm = lax.axis_index("tm")
    sp = lax.axis_index("space")
    t_glob = tm * steps_t + t
    last_t = t_glob == n_tm * steps_t - 1
    has_later_t = tm < n_tm - 1
    has_earlier_t = tm > 0
    has_later_x = sp < n_sp - 1
    has_earlier_x = sp > 0
    mesh_id = pl.DeviceIdType.MESH

    def ahead_t_copy():
        return pltpu.make_async_remote_copy(
            p_any.at[0], ahead_t, at_sems.at[0], at_sems.at[1],
            device_id=(tm - 1, sp), device_id_type=mesh_id)

    def ahead_x_copy(row):
        return pltpu.make_async_remote_copy(
            p_any.at[row, 0], ahead_x.at[row], ax_sems.at[0, row], ax_sems.at[1, row],
            device_id=(tm, sp - 1), device_id_type=mesh_id)

    def behind_t_copy():
        return pltpu.make_async_remote_copy(
            send_t, behind_t, bt_sems.at[0], bt_sems.at[1],
            device_id=(tm + 1, sp), device_id_type=mesh_id)

    def behind_x_copy(row):
        return pltpu.make_async_remote_copy(
            send_x.at[row], behind_x.at[row], bx_sems.at[0, row], bx_sems.at[1, row],
            device_id=(tm, sp + 1), device_id_type=mesh_id)

    @pl.when(t == 0)
    def _():
        barrier = pltpu.get_barrier_semaphore()
        for cond, dev in ((has_earlier_t, (tm - 1, sp)), (has_later_t, (tm + 1, sp)),
                          (has_earlier_x, (tm, sp - 1)), (has_later_x, (tm, sp + 1))):
            @pl.when(cond)
            def _():
                pl.semaphore_signal(barrier, 1, device_id=dev, device_id_type=mesh_id)
        peers = (has_earlier_t.astype(jnp.int32) + has_later_t.astype(jnp.int32)
                 + has_earlier_x.astype(jnp.int32) + has_later_x.astype(jnp.int32))
        pl.semaphore_wait(barrier, peers)

        @pl.when(has_earlier_t)
        def _():
            ahead_t_copy().start()

        @pl.when(has_earlier_x)
        def _():
            for row in range(steps_t):
                ahead_x_copy(row).start()

    row = lax.broadcasted_iota(jnp.int32, (width_y, width_z), 0)
    col = lax.broadcasted_iota(jnp.int32, (width_y, width_z), 1)
    first_row = row == 0
    last_row = row == width_y - 1
    last_col = col == width_z - 1
    first_col = col == 0
    fx_prev = None
    for x in range(rows_x):
        p = pc[0, x]
        if x == 0:
            @pl.when(jnp.logical_and(t == steps_t - 1, has_later_t))
            def _():
                ahead_t_copy().wait_recv()
        nxt = lax.cond(t == steps_t - 1, lambda: ahead_t[x], lambda: pn[0, x])
        grad_t = jnp.where(last_t, 0.0, nxt - p)
        if x < rows_x - 1:
            grad_x = pc[0, x + 1] - p
        else:
            @pl.when(has_later_x)
            def _():
                ahead_x_copy(t).wait_recv()
            grad_x = lax.cond(has_later_x, lambda: ahead_x[t] - p, lambda: jnp.zeros_like(p))
        grad_y = jnp.where(last_row, 0.0, pltpu.roll(p, width_y - 1, 0) - p)
        grad_z = jnp.where(last_col, 0.0, pltpu.roll(p, width_z - 1, 1) - p)
        grads = (grad_t, grad_x, grad_y, grad_z)
        mults = tuple(m[c, 0, x] for c in range(4))
        target = tuple(g + mu * (1.0 / RATE) for g, mu in zip(grads, mults))
        lead = target[0]
        wsq = target[1] * target[1] + target[2] * target[2] + target[3] * target[3]
        excess = lead + 0.5 * wsq
        shifted = lead + 1.0
        half_again = 1.5 * wsq
        stretch = jnp.maximum(1.0, shifted)
        for step in range(NEWTON):
            square = stretch * stretch
            cube = square * stretch
            stretch = jnp.maximum(1.0, stretch * (shifted * square + half_again) / (cube + wsq))
        inside = excess <= 0.0
        shrink = 1.0 / stretch
        proj = (jnp.where(inside, lead, lead - (stretch - 1.0)),) + tuple(
            jnp.where(inside, target[c], target[c] * shrink) for c in (1, 2, 3)
        )
        flux = []
        for c in range(4):
            nm = mults[c] + RATE * (grads[c] - proj[c])
            nm_out[c, 0, x] = nm
            flux.append(nm - RATE * proj[c])
        flow_y = jnp.where(first_row, 0.0, pltpu.roll(flux[2], 1, 0)) - jnp.where(last_row, 0.0, flux[2])
        flow_z = jnp.where(first_col, 0.0, pltpu.roll(flux[3], 1, 1)) - jnp.where(last_col, 0.0, flux[3])
        rest = PROX * p - (flow_y + flow_z)
        rest = rest + jnp.where(t_glob == 0, sd[x], 0.0) - jnp.where(last_t, fd[x], 0.0)
        ft_prev = jnp.where(t == 0, 0.0, ft_carry[x])
        div_t = ft_prev - jnp.where(last_t, 0.0, flux[0])
        ft_carry[x] = flux[0]
        send_t[x] = flux[0]
        if x < rows_x - 1:
            fx_cur = flux[1]
        else:
            fx_cur = jnp.where(has_later_x, flux[1], 0.0)
            send_x[t] = flux[1]

            @pl.when(has_later_x)
            def _():
                behind_x_copy(t).start()
        div_x = -fx_cur if fx_prev is None else fx_prev - fx_cur
        fx_prev = flux[1]
        pay_out[t, x] = rest - div_t - div_x

    @pl.when(t == steps_t - 1)
    def _():
        @pl.when(has_later_t)
        def _():
            behind_t_copy().start()

        @pl.when(has_earlier_t)
        def _():
            ahead_t_copy().wait_send()
            behind_t_copy().wait_recv()
            for x in range(rows_x):
                pay_out[0, x] = pay_out[0, x] - behind_t[x]

        @pl.when(has_earlier_x)
        def _():
            for r in range(steps_t):
                ahead_x_copy(r).wait_send()
                behind_x_copy(r).wait_recv()
                pay_out[r, 0] = pay_out[r, 0] - behind_x[r]

        @pl.when(has_later_x)
        def _():
            for r in range(steps_t):
                behind_x_copy(r).wait_send()

        @pl.when(has_later_t)
        def _():
            behind_t_copy().wait_send()


def cells(potential, multiplier, start_density, final_density, n_tm, n_sp):
    steps_t, rows_x, width_y, width_z = potential.shape
    idx = jnp.stack([lax.axis_index("tm"), lax.axis_index("space")]).astype(jnp.int32)
    slab = (1, rows_x, width_y, width_z)
    plane = (rows_x, width_y, width_z)
    f32 = jnp.float32
    grid_spec = pltpu.PrefetchScalarGridSpec(
        num_scalar_prefetch=1,
        grid=(steps_t,),
        in_specs=[
            pl.BlockSpec(slab, lambda t, s: (t, 0, 0, 0)),
            pl.BlockSpec(slab, lambda t, s: (jnp.minimum(t + 1, steps_t - 1), 0, 0, 0)),
            pl.BlockSpec(memory_space=pl.ANY),
            pl.BlockSpec((4, 1, rows_x, width_y, width_z), lambda t, s: (0, t, 0, 0, 0)),
            pl.BlockSpec(plane, lambda t, s: (0, 0, 0)),
            pl.BlockSpec(plane, lambda t, s: (0, 0, 0)),
        ],
        out_specs=[
            pl.BlockSpec((4, 1, rows_x, width_y, width_z), lambda t, s: (0, t, 0, 0, 0)),
            pl.BlockSpec(potential.shape, lambda t, s: (0, 0, 0, 0)),
        ],
        scratch_shapes=[
            pltpu.VMEM(plane, f32),
            pltpu.VMEM(plane, f32),
            pltpu.VMEM((steps_t, width_y, width_z), f32),
            pltpu.VMEM((steps_t, width_y, width_z), f32),
            pltpu.VMEM(plane, f32),
            pltpu.VMEM(plane, f32),
            pltpu.VMEM((steps_t, width_y, width_z), f32),
            pltpu.SemaphoreType.DMA((2,)),
            pltpu.SemaphoreType.DMA((2, steps_t)),
            pltpu.SemaphoreType.DMA((2,)),
            pltpu.SemaphoreType.DMA((2, steps_t)),
        ],
    )
    cells_n = potential.size
    return pl.pallas_call(
        functools.partial(cell_kernel, n_tm, n_sp),
        grid_spec=grid_spec,
        out_shape=[
            jax.ShapeDtypeStruct(multiplier.shape, f32),
            jax.ShapeDtypeStruct(potential.shape, f32),
        ],
        compiler_params=pltpu.CompilerParams(
            dimension_semantics=("arbitrary",), collective_id=0, has_side_effects=True
        ),
        cost_estimate=pl.CostEstimate(
            flops=cells_n * 200, transcendentals=cells_n * 11, bytes_accessed=cells_n * 4 * 12
        ),
    )(idx, potential, potential, potential, multiplier, start_density, final_density)

def body(potential, multiplier, start_density, final_density):
    high = lax.Precision.HIGHEST
    steps_t, rows_x, width_y, width_z = potential.shape
    n_tm = lax.axis_size("tm")
    n_sp = lax.axis_size("space")
    total_t = steps_t * n_tm
    total_x = rows_x * n_sp
    block_y = width_y // (n_tm * n_sp)
    time_at = lax.axis_index("tm") * steps_t + jnp.arange(steps_t)
    row_at = lax.axis_index("space") * rows_x + jnp.arange(rows_x)
    next_multiplier, partial = cells(
        potential, multiplier, start_density, final_density, n_tm, n_sp
    )
    cos_y = cosine_table(width_y)
    cos_z = cosine_table(width_z)
    payload = jnp.einsum("txyi,ki->txyk", partial, cos_z, precision=high)
    payload = jnp.einsum("txiz,ki->ktxz", payload, cos_y, precision=high)
    both = ("tm", "space")
    middle = lax.all_to_all(payload, both, split_axis=0, concat_axis=0, tiled=True)
    next_multiplier = jnp.where(next_multiplier == next_multiplier, next_multiplier, 0.0)
    middle, next_multiplier = lax.optimization_barrier((middle, next_multiplier))
    middle = middle.reshape(n_tm, n_sp, block_y, steps_t, rows_x, width_z)
    cos_t = cosine_table(total_t).reshape(total_t, n_tm, steps_t)
    cos_x = cosine_table(total_x).reshape(total_x, n_sp, rows_x)
    hat = jnp.einsum("kat,abytxz->kbxyz", cos_t, middle, precision=high)
    hat = jnp.einsum("jbx,kbxyz->kjyz", cos_x, hat, precision=high)
    freq_y = (
        (lax.axis_index("tm") * n_sp + lax.axis_index("space")) * block_y + jnp.arange(block_y)
    ).astype(jnp.float32)
    eig_t = eigen_at(total_t, jnp.arange(total_t, dtype=jnp.float32))
    eig_x = eigen_at(total_x, jnp.arange(total_x, dtype=jnp.float32))
    eig_y = eigen_at(width_y, freq_y)
    eig_z = eigen_at(width_z, jnp.arange(width_z, dtype=jnp.float32))
    denom = eig_t[:, None, None, None] + eig_x[None, :, None, None]
    denom = denom + eig_y[None, None, :, None] + eig_z[None, None, None, :]
    hat = hat / (RATE * denom + PROX)
    hat = jnp.einsum("atk,kjyz->atjyz", cos_t.reshape(n_tm, steps_t, total_t), hat, precision=high)
    solved = jnp.einsum("bxj,atjyz->abytxz", cos_x.reshape(n_sp, rows_x, total_x), hat, precision=high)
    solved = solved.reshape(n_tm * n_sp * block_y, steps_t, rows_x, width_z)
    local = lax.all_to_all(solved, both, split_axis=0, concat_axis=0, tiled=True)
    local = jnp.einsum("ik,ktxz->txiz", cos_y, local, precision=high)
    next_potential = jnp.einsum("ik,txyk->txyi", cos_z, local, precision=high)
    return (next_potential, next_multiplier)


def solution(mesh):
    in_specs = (
        P("tm", "space", None, None),
        P(None, "tm", "space", None, None),
        P("space", None, None),
        P("space", None, None),
    )
    out_specs = (P("tm", "space", None, None), P(None, "tm", "space", None, None))
    return jax.shard_map(body, mesh=mesh, in_specs=in_specs, out_specs=out_specs, check_vma=False)
```

```python
import functools

import jax
import jax.numpy as jnp
from jax import lax
from jax.sharding import PartitionSpec as P
from jax.experimental import pallas as pl
from jax.experimental.pallas import tpu as pltpu

NEWTON = 10


RATE = 4.0
PROX = 0.01


def from_behind(block, axis, distance):
    devices = range(lax.axis_size(axis))
    route = [(i - distance, i) for i in devices if i - distance in devices]
    return lax.ppermute(block, axis, route)


def cosine_table(length):
    freq = jnp.arange(length, dtype=jnp.float32)[:, None]
    place = jnp.arange(length, dtype=jnp.float32)[None, :]
    weight = jnp.where(freq == 0.0, jnp.sqrt(jnp.float32(0.5)), jnp.float32(1.0))
    return (
        jnp.sqrt(jnp.float32(2.0) / length)
        * weight
        * jnp.cos(jnp.pi * freq * (place + 0.5) / length)
    )


def eigen_at(length, freq):
    return 4.0 * jnp.square(jnp.sin(jnp.pi * freq / (2.0 * length)))


def adjoint(face, axis):
    size = face.shape[axis]
    inner = lax.slice_in_dim(face, 0, size - 1, axis=axis)
    edge = jnp.zeros_like(lax.slice_in_dim(face, 0, 1, axis=axis))
    return jnp.concatenate([edge, inner], axis=axis) - jnp.concatenate([inner, edge], axis=axis)


def local_diff(field, axis):
    size = field.shape[axis]
    upper = lax.slice_in_dim(field, 1, size, axis=axis)
    lower = lax.slice_in_dim(field, 0, size - 1, axis=axis)
    edge = jnp.zeros_like(lax.slice_in_dim(field, 0, 1, axis=axis))
    return jnp.concatenate([upper - lower, edge], axis=axis)


def project(target):
    lead = target[0]
    side = target[1:]
    wsq = jnp.sum(side * side, axis=0)
    excess = lead + 0.5 * wsq
    stretch = jnp.maximum(1.0, lead + 1.0)
    shifted = lead + 1.0
    half_again = 1.5 * wsq
    for step in range(NEWTON):
        square = stretch * stretch
        cube = square * stretch
        stretch = jnp.maximum(1.0, stretch * (shifted * square + half_again) / (cube + wsq))
    inside = excess <= 0.0
    new_lead = jnp.where(inside, lead, lead - (stretch - 1.0))
    shrink = 1.0 / stretch
    new_side = jnp.where(inside[None], side, side * shrink[None])
    return jnp.concatenate([new_lead[None], new_side], axis=0)


def cell_kernel(n_tm, n_sp, idx_ref, pc, pn, p_any, m, sd, fd, cy, cz, nm_out, pay_out,
                ft_carry, ahead_t, ahead_x, send_x, send_t, behind_t, behind_x,
                at_sems, ax_sems, bt_sems, bx_sems):
    t = pl.program_id(0)
    steps_t = pl.num_programs(0)
    rows_x, width_y, width_z = pc.shape[1], pc.shape[2], pc.shape[3]
    tm = lax.axis_index("tm")
    sp = lax.axis_index("space")
    t_glob = tm * steps_t + t
    last_t = t_glob == n_tm * steps_t - 1
    has_later_t = tm < n_tm - 1
    has_earlier_t = tm > 0
    has_later_x = sp < n_sp - 1
    has_earlier_x = sp > 0
    mesh_id = pl.DeviceIdType.MESH

    def ahead_t_copy():
        return pltpu.make_async_remote_copy(
            p_any.at[0], ahead_t, at_sems.at[0], at_sems.at[1],
            device_id=(tm - 1, sp), device_id_type=mesh_id)

    def ahead_x_copy(row):
        return pltpu.make_async_remote_copy(
            p_any.at[row, 0], ahead_x.at[row], ax_sems.at[0, row], ax_sems.at[1, row],
            device_id=(tm, sp - 1), device_id_type=mesh_id)

    def behind_t_copy(x):
        return pltpu.make_async_remote_copy(
            send_t.at[x], behind_t.at[x], bt_sems.at[0, x], bt_sems.at[1, x],
            device_id=(tm + 1, sp), device_id_type=mesh_id)

    def transform(v):
        high = lax.Precision.HIGHEST
        along_z = lax.dot_general(v, cz[...], (((1,), (1,)), ((), ())), precision=high,
                                  preferred_element_type=jnp.float32)
        return lax.dot_general(cy[...], along_z, (((1,), (0,)), ((), ())), precision=high,
                               preferred_element_type=jnp.float32)

    def behind_x_copy(row):
        return pltpu.make_async_remote_copy(
            send_x.at[row], behind_x.at[row], bx_sems.at[0, row], bx_sems.at[1, row],
            device_id=(tm, sp + 1), device_id_type=mesh_id)

    @pl.when(t == 0)
    def _():
        barrier = pltpu.get_barrier_semaphore()
        for cond, dev in ((has_earlier_t, (tm - 1, sp)), (has_later_t, (tm + 1, sp)),
                          (has_earlier_x, (tm, sp - 1)), (has_later_x, (tm, sp + 1))):
            @pl.when(cond)
            def _():
                pl.semaphore_signal(barrier, 1, device_id=dev, device_id_type=mesh_id)
        peers = (has_earlier_t.astype(jnp.int32) + has_later_t.astype(jnp.int32)
                 + has_earlier_x.astype(jnp.int32) + has_later_x.astype(jnp.int32))
        pl.semaphore_wait(barrier, peers)

        @pl.when(has_earlier_t)
        def _():
            ahead_t_copy().start()

        @pl.when(has_earlier_x)
        def _():
            for row in range(steps_t):
                ahead_x_copy(row).start()

    row = lax.broadcasted_iota(jnp.int32, (width_y, width_z), 0)
    col = lax.broadcasted_iota(jnp.int32, (width_y, width_z), 1)
    first_row = row == 0
    last_row = row == width_y - 1
    last_col = col == width_z - 1
    first_col = col == 0
    fx_prev = None
    for x in range(rows_x):
        p = pc[0, x]
        if x == 0:
            @pl.when(jnp.logical_and(t == steps_t - 1, has_later_t))
            def _():
                ahead_t_copy().wait_recv()
        nxt = lax.cond(t == steps_t - 1, lambda: ahead_t[x], lambda: pn[0, x])
        grad_t = jnp.where(last_t, 0.0, nxt - p)
        if x < rows_x - 1:
            grad_x = pc[0, x + 1] - p
        else:
            @pl.when(has_later_x)
            def _():
                ahead_x_copy(t).wait_recv()
            grad_x = lax.cond(has_later_x, lambda: ahead_x[t] - p, lambda: jnp.zeros_like(p))
        grad_y = jnp.where(last_row, 0.0, pltpu.roll(p, width_y - 1, 0) - p)
        grad_z = jnp.where(last_col, 0.0, pltpu.roll(p, width_z - 1, 1) - p)
        grads = (grad_t, grad_x, grad_y, grad_z)
        mults = tuple(m[c, 0, x] for c in range(4))
        target = tuple(g + mu * (1.0 / RATE) for g, mu in zip(grads, mults))
        lead = target[0]
        wsq = target[1] * target[1] + target[2] * target[2] + target[3] * target[3]
        excess = lead + 0.5 * wsq
        shifted = lead + 1.0
        half_again = 1.5 * wsq
        stretch = jnp.maximum(1.0, shifted)
        for step in range(NEWTON):
            square = stretch * stretch
            cube = square * stretch
            stretch = jnp.maximum(1.0, stretch * (shifted * square + half_again) / (cube + wsq))
        inside = excess <= 0.0
        shrink = 1.0 / stretch
        proj = (jnp.where(inside, lead, lead - (stretch - 1.0)),) + tuple(
            jnp.where(inside, target[c], target[c] * shrink) for c in (1, 2, 3)
        )
        flux = []
        for c in range(4):
            nm = mults[c] + RATE * (grads[c] - proj[c])
            nm_out[c, 0, x] = nm
            flux.append(nm - RATE * proj[c])
        flow_y = jnp.where(first_row, 0.0, pltpu.roll(flux[2], 1, 0)) - jnp.where(last_row, 0.0, flux[2])
        flow_z = jnp.where(first_col, 0.0, pltpu.roll(flux[3], 1, 1)) - jnp.where(last_col, 0.0, flux[3])
        rest = PROX * p - (flow_y + flow_z)
        rest = rest + jnp.where(t_glob == 0, sd[x], 0.0) - jnp.where(last_t, fd[x], 0.0)
        ft_prev = jnp.where(t == 0, 0.0, ft_carry[x])
        div_t = ft_prev - jnp.where(last_t, 0.0, flux[0])
        ft_carry[x] = flux[0]

        @pl.when(t == steps_t - 1)
        def _():
            send_t[x] = flux[0]

            @pl.when(has_later_t)
            def _():
                behind_t_copy(x).start()
        if x < rows_x - 1:
            fx_cur = flux[1]
        else:
            fx_cur = jnp.where(has_later_x, flux[1], 0.0)
            send_x[t] = flux[1]

            @pl.when(has_later_x)
            def _():
                behind_x_copy(t).start()
        div_x = -fx_cur if fx_prev is None else fx_prev - fx_cur
        fx_prev = flux[1]
        pay_out[t, x] = transform(rest - div_t - div_x)

    @pl.when(t == steps_t - 1)
    def _():
        @pl.when(has_earlier_t)
        def _():
            ahead_t_copy().wait_send()
            for x in range(rows_x):
                behind_t_copy(x).wait_recv()
                pay_out[0, x] = pay_out[0, x] - transform(behind_t[x])

        @pl.when(has_earlier_x)
        def _():
            for r in range(steps_t):
                ahead_x_copy(r).wait_send()
                behind_x_copy(r).wait_recv()
                pay_out[r, 0] = pay_out[r, 0] - transform(behind_x[r])

        @pl.when(has_later_x)
        def _():
            for r in range(steps_t):
                behind_x_copy(r).wait_send()

        @pl.when(has_later_t)
        def _():
            for x in range(rows_x):
                behind_t_copy(x).wait_send()


def cells(potential, multiplier, start_density, final_density, n_tm, n_sp):
    steps_t, rows_x, width_y, width_z = potential.shape
    idx = jnp.stack([lax.axis_index("tm"), lax.axis_index("space")]).astype(jnp.int32)
    slab = (1, rows_x, width_y, width_z)
    plane = (rows_x, width_y, width_z)
    f32 = jnp.float32
    grid_spec = pltpu.PrefetchScalarGridSpec(
        num_scalar_prefetch=1,
        grid=(steps_t,),
        in_specs=[
            pl.BlockSpec(slab, lambda t, s: (t, 0, 0, 0)),
            pl.BlockSpec(slab, lambda t, s: (jnp.minimum(t + 1, steps_t - 1), 0, 0, 0)),
            pl.BlockSpec(memory_space=pl.ANY),
            pl.BlockSpec((4, 1, rows_x, width_y, width_z), lambda t, s: (0, t, 0, 0, 0)),
            pl.BlockSpec(plane, lambda t, s: (0, 0, 0)),
            pl.BlockSpec(plane, lambda t, s: (0, 0, 0)),
            pl.BlockSpec((width_y, width_y), lambda t, s: (0, 0)),
            pl.BlockSpec((width_z, width_z), lambda t, s: (0, 0)),
        ],
        out_specs=[
            pl.BlockSpec((4, 1, rows_x, width_y, width_z), lambda t, s: (0, t, 0, 0, 0)),
            pl.BlockSpec(potential.shape, lambda t, s: (0, 0, 0, 0)),
        ],
        scratch_shapes=[
            pltpu.VMEM(plane, f32),
            pltpu.VMEM(plane, f32),
            pltpu.VMEM((steps_t, width_y, width_z), f32),
            pltpu.VMEM((steps_t, width_y, width_z), f32),
            pltpu.VMEM(plane, f32),
            pltpu.VMEM(plane, f32),
            pltpu.VMEM((steps_t, width_y, width_z), f32),
            pltpu.SemaphoreType.DMA((2,)),
            pltpu.SemaphoreType.DMA((2, steps_t)),
            pltpu.SemaphoreType.DMA((2, rows_x)),
            pltpu.SemaphoreType.DMA((2, steps_t)),
        ],
    )
    cells_n = potential.size
    return pl.pallas_call(
        functools.partial(cell_kernel, n_tm, n_sp),
        grid_spec=grid_spec,
        out_shape=[
            jax.ShapeDtypeStruct(multiplier.shape, f32),
            jax.ShapeDtypeStruct(potential.shape, f32),
        ],
        compiler_params=pltpu.CompilerParams(
            dimension_semantics=("arbitrary",), collective_id=0, has_side_effects=True
        ),
        cost_estimate=pl.CostEstimate(
            flops=cells_n * 200, transcendentals=cells_n * 11, bytes_accessed=cells_n * 4 * 12
        ),
    )(idx, potential, potential, potential, multiplier, start_density, final_density,
      cosine_table(width_y), cosine_table(width_z))

def body(potential, multiplier, start_density, final_density):
    high = lax.Precision.HIGHEST
    steps_t, rows_x, width_y, width_z = potential.shape
    n_tm = lax.axis_size("tm")
    n_sp = lax.axis_size("space")
    total_t = steps_t * n_tm
    total_x = rows_x * n_sp
    block_y = width_y // (n_tm * n_sp)
    time_at = lax.axis_index("tm") * steps_t + jnp.arange(steps_t)
    row_at = lax.axis_index("space") * rows_x + jnp.arange(rows_x)
    next_multiplier, partial = cells(
        potential, multiplier, start_density, final_density, n_tm, n_sp
    )
    cos_y = cosine_table(width_y)
    cos_z = cosine_table(width_z)
    payload = partial.transpose(2, 0, 1, 3)
    both = ("tm", "space")
    middle = lax.all_to_all(payload, both, split_axis=0, concat_axis=0, tiled=True)
    next_multiplier = jnp.where(next_multiplier == next_multiplier, next_multiplier, 0.0)
    middle, next_multiplier = lax.optimization_barrier((middle, next_multiplier))
    middle = middle.reshape(n_tm, n_sp, block_y, steps_t, rows_x, width_z)
    cos_t = cosine_table(total_t).reshape(total_t, n_tm, steps_t)
    cos_x = cosine_table(total_x).reshape(total_x, n_sp, rows_x)
    hat = jnp.einsum("kat,abytxz->kbxyz", cos_t, middle, precision=high)
    hat = jnp.einsum("jbx,kbxyz->kjyz", cos_x, hat, precision=high)
    freq_y = (
        (lax.axis_index("tm") * n_sp + lax.axis_index("space")) * block_y + jnp.arange(block_y)
    ).astype(jnp.float32)
    eig_t = eigen_at(total_t, jnp.arange(total_t, dtype=jnp.float32))
    eig_x = eigen_at(total_x, jnp.arange(total_x, dtype=jnp.float32))
    eig_y = eigen_at(width_y, freq_y)
    eig_z = eigen_at(width_z, jnp.arange(width_z, dtype=jnp.float32))
    denom = eig_t[:, None, None, None] + eig_x[None, :, None, None]
    denom = denom + eig_y[None, None, :, None] + eig_z[None, None, None, :]
    hat = hat / (RATE * denom + PROX)
    hat = jnp.einsum("atk,kjyz->atjyz", cos_t.reshape(n_tm, steps_t, total_t), hat, precision=high)
    solved = jnp.einsum("bxj,atjyz->abytxz", cos_x.reshape(n_sp, rows_x, total_x), hat, precision=high)
    solved = solved.reshape(n_tm * n_sp * block_y, steps_t, rows_x, width_z)
    local = lax.all_to_all(solved, both, split_axis=0, concat_axis=0, tiled=True)
    local = jnp.einsum("ik,ktxz->txiz", cos_y, local, precision=high)
    next_potential = jnp.einsum("ik,txyk->txyi", cos_z, local, precision=high)
    return (next_potential, next_multiplier)


def solution(mesh):
    in_specs = (
        P("tm", "space", None, None),
        P(None, "tm", "space", None, None),
        P("space", None, None),
        P("space", None, None),
    )
    out_specs = (P("tm", "space", None, None), P(None, "tm", "space", None, None))
    return jax.shard_map(body, mesh=mesh, in_specs=in_specs, out_specs=out_specs, check_vma=False)
```

```python
import functools

import jax
import jax.numpy as jnp
from jax import lax
from jax.sharding import PartitionSpec as P
from jax.experimental import pallas as pl
from jax.experimental.pallas import tpu as pltpu

NEWTON = 10


RATE = 4.0
PROX = 0.01


def from_behind(block, axis, distance):
    devices = range(lax.axis_size(axis))
    route = [(i - distance, i) for i in devices if i - distance in devices]
    return lax.ppermute(block, axis, route)


def cosine_table(length):
    freq = jnp.arange(length, dtype=jnp.float32)[:, None]
    place = jnp.arange(length, dtype=jnp.float32)[None, :]
    weight = jnp.where(freq == 0.0, jnp.sqrt(jnp.float32(0.5)), jnp.float32(1.0))
    return (
        jnp.sqrt(jnp.float32(2.0) / length)
        * weight
        * jnp.cos(jnp.pi * freq * (place + 0.5) / length)
    )


def eigen_at(length, freq):
    return 4.0 * jnp.square(jnp.sin(jnp.pi * freq / (2.0 * length)))


def adjoint(face, axis):
    size = face.shape[axis]
    inner = lax.slice_in_dim(face, 0, size - 1, axis=axis)
    edge = jnp.zeros_like(lax.slice_in_dim(face, 0, 1, axis=axis))
    return jnp.concatenate([edge, inner], axis=axis) - jnp.concatenate([inner, edge], axis=axis)


def local_diff(field, axis):
    size = field.shape[axis]
    upper = lax.slice_in_dim(field, 1, size, axis=axis)
    lower = lax.slice_in_dim(field, 0, size - 1, axis=axis)
    edge = jnp.zeros_like(lax.slice_in_dim(field, 0, 1, axis=axis))
    return jnp.concatenate([upper - lower, edge], axis=axis)


def project(target):
    lead = target[0]
    side = target[1:]
    wsq = jnp.sum(side * side, axis=0)
    excess = lead + 0.5 * wsq
    stretch = jnp.maximum(1.0, lead + 1.0)
    shifted = lead + 1.0
    half_again = 1.5 * wsq
    for step in range(NEWTON):
        square = stretch * stretch
        cube = square * stretch
        stretch = jnp.maximum(1.0, stretch * (shifted * square + half_again) / (cube + wsq))
    inside = excess <= 0.0
    new_lead = jnp.where(inside, lead, lead - (stretch - 1.0))
    shrink = 1.0 / stretch
    new_side = jnp.where(inside[None], side, side * shrink[None])
    return jnp.concatenate([new_lead[None], new_side], axis=0)


def visit(step, steps_t):
    return jnp.where(step < 2, step, jnp.where(step == 2, steps_t - 1, step - 1))


def cell_kernel(n_tm, n_sp, idx_ref, pc, pn, p_any, m, sd, fd, nm_out, pay_out,
                ft_store, ahead_t, ahead_x, send_x, send_t, behind_t, behind_x,
                at_sems, ax_sems, bt_sems, bx_sems):
    s = pl.program_id(0)
    steps_t = pl.num_programs(0)
    t = visit(s, steps_t)
    rows_x, width_y, width_z = pc.shape[1], pc.shape[2], pc.shape[3]
    tm = lax.axis_index("tm")
    sp = lax.axis_index("space")
    t_glob = tm * steps_t + t
    last_t = t_glob == n_tm * steps_t - 1
    has_later_t = tm < n_tm - 1
    has_earlier_t = tm > 0
    has_later_x = sp < n_sp - 1
    has_earlier_x = sp > 0
    mesh_id = pl.DeviceIdType.MESH

    def ahead_t_copy():
        return pltpu.make_async_remote_copy(
            p_any.at[0], ahead_t, at_sems.at[0], at_sems.at[1],
            device_id=(tm - 1, sp), device_id_type=mesh_id)

    def ahead_x_copy(row):
        return pltpu.make_async_remote_copy(
            p_any.at[row, 0], ahead_x.at[row], ax_sems.at[0, row], ax_sems.at[1, row],
            device_id=(tm, sp - 1), device_id_type=mesh_id)

    def behind_t_copy(x):
        return pltpu.make_async_remote_copy(
            send_t.at[x], behind_t.at[x], bt_sems.at[0, x], bt_sems.at[1, x],
            device_id=(tm + 1, sp), device_id_type=mesh_id)

    def behind_x_copy(row):
        return pltpu.make_async_remote_copy(
            send_x.at[row], behind_x.at[row], bx_sems.at[0, row], bx_sems.at[1, row],
            device_id=(tm, sp + 1), device_id_type=mesh_id)

    @pl.when(s == 0)
    def _():
        barrier = pltpu.get_barrier_semaphore()
        for cond, dev in ((has_earlier_t, (tm - 1, sp)), (has_later_t, (tm + 1, sp)),
                          (has_earlier_x, (tm, sp - 1)), (has_later_x, (tm, sp + 1))):
            @pl.when(cond)
            def _():
                pl.semaphore_signal(barrier, 1, device_id=dev, device_id_type=mesh_id)
        peers = (has_earlier_t.astype(jnp.int32) + has_later_t.astype(jnp.int32)
                 + has_earlier_x.astype(jnp.int32) + has_later_x.astype(jnp.int32))
        pl.semaphore_wait(barrier, peers)

        @pl.when(has_earlier_t)
        def _():
            ahead_t_copy().start()

        @pl.when(has_earlier_x)
        def _():
            rows = ahead_x.shape[0]
            for row in [0, 1, rows - 1] + list(range(2, rows - 1)):
                ahead_x_copy(row).start()

    row = lax.broadcasted_iota(jnp.int32, (width_y, width_z), 0)
    col = lax.broadcasted_iota(jnp.int32, (width_y, width_z), 1)
    first_row = row == 0
    last_row = row == width_y - 1
    last_col = col == width_z - 1
    first_col = col == 0
    fx_prev = None
    for x in range(rows_x):
        p = pc[0, x]
        if x == 0:
            @pl.when(jnp.logical_and(t == steps_t - 1, has_later_t))
            def _():
                ahead_t_copy().wait_recv()
        nxt = lax.cond(t == steps_t - 1, lambda: ahead_t[x], lambda: pn[0, x])
        grad_t = jnp.where(last_t, 0.0, nxt - p)
        if x < rows_x - 1:
            grad_x = pc[0, x + 1] - p
        else:
            @pl.when(has_later_x)
            def _():
                ahead_x_copy(t).wait_recv()
            grad_x = lax.cond(has_later_x, lambda: ahead_x[t] - p, lambda: jnp.zeros_like(p))
        grad_y = jnp.where(last_row, 0.0, pltpu.roll(p, width_y - 1, 0) - p)
        grad_z = jnp.where(last_col, 0.0, pltpu.roll(p, width_z - 1, 1) - p)
        grads = (grad_t, grad_x, grad_y, grad_z)
        mults = tuple(m[c, 0, x] for c in range(4))
        target = tuple(g + mu * (1.0 / RATE) for g, mu in zip(grads, mults))
        lead = target[0]
        wsq = target[1] * target[1] + target[2] * target[2] + target[3] * target[3]
        excess = lead + 0.5 * wsq
        shifted = lead + 1.0
        half_again = 1.5 * wsq
        stretch = jnp.maximum(1.0, shifted)
        for step in range(NEWTON):
            square = stretch * stretch
            cube = square * stretch
            stretch = jnp.maximum(1.0, stretch * (shifted * square + half_again) / (cube + wsq))
        inside = excess <= 0.0
        shrink = 1.0 / stretch
        proj = (jnp.where(inside, lead, lead - (stretch - 1.0)),) + tuple(
            jnp.where(inside, target[c], target[c] * shrink) for c in (1, 2, 3)
        )
        flux = []
        for c in range(4):
            nm = mults[c] + RATE * (grads[c] - proj[c])
            nm_out[c, 0, x] = nm
            flux.append(nm - RATE * proj[c])
        flow_y = jnp.where(first_row, 0.0, pltpu.roll(flux[2], 1, 0)) - jnp.where(last_row, 0.0, flux[2])
        flow_z = jnp.where(first_col, 0.0, pltpu.roll(flux[3], 1, 1)) - jnp.where(last_col, 0.0, flux[3])
        rest = PROX * p - (flow_y + flow_z)
        rest = rest + jnp.where(t_glob == 0, sd[x], 0.0) - jnp.where(last_t, fd[x], 0.0)
        has_prev = jnp.logical_and(t > 0, t < steps_t - 1)
        ft_prev = lax.cond(has_prev, lambda: ft_store[jnp.maximum(t - 1, 0), x], lambda: jnp.zeros_like(p))
        div_t = ft_prev - jnp.where(last_t, 0.0, flux[0])
        ft_store[t, x] = flux[0]

        @pl.when(t == steps_t - 1)
        def _():
            send_t[x] = flux[0]

            @pl.when(has_later_t)
            def _():
                behind_t_copy(x).start()
        if x < rows_x - 1:
            fx_cur = flux[1]
        else:
            fx_cur = jnp.where(has_later_x, flux[1], 0.0)
            send_x[t] = flux[1]

            @pl.when(has_later_x)
            def _():
                behind_x_copy(t).start()
        div_x = -fx_cur if fx_prev is None else fx_prev - fx_cur
        fx_prev = flux[1]
        pay_out[t, x] = rest - div_t - div_x

    @pl.when(s == steps_t - 1)
    def _():
        for x in range(rows_x):
            pay_out[steps_t - 1, x] = pay_out[steps_t - 1, x] - ft_store[steps_t - 2, x]

        @pl.when(has_earlier_t)
        def _():
            ahead_t_copy().wait_send()
            for x in range(rows_x):
                behind_t_copy(x).wait_recv()
                pay_out[0, x] = pay_out[0, x] - behind_t[x]

        @pl.when(has_earlier_x)
        def _():
            for r in range(steps_t):
                ahead_x_copy(r).wait_send()
                behind_x_copy(r).wait_recv()
                pay_out[r, 0] = pay_out[r, 0] - behind_x[r]

        @pl.when(has_later_x)
        def _():
            for r in range(steps_t):
                behind_x_copy(r).wait_send()

        @pl.when(has_later_t)
        def _():
            for x in range(rows_x):
                behind_t_copy(x).wait_send()


def cells(potential, multiplier, start_density, final_density, n_tm, n_sp):
    steps_t, rows_x, width_y, width_z = potential.shape
    idx = jnp.stack([lax.axis_index("tm"), lax.axis_index("space")]).astype(jnp.int32)
    slab = (1, rows_x, width_y, width_z)
    plane = (rows_x, width_y, width_z)
    f32 = jnp.float32
    grid_spec = pltpu.PrefetchScalarGridSpec(
        num_scalar_prefetch=1,
        grid=(steps_t,),
        in_specs=[
            pl.BlockSpec(slab, lambda i, s: (visit(i, steps_t), 0, 0, 0)),
            pl.BlockSpec(slab, lambda i, s: (jnp.minimum(visit(i, steps_t) + 1, steps_t - 1), 0, 0, 0)),
            pl.BlockSpec(memory_space=pl.ANY),
            pl.BlockSpec((4, 1, rows_x, width_y, width_z), lambda i, s: (0, visit(i, steps_t), 0, 0, 0)),
            pl.BlockSpec(plane, lambda t, s: (0, 0, 0)),
            pl.BlockSpec(plane, lambda t, s: (0, 0, 0)),
        ],
        out_specs=[
            pl.BlockSpec((4, 1, rows_x, width_y, width_z), lambda i, s: (0, visit(i, steps_t), 0, 0, 0)),
            pl.BlockSpec(potential.shape, lambda t, s: (0, 0, 0, 0)),
        ],
        scratch_shapes=[
            pltpu.VMEM((steps_t,) + plane, f32),
            pltpu.VMEM(plane, f32),
            pltpu.VMEM((steps_t, width_y, width_z), f32),
            pltpu.VMEM((steps_t, width_y, width_z), f32),
            pltpu.VMEM(plane, f32),
            pltpu.VMEM(plane, f32),
            pltpu.VMEM((steps_t, width_y, width_z), f32),
            pltpu.SemaphoreType.DMA((2,)),
            pltpu.SemaphoreType.DMA((2, steps_t)),
            pltpu.SemaphoreType.DMA((2, rows_x)),
            pltpu.SemaphoreType.DMA((2, steps_t)),
        ],
    )
    cells_n = potential.size
    return pl.pallas_call(
        functools.partial(cell_kernel, n_tm, n_sp),
        grid_spec=grid_spec,
        out_shape=[
            jax.ShapeDtypeStruct(multiplier.shape, f32),
            jax.ShapeDtypeStruct(potential.shape, f32),
        ],
        compiler_params=pltpu.CompilerParams(
            dimension_semantics=("arbitrary",), collective_id=0, has_side_effects=True
        ),
        cost_estimate=pl.CostEstimate(
            flops=cells_n * 200, transcendentals=cells_n * 11, bytes_accessed=cells_n * 4 * 12
        ),
    )(idx, potential, potential, potential, multiplier, start_density, final_density)

def body(potential, multiplier, start_density, final_density):
    high = lax.Precision.HIGHEST
    steps_t, rows_x, width_y, width_z = potential.shape
    n_tm = lax.axis_size("tm")
    n_sp = lax.axis_size("space")
    total_t = steps_t * n_tm
    total_x = rows_x * n_sp
    block_y = width_y // (n_tm * n_sp)
    time_at = lax.axis_index("tm") * steps_t + jnp.arange(steps_t)
    row_at = lax.axis_index("space") * rows_x + jnp.arange(rows_x)
    next_multiplier, partial = cells(
        potential, multiplier, start_density, final_density, n_tm, n_sp
    )
    cos_y = cosine_table(width_y)
    cos_z = cosine_table(width_z)
    payload = jnp.einsum("txyi,ki->txyk", partial, cos_z, precision=high)
    payload = jnp.einsum("txiz,ki->ktxz", payload, cos_y, precision=high)
    both = ("tm", "space")
    middle = lax.all_to_all(payload, both, split_axis=0, concat_axis=0, tiled=True)
    next_multiplier = jnp.where(next_multiplier == next_multiplier, next_multiplier, 0.0)
    middle, next_multiplier = lax.optimization_barrier((middle, next_multiplier))
    middle = middle.reshape(n_tm, n_sp, block_y, steps_t, rows_x, width_z)
    cos_t = cosine_table(total_t).reshape(total_t, n_tm, steps_t)
    cos_x = cosine_table(total_x).reshape(total_x, n_sp, rows_x)
    hat = jnp.einsum("kat,abytxz->kbxyz", cos_t, middle, precision=high)
    hat = jnp.einsum("jbx,kbxyz->kjyz", cos_x, hat, precision=high)
    freq_y = (
        (lax.axis_index("tm") * n_sp + lax.axis_index("space")) * block_y + jnp.arange(block_y)
    ).astype(jnp.float32)
    eig_t = eigen_at(total_t, jnp.arange(total_t, dtype=jnp.float32))
    eig_x = eigen_at(total_x, jnp.arange(total_x, dtype=jnp.float32))
    eig_y = eigen_at(width_y, freq_y)
    eig_z = eigen_at(width_z, jnp.arange(width_z, dtype=jnp.float32))
    denom = eig_t[:, None, None, None] + eig_x[None, :, None, None]
    denom = denom + eig_y[None, None, :, None] + eig_z[None, None, None, :]
    hat = hat / (RATE * denom + PROX)
    hat = jnp.einsum("atk,kjyz->atjyz", cos_t.reshape(n_tm, steps_t, total_t), hat, precision=high)
    solved = jnp.einsum("bxj,atjyz->abytxz", cos_x.reshape(n_sp, rows_x, total_x), hat, precision=high)
    solved = solved.reshape(n_tm * n_sp * block_y, steps_t, rows_x, width_z)
    local = lax.all_to_all(solved, both, split_axis=0, concat_axis=0, tiled=True)
    local = jnp.einsum("ik,ktxz->txiz", cos_y, local, precision=high)
    next_potential = jnp.einsum("ik,txyk->txyi", cos_z, local, precision=high)
    return (next_potential, next_multiplier)


def solution(mesh):
    in_specs = (
        P("tm", "space", None, None),
        P(None, "tm", "space", None, None),
        P("space", None, None),
        P("space", None, None),
    )
    out_specs = (P("tm", "space", None, None), P(None, "tm", "space", None, None))
    return jax.shard_map(body, mesh=mesh, in_specs=in_specs, out_specs=out_specs, check_vma=False)
```

```python
import functools

import jax
import jax.numpy as jnp
from jax import lax
from jax.sharding import PartitionSpec as P
from jax.experimental import pallas as pl
from jax.experimental.pallas import tpu as pltpu

NEWTON = 10


RATE = 4.0
PROX = 0.01


def from_behind(block, axis, distance):
    devices = range(lax.axis_size(axis))
    route = [(i - distance, i) for i in devices if i - distance in devices]
    return lax.ppermute(block, axis, route)


def cosine_table(length):
    freq = jnp.arange(length, dtype=jnp.float32)[:, None]
    place = jnp.arange(length, dtype=jnp.float32)[None, :]
    weight = jnp.where(freq == 0.0, jnp.sqrt(jnp.float32(0.5)), jnp.float32(1.0))
    return (
        jnp.sqrt(jnp.float32(2.0) / length)
        * weight
        * jnp.cos(jnp.pi * freq * (place + 0.5) / length)
    )


def eigen_at(length, freq):
    return 4.0 * jnp.square(jnp.sin(jnp.pi * freq / (2.0 * length)))


def adjoint(face, axis):
    size = face.shape[axis]
    inner = lax.slice_in_dim(face, 0, size - 1, axis=axis)
    edge = jnp.zeros_like(lax.slice_in_dim(face, 0, 1, axis=axis))
    return jnp.concatenate([edge, inner], axis=axis) - jnp.concatenate([inner, edge], axis=axis)


def local_diff(field, axis):
    size = field.shape[axis]
    upper = lax.slice_in_dim(field, 1, size, axis=axis)
    lower = lax.slice_in_dim(field, 0, size - 1, axis=axis)
    edge = jnp.zeros_like(lax.slice_in_dim(field, 0, 1, axis=axis))
    return jnp.concatenate([upper - lower, edge], axis=axis)


def project(target):
    lead = target[0]
    side = target[1:]
    wsq = jnp.sum(side * side, axis=0)
    excess = lead + 0.5 * wsq
    stretch = jnp.maximum(1.0, lead + 1.0)
    shifted = lead + 1.0
    half_again = 1.5 * wsq
    for step in range(NEWTON):
        square = stretch * stretch
        cube = square * stretch
        stretch = jnp.maximum(1.0, stretch * (shifted * square + half_again) / (cube + wsq))
    inside = excess <= 0.0
    new_lead = jnp.where(inside, lead, lead - (stretch - 1.0))
    shrink = 1.0 / stretch
    new_side = jnp.where(inside[None], side, side * shrink[None])
    return jnp.concatenate([new_lead[None], new_side], axis=0)


def visit(step, steps_t):
    return jnp.where(step < 2, step, jnp.where(step == 2, steps_t - 1, step - 1))


def cell_kernel(n_tm, n_sp, idx_ref, pc, pn, p_any, m, sd, fd, nm_out, pay_out,
                ft_store, ahead_t, ahead_x, send_x, send_t, behind_t, behind_x,
                at_sems, ax_sems, bt_sems, bx_sems):
    s = pl.program_id(0)
    steps_t = pl.num_programs(0)
    t = visit(s, steps_t)
    rows_x, width_y, width_z = pc.shape[1], pc.shape[2], pc.shape[3]
    tm = lax.axis_index("tm")
    sp = lax.axis_index("space")
    t_glob = tm * steps_t + t
    last_t = t_glob == n_tm * steps_t - 1
    has_later_t = tm < n_tm - 1
    has_earlier_t = tm > 0
    has_later_x = sp < n_sp - 1
    has_earlier_x = sp > 0
    mesh_id = pl.DeviceIdType.MESH

    def ahead_t_copy():
        return pltpu.make_async_remote_copy(
            p_any.at[0], ahead_t, at_sems.at[0], at_sems.at[1],
            device_id=(tm - 1, sp), device_id_type=mesh_id)

    def ahead_x_copy(row):
        return pltpu.make_async_remote_copy(
            p_any.at[row, 0], ahead_x.at[row], ax_sems.at[0, row], ax_sems.at[1, row],
            device_id=(tm, sp - 1), device_id_type=mesh_id)

    def behind_t_copy(x):
        return pltpu.make_async_remote_copy(
            send_t.at[x], behind_t.at[x], bt_sems.at[0, x], bt_sems.at[1, x],
            device_id=(tm + 1, sp), device_id_type=mesh_id)

    def behind_x_copy(row):
        return pltpu.make_async_remote_copy(
            send_x.at[row], behind_x.at[row], bx_sems.at[0, row], bx_sems.at[1, row],
            device_id=(tm, sp + 1), device_id_type=mesh_id)

    @pl.when(s == 0)
    def _():
        barrier = pltpu.get_barrier_semaphore()
        for cond, dev in ((has_earlier_t, (tm - 1, sp)), (has_later_t, (tm + 1, sp)),
                          (has_earlier_x, (tm, sp - 1)), (has_later_x, (tm, sp + 1))):
            @pl.when(cond)
            def _():
                pl.semaphore_signal(barrier, 1, device_id=dev, device_id_type=mesh_id)
        peers = (has_earlier_t.astype(jnp.int32) + has_later_t.astype(jnp.int32)
                 + has_earlier_x.astype(jnp.int32) + has_later_x.astype(jnp.int32))
        pl.semaphore_wait(barrier, peers)

        @pl.when(has_earlier_t)
        def _():
            ahead_t_copy().start()

        @pl.when(has_earlier_x)
        def _():
            rows = ahead_x.shape[0]
            for row in [0, 1, rows - 1] + list(range(2, rows - 1)):
                ahead_x_copy(row).start()

    row = lax.broadcasted_iota(jnp.int32, (width_y, width_z), 0)
    col = lax.broadcasted_iota(jnp.int32, (width_y, width_z), 1)
    first_row = row == 0
    last_row = row == width_y - 1
    last_col = col == width_z - 1
    first_col = col == 0
    fx_prev = None
    for x in range(rows_x):
        p = pc[0, x]
        if x == 0:
            @pl.when(jnp.logical_and(t == steps_t - 1, has_later_t))
            def _():
                ahead_t_copy().wait_recv()
        nxt = lax.cond(t == steps_t - 1, lambda: ahead_t[x], lambda: pn[0, x])
        grad_t = jnp.where(last_t, 0.0, nxt - p)
        if x < rows_x - 1:
            grad_x = pc[0, x + 1] - p
        else:
            @pl.when(has_later_x)
            def _():
                ahead_x_copy(t).wait_recv()
            grad_x = lax.cond(has_later_x, lambda: ahead_x[t] - p, lambda: jnp.zeros_like(p))
        grad_y = jnp.where(last_row, 0.0, pltpu.roll(p, width_y - 1, 0) - p)
        grad_z = jnp.where(last_col, 0.0, pltpu.roll(p, width_z - 1, 1) - p)
        grads = (grad_t, grad_x, grad_y, grad_z)
        mults = tuple(m[c, 0, x] for c in range(4))
        target = tuple(g + mu * (1.0 / RATE) for g, mu in zip(grads, mults))
        lead = target[0]
        wsq = target[1] * target[1] + target[2] * target[2] + target[3] * target[3]
        excess = lead + 0.5 * wsq
        shifted = lead + 1.0
        half_again = 1.5 * wsq
        stretch = jnp.maximum(1.0, shifted)
        for step in range(NEWTON):
            square = stretch * stretch
            cube = square * stretch
            stretch = jnp.maximum(1.0, stretch * (shifted * square + half_again) / (cube + wsq))
        inside = excess <= 0.0
        shrink = 1.0 / stretch
        proj = (jnp.where(inside, lead, lead - (stretch - 1.0)),) + tuple(
            jnp.where(inside, target[c], target[c] * shrink) for c in (1, 2, 3)
        )
        flux = []
        for c in range(4):
            nm = mults[c] + RATE * (grads[c] - proj[c])
            nm_out[c, 0, x] = nm
            flux.append(nm - RATE * proj[c])
        flow_y = jnp.where(first_row, 0.0, pltpu.roll(flux[2], 1, 0)) - jnp.where(last_row, 0.0, flux[2])
        flow_z = jnp.where(first_col, 0.0, pltpu.roll(flux[3], 1, 1)) - jnp.where(last_col, 0.0, flux[3])
        rest = PROX * p - (flow_y + flow_z)
        rest = rest + jnp.where(t_glob == 0, sd[x], 0.0) - jnp.where(last_t, fd[x], 0.0)
        has_prev = jnp.logical_and(t > 0, t < steps_t - 1)
        ft_prev = lax.cond(has_prev, lambda: ft_store[jnp.maximum(t - 1, 0), x], lambda: jnp.zeros_like(p))
        div_t = ft_prev - jnp.where(last_t, 0.0, flux[0])
        ft_store[t, x] = flux[0]

        @pl.when(t == steps_t - 1)
        def _():
            send_t[x] = flux[0]

            @pl.when(has_later_t)
            def _():
                behind_t_copy(x).start()
        if x < rows_x - 1:
            fx_cur = flux[1]
        else:
            fx_cur = jnp.where(has_later_x, flux[1], 0.0)
            send_x[t] = flux[1]

            @pl.when(has_later_x)
            def _():
                behind_x_copy(t).start()
        div_x = -fx_cur if fx_prev is None else fx_prev - fx_cur
        fx_prev = flux[1]
        pay_out[t, x] = rest - div_t - div_x

    @pl.when(s == steps_t - 1)
    def _():
        for x in range(rows_x):
            pay_out[steps_t - 1, x] = pay_out[steps_t - 1, x] - ft_store[steps_t - 2, x]

        @pl.when(has_earlier_t)
        def _():
            ahead_t_copy().wait_send()
            for x in range(rows_x):
                behind_t_copy(x).wait_recv()
                pay_out[0, x] = pay_out[0, x] - behind_t[x]

        @pl.when(has_earlier_x)
        def _():
            for r in range(steps_t):
                ahead_x_copy(r).wait_send()
                behind_x_copy(r).wait_recv()
                pay_out[r, 0] = pay_out[r, 0] - behind_x[r]

        @pl.when(has_later_x)
        def _():
            for r in range(steps_t):
                behind_x_copy(r).wait_send()

        @pl.when(has_later_t)
        def _():
            for x in range(rows_x):
                behind_t_copy(x).wait_send()


def cells(potential, multiplier, start_density, final_density, n_tm, n_sp):
    steps_t, rows_x, width_y, width_z = potential.shape
    idx = jnp.stack([lax.axis_index("tm"), lax.axis_index("space")]).astype(jnp.int32)
    slab = (1, rows_x, width_y, width_z)
    plane = (rows_x, width_y, width_z)
    f32 = jnp.float32
    grid_spec = pltpu.PrefetchScalarGridSpec(
        num_scalar_prefetch=1,
        grid=(steps_t,),
        in_specs=[
            pl.BlockSpec(slab, lambda i, s: (visit(i, steps_t), 0, 0, 0)),
            pl.BlockSpec(slab, lambda i, s: (jnp.minimum(visit(i, steps_t) + 1, steps_t - 1), 0, 0, 0)),
            pl.BlockSpec(memory_space=pl.ANY),
            pl.BlockSpec((4, 1, rows_x, width_y, width_z), lambda i, s: (0, visit(i, steps_t), 0, 0, 0)),
            pl.BlockSpec(plane, lambda t, s: (0, 0, 0)),
            pl.BlockSpec(plane, lambda t, s: (0, 0, 0)),
        ],
        out_specs=[
            pl.BlockSpec((4, 1, rows_x, width_y, width_z), lambda i, s: (0, visit(i, steps_t), 0, 0, 0)),
            pl.BlockSpec(potential.shape, lambda t, s: (0, 0, 0, 0)),
        ],
        scratch_shapes=[
            pltpu.VMEM((steps_t,) + plane, f32),
            pltpu.VMEM(plane, f32),
            pltpu.VMEM((steps_t, width_y, width_z), f32),
            pltpu.VMEM((steps_t, width_y, width_z), f32),
            pltpu.VMEM(plane, f32),
            pltpu.VMEM(plane, f32),
            pltpu.VMEM((steps_t, width_y, width_z), f32),
            pltpu.SemaphoreType.DMA((2,)),
            pltpu.SemaphoreType.DMA((2, steps_t)),
            pltpu.SemaphoreType.DMA((2, rows_x)),
            pltpu.SemaphoreType.DMA((2, steps_t)),
        ],
    )
    cells_n = potential.size
    return pl.pallas_call(
        functools.partial(cell_kernel, n_tm, n_sp),
        grid_spec=grid_spec,
        out_shape=[
            jax.ShapeDtypeStruct(multiplier.shape, f32),
            jax.ShapeDtypeStruct(potential.shape, f32),
        ],
        compiler_params=pltpu.CompilerParams(
            dimension_semantics=("arbitrary",), collective_id=0, has_side_effects=True
        ),
        cost_estimate=pl.CostEstimate(
            flops=cells_n * 200, transcendentals=cells_n * 11, bytes_accessed=cells_n * 4 * 12
        ),
    )(idx, potential, potential, potential, multiplier, start_density, final_density)

def body(potential, multiplier, start_density, final_density):
    high = lax.Precision.HIGH
    steps_t, rows_x, width_y, width_z = potential.shape
    n_tm = lax.axis_size("tm")
    n_sp = lax.axis_size("space")
    total_t = steps_t * n_tm
    total_x = rows_x * n_sp
    block_y = width_y // (n_tm * n_sp)
    time_at = lax.axis_index("tm") * steps_t + jnp.arange(steps_t)
    row_at = lax.axis_index("space") * rows_x + jnp.arange(rows_x)
    next_multiplier, partial = cells(
        potential, multiplier, start_density, final_density, n_tm, n_sp
    )
    cos_y = cosine_table(width_y)
    cos_z = cosine_table(width_z)
    payload = jnp.einsum("txyi,ki->txyk", partial, cos_z, precision=high)
    payload = jnp.einsum("txiz,ki->ktxz", payload, cos_y, precision=high)
    both = ("tm", "space")
    middle = lax.all_to_all(payload, both, split_axis=0, concat_axis=0, tiled=True)
    next_multiplier = jnp.where(next_multiplier == next_multiplier, next_multiplier, 0.0)
    middle, next_multiplier = lax.optimization_barrier((middle, next_multiplier))
    middle = middle.reshape(n_tm, n_sp, block_y, steps_t, rows_x, width_z)
    cos_t = cosine_table(total_t).reshape(total_t, n_tm, steps_t)
    cos_x = cosine_table(total_x).reshape(total_x, n_sp, rows_x)
    hat = jnp.einsum("kat,abytxz->kbxyz", cos_t, middle, precision=high)
    hat = jnp.einsum("jbx,kbxyz->kjyz", cos_x, hat, precision=high)
    freq_y = (
        (lax.axis_index("tm") * n_sp + lax.axis_index("space")) * block_y + jnp.arange(block_y)
    ).astype(jnp.float32)
    eig_t = eigen_at(total_t, jnp.arange(total_t, dtype=jnp.float32))
    eig_x = eigen_at(total_x, jnp.arange(total_x, dtype=jnp.float32))
    eig_y = eigen_at(width_y, freq_y)
    eig_z = eigen_at(width_z, jnp.arange(width_z, dtype=jnp.float32))
    denom = eig_t[:, None, None, None] + eig_x[None, :, None, None]
    denom = denom + eig_y[None, None, :, None] + eig_z[None, None, None, :]
    hat = hat / (RATE * denom + PROX)
    hat = jnp.einsum("atk,kjyz->atjyz", cos_t.reshape(n_tm, steps_t, total_t), hat, precision=high)
    solved = jnp.einsum("bxj,atjyz->abytxz", cos_x.reshape(n_sp, rows_x, total_x), hat, precision=high)
    solved = solved.reshape(n_tm * n_sp * block_y, steps_t, rows_x, width_z)
    local = lax.all_to_all(solved, both, split_axis=0, concat_axis=0, tiled=True)
    local = jnp.einsum("ik,ktxz->txiz", cos_y, local, precision=high)
    next_potential = jnp.einsum("ik,txyk->txyi", cos_z, local, precision=high)
    return (next_potential, next_multiplier)


def solution(mesh):
    in_specs = (
        P("tm", "space", None, None),
        P(None, "tm", "space", None, None),
        P("space", None, None),
        P("space", None, None),
    )
    out_specs = (P("tm", "space", None, None), P(None, "tm", "space", None, None))
    return jax.shard_map(body, mesh=mesh, in_specs=in_specs, out_specs=out_specs, check_vma=False)
```

```python
import functools

import jax
import jax.numpy as jnp
from jax import lax
from jax.sharding import PartitionSpec as P
from jax.experimental import pallas as pl
from jax.experimental.pallas import tpu as pltpu

NEWTON = 10


RATE = 4.0
PROX = 0.01


def from_behind(block, axis, distance):
    devices = range(lax.axis_size(axis))
    route = [(i - distance, i) for i in devices if i - distance in devices]
    return lax.ppermute(block, axis, route)


def cosine_table(length):
    freq = jnp.arange(length, dtype=jnp.float32)[:, None]
    place = jnp.arange(length, dtype=jnp.float32)[None, :]
    weight = jnp.where(freq == 0.0, jnp.sqrt(jnp.float32(0.5)), jnp.float32(1.0))
    return (
        jnp.sqrt(jnp.float32(2.0) / length)
        * weight
        * jnp.cos(jnp.pi * freq * (place + 0.5) / length)
    )


def eigen_at(length, freq):
    return 4.0 * jnp.square(jnp.sin(jnp.pi * freq / (2.0 * length)))


def adjoint(face, axis):
    size = face.shape[axis]
    inner = lax.slice_in_dim(face, 0, size - 1, axis=axis)
    edge = jnp.zeros_like(lax.slice_in_dim(face, 0, 1, axis=axis))
    return jnp.concatenate([edge, inner], axis=axis) - jnp.concatenate([inner, edge], axis=axis)


def local_diff(field, axis):
    size = field.shape[axis]
    upper = lax.slice_in_dim(field, 1, size, axis=axis)
    lower = lax.slice_in_dim(field, 0, size - 1, axis=axis)
    edge = jnp.zeros_like(lax.slice_in_dim(field, 0, 1, axis=axis))
    return jnp.concatenate([upper - lower, edge], axis=axis)


def project(target):
    lead = target[0]
    side = target[1:]
    wsq = jnp.sum(side * side, axis=0)
    excess = lead + 0.5 * wsq
    stretch = jnp.maximum(1.0, lead + 1.0)
    shifted = lead + 1.0
    half_again = 1.5 * wsq
    for step in range(NEWTON):
        square = stretch * stretch
        cube = square * stretch
        stretch = jnp.maximum(1.0, stretch * (shifted * square + half_again) / (cube + wsq))
    inside = excess <= 0.0
    new_lead = jnp.where(inside, lead, lead - (stretch - 1.0))
    shrink = 1.0 / stretch
    new_side = jnp.where(inside[None], side, side * shrink[None])
    return jnp.concatenate([new_lead[None], new_side], axis=0)


def visit(step, steps_t):
    return jnp.where(step < 3, step, jnp.where(step == 3, steps_t - 1, step - 1))


def cell_kernel(n_tm, n_sp, idx_ref, pc, pn, p_any, m, sd, fd, nm_out, pay_out,
                ft_store, ahead_t, ahead_x, send_x, send_t, behind_t, behind_x,
                at_sems, ax_sems, bt_sems, bx_sems):
    s = pl.program_id(0)
    steps_t = pl.num_programs(0)
    t = visit(s, steps_t)
    rows_x, width_y, width_z = pc.shape[1], pc.shape[2], pc.shape[3]
    tm = lax.axis_index("tm")
    sp = lax.axis_index("space")
    t_glob = tm * steps_t + t
    last_t = t_glob == n_tm * steps_t - 1
    has_later_t = tm < n_tm - 1
    has_earlier_t = tm > 0
    has_later_x = sp < n_sp - 1
    has_earlier_x = sp > 0
    mesh_id = pl.DeviceIdType.MESH

    def ahead_t_copy(x):
        return pltpu.make_async_remote_copy(
            p_any.at[0, x], ahead_t.at[x], at_sems.at[0, x], at_sems.at[1, x],
            device_id=(tm - 1, sp), device_id_type=mesh_id)

    def ahead_x_copy(row):
        return pltpu.make_async_remote_copy(
            p_any.at[row, 0], ahead_x.at[row], ax_sems.at[0, row], ax_sems.at[1, row],
            device_id=(tm, sp - 1), device_id_type=mesh_id)

    def behind_t_copy(x):
        return pltpu.make_async_remote_copy(
            send_t.at[x], behind_t.at[x], bt_sems.at[0, x], bt_sems.at[1, x],
            device_id=(tm + 1, sp), device_id_type=mesh_id)

    def behind_x_copy(row):
        return pltpu.make_async_remote_copy(
            send_x.at[row], behind_x.at[row], bx_sems.at[0, row], bx_sems.at[1, row],
            device_id=(tm, sp + 1), device_id_type=mesh_id)

    @pl.when(s == 0)
    def _():
        barrier = pltpu.get_barrier_semaphore()
        for cond, dev in ((has_earlier_t, (tm - 1, sp)), (has_later_t, (tm + 1, sp)),
                          (has_earlier_x, (tm, sp - 1)), (has_later_x, (tm, sp + 1))):
            @pl.when(cond)
            def _():
                pl.semaphore_signal(barrier, 1, device_id=dev, device_id_type=mesh_id)
        peers = (has_earlier_t.astype(jnp.int32) + has_later_t.astype(jnp.int32)
                 + has_earlier_x.astype(jnp.int32) + has_later_x.astype(jnp.int32))
        pl.semaphore_wait(barrier, peers)

        @pl.when(has_earlier_t)
        def _():
            for x in range(rows_x):
                ahead_t_copy(x).start()

        @pl.when(has_earlier_x)
        def _():
            rows = ahead_x.shape[0]
            for row in [0, 1, 2, rows - 1] + list(range(3, rows - 1)):
                ahead_x_copy(row).start()

    row = lax.broadcasted_iota(jnp.int32, (width_y, width_z), 0)
    col = lax.broadcasted_iota(jnp.int32, (width_y, width_z), 1)
    first_row = row == 0
    last_row = row == width_y - 1
    last_col = col == width_z - 1
    first_col = col == 0
    fx_prev = None
    for x in range(rows_x):
        p = pc[0, x]
        @pl.when(jnp.logical_and(t == steps_t - 1, has_later_t))
        def _():
            ahead_t_copy(x).wait_recv()
        nxt = lax.cond(t == steps_t - 1, lambda: ahead_t[x], lambda: pn[0, x])
        grad_t = jnp.where(last_t, 0.0, nxt - p)
        if x < rows_x - 1:
            grad_x = pc[0, x + 1] - p
        else:
            @pl.when(has_later_x)
            def _():
                ahead_x_copy(t).wait_recv()
            grad_x = lax.cond(has_later_x, lambda: ahead_x[t] - p, lambda: jnp.zeros_like(p))
        grad_y = jnp.where(last_row, 0.0, pltpu.roll(p, width_y - 1, 0) - p)
        grad_z = jnp.where(last_col, 0.0, pltpu.roll(p, width_z - 1, 1) - p)
        grads = (grad_t, grad_x, grad_y, grad_z)
        mults = tuple(m[c, 0, x] for c in range(4))
        target = tuple(g + mu * (1.0 / RATE) for g, mu in zip(grads, mults))
        lead = target[0]
        wsq = target[1] * target[1] + target[2] * target[2] + target[3] * target[3]
        excess = lead + 0.5 * wsq
        shifted = lead + 1.0
        half_again = 1.5 * wsq
        stretch = jnp.maximum(1.0, shifted)
        for step in range(NEWTON):
            square = stretch * stretch
            cube = square * stretch
            stretch = jnp.maximum(1.0, stretch * (shifted * square + half_again) / (cube + wsq))
        inside = excess <= 0.0
        shrink = 1.0 / stretch
        proj = (jnp.where(inside, lead, lead - (stretch - 1.0)),) + tuple(
            jnp.where(inside, target[c], target[c] * shrink) for c in (1, 2, 3)
        )
        flux = []
        for c in range(4):
            nm = mults[c] + RATE * (grads[c] - proj[c])
            nm_out[c, 0, x] = nm
            flux.append(nm - RATE * proj[c])
        flow_y = jnp.where(first_row, 0.0, pltpu.roll(flux[2], 1, 0)) - jnp.where(last_row, 0.0, flux[2])
        flow_z = jnp.where(first_col, 0.0, pltpu.roll(flux[3], 1, 1)) - jnp.where(last_col, 0.0, flux[3])
        rest = PROX * p - (flow_y + flow_z)
        rest = rest + jnp.where(t_glob == 0, sd[x], 0.0) - jnp.where(last_t, fd[x], 0.0)
        has_prev = jnp.logical_and(t > 0, t < steps_t - 1)
        ft_prev = lax.cond(has_prev, lambda: ft_store[jnp.maximum(t - 1, 0), x], lambda: jnp.zeros_like(p))
        div_t = ft_prev - jnp.where(last_t, 0.0, flux[0])
        ft_store[t, x] = flux[0]

        @pl.when(t == steps_t - 1)
        def _():
            send_t[x] = flux[0]

            @pl.when(has_later_t)
            def _():
                behind_t_copy(x).start()
        if x < rows_x - 1:
            fx_cur = flux[1]
        else:
            fx_cur = jnp.where(has_later_x, flux[1], 0.0)
            send_x[t] = flux[1]

            @pl.when(has_later_x)
            def _():
                behind_x_copy(t).start()
        div_x = -fx_cur if fx_prev is None else fx_prev - fx_cur
        fx_prev = flux[1]
        pay_out[t, x] = rest - div_t - div_x

    @pl.when(s == steps_t - 1)
    def _():
        for x in range(rows_x):
            pay_out[steps_t - 1, x] = pay_out[steps_t - 1, x] - ft_store[steps_t - 2, x]

        @pl.when(has_earlier_t)
        def _():
            for x in range(rows_x):
                ahead_t_copy(x).wait_send()
            for x in range(rows_x):
                behind_t_copy(x).wait_recv()
                pay_out[0, x] = pay_out[0, x] - behind_t[x]

        @pl.when(has_earlier_x)
        def _():
            for r in range(steps_t):
                ahead_x_copy(r).wait_send()
                behind_x_copy(r).wait_recv()
                pay_out[r, 0] = pay_out[r, 0] - behind_x[r]

        @pl.when(has_later_x)
        def _():
            for r in range(steps_t):
                behind_x_copy(r).wait_send()

        @pl.when(has_later_t)
        def _():
            for x in range(rows_x):
                behind_t_copy(x).wait_send()


def cells(potential, multiplier, start_density, final_density, n_tm, n_sp):
    steps_t, rows_x, width_y, width_z = potential.shape
    idx = jnp.stack([lax.axis_index("tm"), lax.axis_index("space")]).astype(jnp.int32)
    slab = (1, rows_x, width_y, width_z)
    plane = (rows_x, width_y, width_z)
    f32 = jnp.float32
    grid_spec = pltpu.PrefetchScalarGridSpec(
        num_scalar_prefetch=1,
        grid=(steps_t,),
        in_specs=[
            pl.BlockSpec(slab, lambda i, s: (visit(i, steps_t), 0, 0, 0)),
            pl.BlockSpec(slab, lambda i, s: (jnp.minimum(visit(i, steps_t) + 1, steps_t - 1), 0, 0, 0)),
            pl.BlockSpec(memory_space=pl.ANY),
            pl.BlockSpec((4, 1, rows_x, width_y, width_z), lambda i, s: (0, visit(i, steps_t), 0, 0, 0)),
            pl.BlockSpec(plane, lambda t, s: (0, 0, 0)),
            pl.BlockSpec(plane, lambda t, s: (0, 0, 0)),
        ],
        out_specs=[
            pl.BlockSpec((4, 1, rows_x, width_y, width_z), lambda i, s: (0, visit(i, steps_t), 0, 0, 0)),
            pl.BlockSpec(potential.shape, lambda t, s: (0, 0, 0, 0)),
        ],
        scratch_shapes=[
            pltpu.VMEM((steps_t,) + plane, f32),
            pltpu.VMEM(plane, f32),
            pltpu.VMEM((steps_t, width_y, width_z), f32),
            pltpu.VMEM((steps_t, width_y, width_z), f32),
            pltpu.VMEM(plane, f32),
            pltpu.VMEM(plane, f32),
            pltpu.VMEM((steps_t, width_y, width_z), f32),
            pltpu.SemaphoreType.DMA((2, rows_x)),
            pltpu.SemaphoreType.DMA((2, steps_t)),
            pltpu.SemaphoreType.DMA((2, rows_x)),
            pltpu.SemaphoreType.DMA((2, steps_t)),
        ],
    )
    cells_n = potential.size
    return pl.pallas_call(
        functools.partial(cell_kernel, n_tm, n_sp),
        grid_spec=grid_spec,
        out_shape=[
            jax.ShapeDtypeStruct(multiplier.shape, f32),
            jax.ShapeDtypeStruct(potential.shape, f32),
        ],
        compiler_params=pltpu.CompilerParams(
            dimension_semantics=("arbitrary",), collective_id=0, has_side_effects=True
        ),
        cost_estimate=pl.CostEstimate(
            flops=cells_n * 200, transcendentals=cells_n * 11, bytes_accessed=cells_n * 4 * 12
        ),
    )(idx, potential, potential, potential, multiplier, start_density, final_density)

def body(potential, multiplier, start_density, final_density):
    high = lax.Precision.HIGH
    steps_t, rows_x, width_y, width_z = potential.shape
    n_tm = lax.axis_size("tm")
    n_sp = lax.axis_size("space")
    total_t = steps_t * n_tm
    total_x = rows_x * n_sp
    block_y = width_y // (n_tm * n_sp)
    time_at = lax.axis_index("tm") * steps_t + jnp.arange(steps_t)
    row_at = lax.axis_index("space") * rows_x + jnp.arange(rows_x)
    next_multiplier, partial = cells(
        potential, multiplier, start_density, final_density, n_tm, n_sp
    )
    cos_y = cosine_table(width_y)
    cos_z = cosine_table(width_z)
    payload = jnp.einsum("txyi,ki->txyk", partial, cos_z, precision=high)
    payload = jnp.einsum("txiz,ki->ktxz", payload, cos_y, precision=high)
    both = ("tm", "space")
    middle = lax.all_to_all(payload, both, split_axis=0, concat_axis=0, tiled=True)
    next_multiplier = jnp.where(next_multiplier == next_multiplier, next_multiplier, 0.0)
    middle, next_multiplier = lax.optimization_barrier((middle, next_multiplier))
    middle = middle.reshape(n_tm, n_sp, block_y, steps_t, rows_x, width_z)
    cos_t = cosine_table(total_t).reshape(total_t, n_tm, steps_t)
    cos_x = cosine_table(total_x).reshape(total_x, n_sp, rows_x)
    hat = jnp.einsum("kat,abytxz->kbxyz", cos_t, middle, precision=high)
    hat = jnp.einsum("jbx,kbxyz->kjyz", cos_x, hat, precision=high)
    freq_y = (
        (lax.axis_index("tm") * n_sp + lax.axis_index("space")) * block_y + jnp.arange(block_y)
    ).astype(jnp.float32)
    eig_t = eigen_at(total_t, jnp.arange(total_t, dtype=jnp.float32))
    eig_x = eigen_at(total_x, jnp.arange(total_x, dtype=jnp.float32))
    eig_y = eigen_at(width_y, freq_y)
    eig_z = eigen_at(width_z, jnp.arange(width_z, dtype=jnp.float32))
    denom = eig_t[:, None, None, None] + eig_x[None, :, None, None]
    denom = denom + eig_y[None, None, :, None] + eig_z[None, None, None, :]
    hat = hat / (RATE * denom + PROX)
    hat = jnp.einsum("atk,kjyz->atjyz", cos_t.reshape(n_tm, steps_t, total_t), hat, precision=high)
    solved = jnp.einsum("bxj,atjyz->abytxz", cos_x.reshape(n_sp, rows_x, total_x), hat, precision=high)
    solved = solved.reshape(n_tm * n_sp * block_y, steps_t, rows_x, width_z)
    local = lax.all_to_all(solved, both, split_axis=0, concat_axis=0, tiled=True)
    local = jnp.einsum("ik,ktxz->txiz", cos_y, local, precision=high)
    next_potential = jnp.einsum("ik,txyk->txyi", cos_z, local, precision=high)
    return (next_potential, next_multiplier)


def solution(mesh):
    in_specs = (
        P("tm", "space", None, None),
        P(None, "tm", "space", None, None),
        P("space", None, None),
        P("space", None, None),
    )
    out_specs = (P("tm", "space", None, None), P(None, "tm", "space", None, None))
    return jax.shard_map(body, mesh=mesh, in_specs=in_specs, out_specs=out_specs, check_vma=False)
```

```python
import functools

import jax
import jax.numpy as jnp
from jax import lax
from jax.sharding import PartitionSpec as P
from jax.experimental import pallas as pl
from jax.experimental.pallas import tpu as pltpu

NEWTON = 10


RATE = 4.0
PROX = 0.01


def from_behind(block, axis, distance):
    devices = range(lax.axis_size(axis))
    route = [(i - distance, i) for i in devices if i - distance in devices]
    return lax.ppermute(block, axis, route)


def cosine_table(length):
    freq = jnp.arange(length, dtype=jnp.float32)[:, None]
    place = jnp.arange(length, dtype=jnp.float32)[None, :]
    weight = jnp.where(freq == 0.0, jnp.sqrt(jnp.float32(0.5)), jnp.float32(1.0))
    return (
        jnp.sqrt(jnp.float32(2.0) / length)
        * weight
        * jnp.cos(jnp.pi * freq * (place + 0.5) / length)
    )


def eigen_at(length, freq):
    return 4.0 * jnp.square(jnp.sin(jnp.pi * freq / (2.0 * length)))


def adjoint(face, axis):
    size = face.shape[axis]
    inner = lax.slice_in_dim(face, 0, size - 1, axis=axis)
    edge = jnp.zeros_like(lax.slice_in_dim(face, 0, 1, axis=axis))
    return jnp.concatenate([edge, inner], axis=axis) - jnp.concatenate([inner, edge], axis=axis)


def local_diff(field, axis):
    size = field.shape[axis]
    upper = lax.slice_in_dim(field, 1, size, axis=axis)
    lower = lax.slice_in_dim(field, 0, size - 1, axis=axis)
    edge = jnp.zeros_like(lax.slice_in_dim(field, 0, 1, axis=axis))
    return jnp.concatenate([upper - lower, edge], axis=axis)


def project(target):
    lead = target[0]
    side = target[1:]
    wsq = jnp.sum(side * side, axis=0)
    excess = lead + 0.5 * wsq
    stretch = jnp.maximum(1.0, lead + 1.0)
    shifted = lead + 1.0
    half_again = 1.5 * wsq
    for step in range(NEWTON):
        square = stretch * stretch
        cube = square * stretch
        stretch = jnp.maximum(1.0, stretch * (shifted * square + half_again) / (cube + wsq))
    inside = excess <= 0.0
    new_lead = jnp.where(inside, lead, lead - (stretch - 1.0))
    shrink = 1.0 / stretch
    new_side = jnp.where(inside[None], side, side * shrink[None])
    return jnp.concatenate([new_lead[None], new_side], axis=0)


def visit(step, steps_t):
    return jnp.where(step < 2, step, jnp.where(step == 2, steps_t - 1, step - 1))


def cell_kernel(n_tm, n_sp, idx_ref, pc, pn, p_any, m, sd, fd, nm_out, pay_out,
                ft_store, ahead_t, ahead_x, send_x, send_t, behind_t, behind_x,
                at_sems, ax_sems, bt_sems, bx_sems):
    s = pl.program_id(0)
    steps_t = pl.num_programs(0)
    t = visit(s, steps_t)
    rows_x, width_y, width_z = pc.shape[1], pc.shape[2], pc.shape[3]
    tm = lax.axis_index("tm")
    sp = lax.axis_index("space")
    t_glob = tm * steps_t + t
    last_t = t_glob == n_tm * steps_t - 1
    has_later_t = tm < n_tm - 1
    has_earlier_t = tm > 0
    has_later_x = sp < n_sp - 1
    has_earlier_x = sp > 0
    mesh_id = pl.DeviceIdType.MESH

    def ahead_t_copy():
        return pltpu.make_async_remote_copy(
            p_any.at[0], ahead_t, at_sems.at[0], at_sems.at[1],
            device_id=(tm - 1, sp), device_id_type=mesh_id)

    def ahead_x_copy(row):
        return pltpu.make_async_remote_copy(
            p_any.at[row, 0], ahead_x.at[row], ax_sems.at[0, row], ax_sems.at[1, row],
            device_id=(tm, sp - 1), device_id_type=mesh_id)

    def behind_t_copy(x):
        return pltpu.make_async_remote_copy(
            send_t.at[x], behind_t.at[x], bt_sems.at[0, x], bt_sems.at[1, x],
            device_id=(tm + 1, sp), device_id_type=mesh_id)

    def behind_x_copy(row):
        return pltpu.make_async_remote_copy(
            send_x.at[row], behind_x.at[row], bx_sems.at[0, row], bx_sems.at[1, row],
            device_id=(tm, sp + 1), device_id_type=mesh_id)

    @pl.when(s == 0)
    def _():
        barrier = pltpu.get_barrier_semaphore()
        for cond, dev in ((has_earlier_t, (tm - 1, sp)), (has_later_t, (tm + 1, sp)),
                          (has_earlier_x, (tm, sp - 1)), (has_later_x, (tm, sp + 1))):
            @pl.when(cond)
            def _():
                pl.semaphore_signal(barrier, 1, device_id=dev, device_id_type=mesh_id)
        peers = (has_earlier_t.astype(jnp.int32) + has_later_t.astype(jnp.int32)
                 + has_earlier_x.astype(jnp.int32) + has_later_x.astype(jnp.int32))
        pl.semaphore_wait(barrier, peers)

        @pl.when(has_earlier_t)
        def _():
            ahead_t_copy().start()

        @pl.when(has_earlier_x)
        def _():
            rows = ahead_x.shape[0]
            for row in [0, 1, rows - 1] + list(range(2, rows - 1)):
                ahead_x_copy(row).start()

    row = lax.broadcasted_iota(jnp.int32, (width_y, width_z), 0)
    col = lax.broadcasted_iota(jnp.int32, (width_y, width_z), 1)
    first_row = row == 0
    last_row = row == width_y - 1
    last_col = col == width_z - 1
    first_col = col == 0
    def rows_in(order):
        fx_done = {}
        for x in order:
            p = pc[0, x]
            if x == order[0]:
                @pl.when(jnp.logical_and(t == steps_t - 1, has_later_t))
                def _():
                    ahead_t_copy().wait_recv()
            nxt = lax.cond(t == steps_t - 1, lambda: ahead_t[x], lambda: pn[0, x])
            grad_t = jnp.where(last_t, 0.0, nxt - p)
            if x < rows_x - 1:
                grad_x = pc[0, x + 1] - p
            else:
                @pl.when(has_later_x)
                def _():
                    ahead_x_copy(t).wait_recv()
                grad_x = lax.cond(has_later_x, lambda: ahead_x[t] - p, lambda: jnp.zeros_like(p))
            grad_y = jnp.where(last_row, 0.0, pltpu.roll(p, width_y - 1, 0) - p)
            grad_z = jnp.where(last_col, 0.0, pltpu.roll(p, width_z - 1, 1) - p)
            grads = (grad_t, grad_x, grad_y, grad_z)
            mults = tuple(m[c, 0, x] for c in range(4))
            target = tuple(g + mu * (1.0 / RATE) for g, mu in zip(grads, mults))
            lead = target[0]
            wsq = target[1] * target[1] + target[2] * target[2] + target[3] * target[3]
            excess = lead + 0.5 * wsq
            shifted = lead + 1.0
            half_again = 1.5 * wsq
            stretch = jnp.maximum(1.0, shifted)
            for step in range(NEWTON):
                square = stretch * stretch
                cube = square * stretch
                stretch = jnp.maximum(1.0, stretch * (shifted * square + half_again) / (cube + wsq))
            inside = excess <= 0.0
            shrink = 1.0 / stretch
            proj = (jnp.where(inside, lead, lead - (stretch - 1.0)),) + tuple(
                jnp.where(inside, target[c], target[c] * shrink) for c in (1, 2, 3)
            )
            flux = []
            for c in range(4):
                nm = mults[c] + RATE * (grads[c] - proj[c])
                nm_out[c, 0, x] = nm
                flux.append(nm - RATE * proj[c])
            flow_y = jnp.where(first_row, 0.0, pltpu.roll(flux[2], 1, 0)) - jnp.where(last_row, 0.0, flux[2])
            flow_z = jnp.where(first_col, 0.0, pltpu.roll(flux[3], 1, 1)) - jnp.where(last_col, 0.0, flux[3])
            rest = PROX * p - (flow_y + flow_z)
            rest = rest + jnp.where(t_glob == 0, sd[x], 0.0) - jnp.where(last_t, fd[x], 0.0)
            has_prev = jnp.logical_and(t > 0, t < steps_t - 1)
            ft_prev = lax.cond(has_prev, lambda: ft_store[jnp.maximum(t - 1, 0), x], lambda: jnp.zeros_like(p))
            div_t = ft_prev - jnp.where(last_t, 0.0, flux[0])
            ft_store[t, x] = flux[0]

            @pl.when(t == steps_t - 1)
            def _():
                send_t[x] = flux[0]

                @pl.when(has_later_t)
                def _():
                    behind_t_copy(x).start()
            if x < rows_x - 1:
                fx_cur = flux[1]
            else:
                fx_cur = jnp.where(has_later_x, flux[1], 0.0)
                send_x[t] = flux[1]

                @pl.when(has_later_x)
                def _():
                    behind_x_copy(t).start()
            value = rest - div_t + fx_cur
            if x - 1 in fx_done:
                value = value - fx_done[x - 1]
            pay_out[t, x] = value
            if x + 1 in fx_done:
                pay_out[t, x + 1] = pay_out[t, x + 1] - flux[1]
            fx_done[x] = flux[1]

    @pl.when(s == steps_t - 1)
    def _():
        rows_in([rows_x - 1] + list(range(rows_x - 1)))

    @pl.when(s < steps_t - 1)
    def _():
        rows_in(list(range(rows_x)))

    @pl.when(s == steps_t - 1)
    def _():
        for x in range(rows_x):
            pay_out[steps_t - 1, x] = pay_out[steps_t - 1, x] - ft_store[steps_t - 2, x]

        @pl.when(has_earlier_t)
        def _():
            ahead_t_copy().wait_send()
            for x in range(rows_x):
                behind_t_copy(x).wait_recv()
                pay_out[0, x] = pay_out[0, x] - behind_t[x]

        @pl.when(has_earlier_x)
        def _():
            for r in range(steps_t):
                ahead_x_copy(r).wait_send()
                behind_x_copy(r).wait_recv()
                pay_out[r, 0] = pay_out[r, 0] - behind_x[r]

        @pl.when(has_later_x)
        def _():
            for r in range(steps_t):
                behind_x_copy(r).wait_send()

        @pl.when(has_later_t)
        def _():
            for x in range(rows_x):
                behind_t_copy(x).wait_send()


def cells(potential, multiplier, start_density, final_density, n_tm, n_sp):
    steps_t, rows_x, width_y, width_z = potential.shape
    idx = jnp.stack([lax.axis_index("tm"), lax.axis_index("space")]).astype(jnp.int32)
    slab = (1, rows_x, width_y, width_z)
    plane = (rows_x, width_y, width_z)
    f32 = jnp.float32
    grid_spec = pltpu.PrefetchScalarGridSpec(
        num_scalar_prefetch=1,
        grid=(steps_t,),
        in_specs=[
            pl.BlockSpec(slab, lambda i, s: (visit(i, steps_t), 0, 0, 0)),
            pl.BlockSpec(slab, lambda i, s: (jnp.minimum(visit(i, steps_t) + 1, steps_t - 1), 0, 0, 0)),
            pl.BlockSpec(memory_space=pl.ANY),
            pl.BlockSpec((4, 1, rows_x, width_y, width_z), lambda i, s: (0, visit(i, steps_t), 0, 0, 0)),
            pl.BlockSpec(plane, lambda t, s: (0, 0, 0)),
            pl.BlockSpec(plane, lambda t, s: (0, 0, 0)),
        ],
        out_specs=[
            pl.BlockSpec((4, 1, rows_x, width_y, width_z), lambda i, s: (0, visit(i, steps_t), 0, 0, 0)),
            pl.BlockSpec(potential.shape, lambda t, s: (0, 0, 0, 0)),
        ],
        scratch_shapes=[
            pltpu.VMEM((steps_t,) + plane, f32),
            pltpu.VMEM(plane, f32),
            pltpu.VMEM((steps_t, width_y, width_z), f32),
            pltpu.VMEM((steps_t, width_y, width_z), f32),
            pltpu.VMEM(plane, f32),
            pltpu.VMEM(plane, f32),
            pltpu.VMEM((steps_t, width_y, width_z), f32),
            pltpu.SemaphoreType.DMA((2,)),
            pltpu.SemaphoreType.DMA((2, steps_t)),
            pltpu.SemaphoreType.DMA((2, rows_x)),
            pltpu.SemaphoreType.DMA((2, steps_t)),
        ],
    )
    cells_n = potential.size
    return pl.pallas_call(
        functools.partial(cell_kernel, n_tm, n_sp),
        grid_spec=grid_spec,
        out_shape=[
            jax.ShapeDtypeStruct(multiplier.shape, f32),
            jax.ShapeDtypeStruct(potential.shape, f32),
        ],
        compiler_params=pltpu.CompilerParams(
            dimension_semantics=("arbitrary",), collective_id=0, has_side_effects=True
        ),
        cost_estimate=pl.CostEstimate(
            flops=cells_n * 200, transcendentals=cells_n * 11, bytes_accessed=cells_n * 4 * 12
        ),
    )(idx, potential, potential, potential, multiplier, start_density, final_density)

def body(potential, multiplier, start_density, final_density):
    high = lax.Precision.HIGH
    steps_t, rows_x, width_y, width_z = potential.shape
    n_tm = lax.axis_size("tm")
    n_sp = lax.axis_size("space")
    total_t = steps_t * n_tm
    total_x = rows_x * n_sp
    block_y = width_y // (n_tm * n_sp)
    time_at = lax.axis_index("tm") * steps_t + jnp.arange(steps_t)
    row_at = lax.axis_index("space") * rows_x + jnp.arange(rows_x)
    next_multiplier, partial = cells(
        potential, multiplier, start_density, final_density, n_tm, n_sp
    )
    cos_y = cosine_table(width_y)
    cos_z = cosine_table(width_z)
    payload = jnp.einsum("txyi,ki->txyk", partial, cos_z, precision=high)
    payload = jnp.einsum("txiz,ki->ktxz", payload, cos_y, precision=high)
    both = ("tm", "space")
    middle = lax.all_to_all(payload, both, split_axis=0, concat_axis=0, tiled=True)
    next_multiplier = jnp.where(next_multiplier == next_multiplier, next_multiplier, 0.0)
    middle, next_multiplier = lax.optimization_barrier((middle, next_multiplier))
    middle = middle.reshape(n_tm, n_sp, block_y, steps_t, rows_x, width_z)
    cos_t = cosine_table(total_t).reshape(total_t, n_tm, steps_t)
    cos_x = cosine_table(total_x).reshape(total_x, n_sp, rows_x)
    hat = jnp.einsum("kat,abytxz->kbxyz", cos_t, middle, precision=high)
    hat = jnp.einsum("jbx,kbxyz->kjyz", cos_x, hat, precision=high)
    freq_y = (
        (lax.axis_index("tm") * n_sp + lax.axis_index("space")) * block_y + jnp.arange(block_y)
    ).astype(jnp.float32)
    eig_t = eigen_at(total_t, jnp.arange(total_t, dtype=jnp.float32))
    eig_x = eigen_at(total_x, jnp.arange(total_x, dtype=jnp.float32))
    eig_y = eigen_at(width_y, freq_y)
    eig_z = eigen_at(width_z, jnp.arange(width_z, dtype=jnp.float32))
    denom = eig_t[:, None, None, None] + eig_x[None, :, None, None]
    denom = denom + eig_y[None, None, :, None] + eig_z[None, None, None, :]
    hat = hat / (RATE * denom + PROX)
    hat = jnp.einsum("atk,kjyz->atjyz", cos_t.reshape(n_tm, steps_t, total_t), hat, precision=high)
    solved = jnp.einsum("bxj,atjyz->abytxz", cos_x.reshape(n_sp, rows_x, total_x), hat, precision=high)
    solved = solved.reshape(n_tm * n_sp * block_y, steps_t, rows_x, width_z)
    local = lax.all_to_all(solved, both, split_axis=0, concat_axis=0, tiled=True)
    local = jnp.einsum("ik,ktxz->txiz", cos_y, local, precision=high)
    next_potential = jnp.einsum("ik,txyk->txyi", cos_z, local, precision=high)
    return (next_potential, next_multiplier)


def solution(mesh):
    in_specs = (
        P("tm", "space", None, None),
        P(None, "tm", "space", None, None),
        P("space", None, None),
        P("space", None, None),
    )
    out_specs = (P("tm", "space", None, None), P(None, "tm", "space", None, None))
    return jax.shard_map(body, mesh=mesh, in_specs=in_specs, out_specs=out_specs, check_vma=False)
```

```python
import functools

import jax
import jax.numpy as jnp
from jax import lax
from jax.sharding import PartitionSpec as P
from jax.experimental import pallas as pl
from jax.experimental.pallas import tpu as pltpu

NEWTON = 10


RATE = 4.0
PROX = 0.01


def from_behind(block, axis, distance):
    devices = range(lax.axis_size(axis))
    route = [(i - distance, i) for i in devices if i - distance in devices]
    return lax.ppermute(block, axis, route)


def cosine_table(length):
    freq = jnp.arange(length, dtype=jnp.float32)[:, None]
    place = jnp.arange(length, dtype=jnp.float32)[None, :]
    weight = jnp.where(freq == 0.0, jnp.sqrt(jnp.float32(0.5)), jnp.float32(1.0))
    return (
        jnp.sqrt(jnp.float32(2.0) / length)
        * weight
        * jnp.cos(jnp.pi * freq * (place + 0.5) / length)
    )


def eigen_at(length, freq):
    return 4.0 * jnp.square(jnp.sin(jnp.pi * freq / (2.0 * length)))


def adjoint(face, axis):
    size = face.shape[axis]
    inner = lax.slice_in_dim(face, 0, size - 1, axis=axis)
    edge = jnp.zeros_like(lax.slice_in_dim(face, 0, 1, axis=axis))
    return jnp.concatenate([edge, inner], axis=axis) - jnp.concatenate([inner, edge], axis=axis)


def local_diff(field, axis):
    size = field.shape[axis]
    upper = lax.slice_in_dim(field, 1, size, axis=axis)
    lower = lax.slice_in_dim(field, 0, size - 1, axis=axis)
    edge = jnp.zeros_like(lax.slice_in_dim(field, 0, 1, axis=axis))
    return jnp.concatenate([upper - lower, edge], axis=axis)


def project(target):
    lead = target[0]
    side = target[1:]
    wsq = jnp.sum(side * side, axis=0)
    excess = lead + 0.5 * wsq
    stretch = jnp.maximum(1.0, lead + 1.0)
    shifted = lead + 1.0
    half_again = 1.5 * wsq
    for step in range(NEWTON):
        square = stretch * stretch
        cube = square * stretch
        stretch = jnp.maximum(1.0, stretch * (shifted * square + half_again) / (cube + wsq))
    inside = excess <= 0.0
    new_lead = jnp.where(inside, lead, lead - (stretch - 1.0))
    shrink = 1.0 / stretch
    new_side = jnp.where(inside[None], side, side * shrink[None])
    return jnp.concatenate([new_lead[None], new_side], axis=0)


def visit(step, steps_t):
    return jnp.where(step < 1, step, jnp.where(step == 1, steps_t - 1, step - 1))


def cell_kernel(n_tm, n_sp, idx_ref, pc, pn, p_any, m, sd, fd, nm_out, pay_out,
                ft_store, ahead_t, ahead_x, send_x, send_t, behind_t, behind_x,
                at_sems, ax_sems, bt_sems, bx_sems):
    s = pl.program_id(0)
    steps_t = pl.num_programs(0)
    t = visit(s, steps_t)
    rows_x, width_y, width_z = pc.shape[1], pc.shape[2], pc.shape[3]
    tm = lax.axis_index("tm")
    sp = lax.axis_index("space")
    t_glob = tm * steps_t + t
    last_t = t_glob == n_tm * steps_t - 1
    has_later_t = tm < n_tm - 1
    has_earlier_t = tm > 0
    has_later_x = sp < n_sp - 1
    has_earlier_x = sp > 0
    mesh_id = pl.DeviceIdType.MESH

    def ahead_t_copy():
        return pltpu.make_async_remote_copy(
            p_any.at[0], ahead_t, at_sems.at[0], at_sems.at[1],
            device_id=(tm - 1, sp), device_id_type=mesh_id)

    def ahead_x_copy(row):
        return pltpu.make_async_remote_copy(
            p_any.at[row, 0], ahead_x.at[row], ax_sems.at[0, row], ax_sems.at[1, row],
            device_id=(tm, sp - 1), device_id_type=mesh_id)

    def behind_t_copy(x):
        return pltpu.make_async_remote_copy(
            send_t.at[x], behind_t.at[x], bt_sems.at[0, x], bt_sems.at[1, x],
            device_id=(tm + 1, sp), device_id_type=mesh_id)

    def behind_x_copy(row):
        return pltpu.make_async_remote_copy(
            send_x.at[row], behind_x.at[row], bx_sems.at[0, row], bx_sems.at[1, row],
            device_id=(tm, sp + 1), device_id_type=mesh_id)

    @pl.when(s == 0)
    def _():
        barrier = pltpu.get_barrier_semaphore()
        for cond, dev in ((has_earlier_t, (tm - 1, sp)), (has_later_t, (tm + 1, sp)),
                          (has_earlier_x, (tm, sp - 1)), (has_later_x, (tm, sp + 1))):
            @pl.when(cond)
            def _():
                pl.semaphore_signal(barrier, 1, device_id=dev, device_id_type=mesh_id)
        peers = (has_earlier_t.astype(jnp.int32) + has_later_t.astype(jnp.int32)
                 + has_earlier_x.astype(jnp.int32) + has_later_x.astype(jnp.int32))
        pl.semaphore_wait(barrier, peers)

        @pl.when(has_earlier_t)
        def _():
            ahead_t_copy().start()

        @pl.when(has_earlier_x)
        def _():
            rows = ahead_x.shape[0]
            for row in [0, rows - 1] + list(range(1, rows - 1)):
                ahead_x_copy(row).start()

    row = lax.broadcasted_iota(jnp.int32, (width_y, width_z), 0)
    col = lax.broadcasted_iota(jnp.int32, (width_y, width_z), 1)
    first_row = row == 0
    last_row = row == width_y - 1
    last_col = col == width_z - 1
    first_col = col == 0
    def rows_in(order):
        fx_done = {}
        for x in order:
            p = pc[0, x]
            if x == order[0]:
                @pl.when(jnp.logical_and(t == steps_t - 1, has_later_t))
                def _():
                    ahead_t_copy().wait_recv()
            nxt = lax.cond(t == steps_t - 1, lambda: ahead_t[x], lambda: pn[0, x])
            grad_t = jnp.where(last_t, 0.0, nxt - p)
            if x < rows_x - 1:
                grad_x = pc[0, x + 1] - p
            else:
                @pl.when(has_later_x)
                def _():
                    ahead_x_copy(t).wait_recv()
                grad_x = lax.cond(has_later_x, lambda: ahead_x[t] - p, lambda: jnp.zeros_like(p))
            grad_y = jnp.where(last_row, 0.0, pltpu.roll(p, width_y - 1, 0) - p)
            grad_z = jnp.where(last_col, 0.0, pltpu.roll(p, width_z - 1, 1) - p)
            grads = (grad_t, grad_x, grad_y, grad_z)
            mults = tuple(m[c, 0, x] for c in range(4))
            target = tuple(g + mu * (1.0 / RATE) for g, mu in zip(grads, mults))
            lead = target[0]
            wsq = target[1] * target[1] + target[2] * target[2] + target[3] * target[3]
            excess = lead + 0.5 * wsq
            shifted = lead + 1.0
            half_again = 1.5 * wsq
            stretch = jnp.maximum(1.0, shifted)
            for step in range(NEWTON):
                square = stretch * stretch
                cube = square * stretch
                stretch = jnp.maximum(1.0, stretch * (shifted * square + half_again) / (cube + wsq))
            inside = excess <= 0.0
            shrink = 1.0 / stretch
            proj = (jnp.where(inside, lead, lead - (stretch - 1.0)),) + tuple(
                jnp.where(inside, target[c], target[c] * shrink) for c in (1, 2, 3)
            )
            flux = []
            for c in range(4):
                nm = mults[c] + RATE * (grads[c] - proj[c])
                nm_out[c, 0, x] = nm
                flux.append(nm - RATE * proj[c])
            flow_y = jnp.where(first_row, 0.0, pltpu.roll(flux[2], 1, 0)) - jnp.where(last_row, 0.0, flux[2])
            flow_z = jnp.where(first_col, 0.0, pltpu.roll(flux[3], 1, 1)) - jnp.where(last_col, 0.0, flux[3])
            rest = PROX * p - (flow_y + flow_z)
            rest = rest + jnp.where(t_glob == 0, sd[x], 0.0) - jnp.where(last_t, fd[x], 0.0)
            has_prev = jnp.logical_and(t > 0, t < steps_t - 1)
            ft_prev = lax.cond(has_prev, lambda: ft_store[jnp.maximum(t - 1, 0), x], lambda: jnp.zeros_like(p))
            div_t = ft_prev - jnp.where(last_t, 0.0, flux[0])
            ft_store[t, x] = flux[0]

            @pl.when(t == steps_t - 1)
            def _():
                send_t[x] = flux[0]

                @pl.when(has_later_t)
                def _():
                    behind_t_copy(x).start()
            if x < rows_x - 1:
                fx_cur = flux[1]
            else:
                fx_cur = jnp.where(has_later_x, flux[1], 0.0)
                send_x[t] = flux[1]

                @pl.when(has_later_x)
                def _():
                    behind_x_copy(t).start()
            value = rest - div_t + fx_cur
            if x - 1 in fx_done:
                value = value - fx_done[x - 1]
            pay_out[t, x] = value
            if x + 1 in fx_done:
                pay_out[t, x + 1] = pay_out[t, x + 1] - flux[1]
            fx_done[x] = flux[1]

    @pl.when(s == steps_t - 1)
    def _():
        rows_in([rows_x - 1] + list(range(rows_x - 1)))

    @pl.when(s < steps_t - 1)
    def _():
        rows_in(list(range(rows_x)))

    @pl.when(s == steps_t - 1)
    def _():
        for x in range(rows_x):
            pay_out[steps_t - 1, x] = pay_out[steps_t - 1, x] - ft_store[steps_t - 2, x]

        @pl.when(has_earlier_t)
        def _():
            ahead_t_copy().wait_send()
            for x in range(rows_x):
                behind_t_copy(x).wait_recv()
                pay_out[0, x] = pay_out[0, x] - behind_t[x]

        @pl.when(has_earlier_x)
        def _():
            for r in range(steps_t):
                ahead_x_copy(r).wait_send()
                behind_x_copy(r).wait_recv()
                pay_out[r, 0] = pay_out[r, 0] - behind_x[r]

        @pl.when(has_later_x)
        def _():
            for r in range(steps_t):
                behind_x_copy(r).wait_send()

        @pl.when(has_later_t)
        def _():
            for x in range(rows_x):
                behind_t_copy(x).wait_send()


def cells(potential, multiplier, start_density, final_density, n_tm, n_sp):
    steps_t, rows_x, width_y, width_z = potential.shape
    idx = jnp.stack([lax.axis_index("tm"), lax.axis_index("space")]).astype(jnp.int32)
    slab = (1, rows_x, width_y, width_z)
    plane = (rows_x, width_y, width_z)
    f32 = jnp.float32
    grid_spec = pltpu.PrefetchScalarGridSpec(
        num_scalar_prefetch=1,
        grid=(steps_t,),
        in_specs=[
            pl.BlockSpec(slab, lambda i, s: (visit(i, steps_t), 0, 0, 0)),
            pl.BlockSpec(slab, lambda i, s: (jnp.minimum(visit(i, steps_t) + 1, steps_t - 1), 0, 0, 0)),
            pl.BlockSpec(memory_space=pl.ANY),
            pl.BlockSpec((4, 1, rows_x, width_y, width_z), lambda i, s: (0, visit(i, steps_t), 0, 0, 0)),
            pl.BlockSpec(plane, lambda t, s: (0, 0, 0)),
            pl.BlockSpec(plane, lambda t, s: (0, 0, 0)),
        ],
        out_specs=[
            pl.BlockSpec((4, 1, rows_x, width_y, width_z), lambda i, s: (0, visit(i, steps_t), 0, 0, 0)),
            pl.BlockSpec(potential.shape, lambda t, s: (0, 0, 0, 0)),
        ],
        scratch_shapes=[
            pltpu.VMEM((steps_t,) + plane, f32),
            pltpu.VMEM(plane, f32),
            pltpu.VMEM((steps_t, width_y, width_z), f32),
            pltpu.VMEM((steps_t, width_y, width_z), f32),
            pltpu.VMEM(plane, f32),
            pltpu.VMEM(plane, f32),
            pltpu.VMEM((steps_t, width_y, width_z), f32),
            pltpu.SemaphoreType.DMA((2,)),
            pltpu.SemaphoreType.DMA((2, steps_t)),
            pltpu.SemaphoreType.DMA((2, rows_x)),
            pltpu.SemaphoreType.DMA((2, steps_t)),
        ],
    )
    cells_n = potential.size
    return pl.pallas_call(
        functools.partial(cell_kernel, n_tm, n_sp),
        grid_spec=grid_spec,
        out_shape=[
            jax.ShapeDtypeStruct(multiplier.shape, f32),
            jax.ShapeDtypeStruct(potential.shape, f32),
        ],
        compiler_params=pltpu.CompilerParams(
            dimension_semantics=("arbitrary",), collective_id=0, has_side_effects=True
        ),
        cost_estimate=pl.CostEstimate(
            flops=cells_n * 200, transcendentals=cells_n * 11, bytes_accessed=cells_n * 4 * 12
        ),
    )(idx, potential, potential, potential, multiplier, start_density, final_density)

def body(potential, multiplier, start_density, final_density):
    high = lax.Precision.HIGH
    steps_t, rows_x, width_y, width_z = potential.shape
    n_tm = lax.axis_size("tm")
    n_sp = lax.axis_size("space")
    total_t = steps_t * n_tm
    total_x = rows_x * n_sp
    block_y = width_y // (n_tm * n_sp)
    time_at = lax.axis_index("tm") * steps_t + jnp.arange(steps_t)
    row_at = lax.axis_index("space") * rows_x + jnp.arange(rows_x)
    next_multiplier, partial = cells(
        potential, multiplier, start_density, final_density, n_tm, n_sp
    )
    cos_y = cosine_table(width_y)
    cos_z = cosine_table(width_z)
    payload = jnp.einsum("txyi,ki->txyk", partial, cos_z, precision=high)
    payload = jnp.einsum("txiz,ki->ktxz", payload, cos_y, precision=high)
    both = ("tm", "space")
    middle = lax.all_to_all(payload, both, split_axis=0, concat_axis=0, tiled=True)
    next_multiplier = jnp.where(next_multiplier == next_multiplier, next_multiplier, 0.0)
    middle, next_multiplier = lax.optimization_barrier((middle, next_multiplier))
    middle = middle.reshape(n_tm, n_sp, block_y, steps_t, rows_x, width_z)
    cos_t = cosine_table(total_t).reshape(total_t, n_tm, steps_t)
    cos_x = cosine_table(total_x).reshape(total_x, n_sp, rows_x)
    hat = jnp.einsum("kat,abytxz->kbxyz", cos_t, middle, precision=high)
    hat = jnp.einsum("jbx,kbxyz->kjyz", cos_x, hat, precision=high)
    freq_y = (
        (lax.axis_index("tm") * n_sp + lax.axis_index("space")) * block_y + jnp.arange(block_y)
    ).astype(jnp.float32)
    eig_t = eigen_at(total_t, jnp.arange(total_t, dtype=jnp.float32))
    eig_x = eigen_at(total_x, jnp.arange(total_x, dtype=jnp.float32))
    eig_y = eigen_at(width_y, freq_y)
    eig_z = eigen_at(width_z, jnp.arange(width_z, dtype=jnp.float32))
    denom = eig_t[:, None, None, None] + eig_x[None, :, None, None]
    denom = denom + eig_y[None, None, :, None] + eig_z[None, None, None, :]
    hat = hat / (RATE * denom + PROX)
    hat = jnp.einsum("atk,kjyz->atjyz", cos_t.reshape(n_tm, steps_t, total_t), hat, precision=high)
    solved = jnp.einsum("bxj,atjyz->abytxz", cos_x.reshape(n_sp, rows_x, total_x), hat, precision=high)
    solved = solved.reshape(n_tm * n_sp * block_y, steps_t, rows_x, width_z)
    local = lax.all_to_all(solved, both, split_axis=0, concat_axis=0, tiled=True)
    local = jnp.einsum("ik,ktxz->txiz", cos_y, local, precision=high)
    next_potential = jnp.einsum("ik,txyk->txyi", cos_z, local, precision=high)
    return (next_potential, next_multiplier)


def solution(mesh):
    in_specs = (
        P("tm", "space", None, None),
        P(None, "tm", "space", None, None),
        P("space", None, None),
        P("space", None, None),
    )
    out_specs = (P("tm", "space", None, None), P(None, "tm", "space", None, None))
    return jax.shard_map(body, mesh=mesh, in_specs=in_specs, out_specs=out_specs, check_vma=False)
```

```python
import functools

import jax
import jax.numpy as jnp
from jax import lax
from jax.sharding import PartitionSpec as P
from jax.experimental import pallas as pl
from jax.experimental.pallas import tpu as pltpu

NEWTON = 10


RATE = 4.0
PROX = 0.01


def from_behind(block, axis, distance):
    devices = range(lax.axis_size(axis))
    route = [(i - distance, i) for i in devices if i - distance in devices]
    return lax.ppermute(block, axis, route)


def cosine_table(length):
    freq = jnp.arange(length, dtype=jnp.float32)[:, None]
    place = jnp.arange(length, dtype=jnp.float32)[None, :]
    weight = jnp.where(freq == 0.0, jnp.sqrt(jnp.float32(0.5)), jnp.float32(1.0))
    return (
        jnp.sqrt(jnp.float32(2.0) / length)
        * weight
        * jnp.cos(jnp.pi * freq * (place + 0.5) / length)
    )


def eigen_at(length, freq):
    return 4.0 * jnp.square(jnp.sin(jnp.pi * freq / (2.0 * length)))


def adjoint(face, axis):
    size = face.shape[axis]
    inner = lax.slice_in_dim(face, 0, size - 1, axis=axis)
    edge = jnp.zeros_like(lax.slice_in_dim(face, 0, 1, axis=axis))
    return jnp.concatenate([edge, inner], axis=axis) - jnp.concatenate([inner, edge], axis=axis)


def local_diff(field, axis):
    size = field.shape[axis]
    upper = lax.slice_in_dim(field, 1, size, axis=axis)
    lower = lax.slice_in_dim(field, 0, size - 1, axis=axis)
    edge = jnp.zeros_like(lax.slice_in_dim(field, 0, 1, axis=axis))
    return jnp.concatenate([upper - lower, edge], axis=axis)


def project(target):
    lead = target[0]
    side = target[1:]
    wsq = jnp.sum(side * side, axis=0)
    excess = lead + 0.5 * wsq
    stretch = jnp.maximum(1.0, lead + 1.0)
    shifted = lead + 1.0
    half_again = 1.5 * wsq
    for step in range(NEWTON):
        square = stretch * stretch
        cube = square * stretch
        stretch = jnp.maximum(1.0, stretch * (shifted * square + half_again) / (cube + wsq))
    inside = excess <= 0.0
    new_lead = jnp.where(inside, lead, lead - (stretch - 1.0))
    shrink = 1.0 / stretch
    new_side = jnp.where(inside[None], side, side * shrink[None])
    return jnp.concatenate([new_lead[None], new_side], axis=0)


def visit(step, steps_t):
    return jnp.where(step == 0, steps_t - 1, step - 1)


def cell_kernel(n_tm, n_sp, idx_ref, pc, pn, p_any, m, sd, fd, nm_out, pay_out,
                ft_store, ahead_t, ahead_x, send_x, send_t, behind_t, behind_x,
                at_sems, ax_sems, bt_sems, bx_sems):
    s = pl.program_id(0)
    steps_t = pl.num_programs(0)
    t = visit(s, steps_t)
    rows_x, width_y, width_z = pc.shape[1], pc.shape[2], pc.shape[3]
    tm = lax.axis_index("tm")
    sp = lax.axis_index("space")
    t_glob = tm * steps_t + t
    last_t = t_glob == n_tm * steps_t - 1
    has_later_t = tm < n_tm - 1
    has_earlier_t = tm > 0
    has_later_x = sp < n_sp - 1
    has_earlier_x = sp > 0
    mesh_id = pl.DeviceIdType.MESH

    def ahead_t_copy():
        return pltpu.make_async_remote_copy(
            p_any.at[0], ahead_t, at_sems.at[0], at_sems.at[1],
            device_id=(tm - 1, sp), device_id_type=mesh_id)

    def ahead_x_copy(row):
        return pltpu.make_async_remote_copy(
            p_any.at[row, 0], ahead_x.at[row], ax_sems.at[0, row], ax_sems.at[1, row],
            device_id=(tm, sp - 1), device_id_type=mesh_id)

    def behind_t_copy(x):
        return pltpu.make_async_remote_copy(
            send_t.at[x], behind_t.at[x], bt_sems.at[0, x], bt_sems.at[1, x],
            device_id=(tm + 1, sp), device_id_type=mesh_id)

    def behind_x_copy(row):
        return pltpu.make_async_remote_copy(
            send_x.at[row], behind_x.at[row], bx_sems.at[0, row], bx_sems.at[1, row],
            device_id=(tm, sp + 1), device_id_type=mesh_id)

    @pl.when(s == 0)
    def _():
        barrier = pltpu.get_barrier_semaphore()
        for cond, dev in ((has_earlier_t, (tm - 1, sp)), (has_later_t, (tm + 1, sp)),
                          (has_earlier_x, (tm, sp - 1)), (has_later_x, (tm, sp + 1))):
            @pl.when(cond)
            def _():
                pl.semaphore_signal(barrier, 1, device_id=dev, device_id_type=mesh_id)
        peers = (has_earlier_t.astype(jnp.int32) + has_later_t.astype(jnp.int32)
                 + has_earlier_x.astype(jnp.int32) + has_later_x.astype(jnp.int32))
        pl.semaphore_wait(barrier, peers)

        @pl.when(has_earlier_t)
        def _():
            ahead_t_copy().start()

        @pl.when(has_earlier_x)
        def _():
            rows = ahead_x.shape[0]
            for row in [rows - 1] + list(range(rows - 1)):
                ahead_x_copy(row).start()

    row = lax.broadcasted_iota(jnp.int32, (width_y, width_z), 0)
    col = lax.broadcasted_iota(jnp.int32, (width_y, width_z), 1)
    first_row = row == 0
    last_row = row == width_y - 1
    last_col = col == width_z - 1
    first_col = col == 0
    def rows_in(order):
        fx_done = {}
        for x in order:
            p = pc[0, x]
            if x == order[0]:
                @pl.when(jnp.logical_and(t == steps_t - 1, has_later_t))
                def _():
                    ahead_t_copy().wait_recv()
            nxt = lax.cond(t == steps_t - 1, lambda: ahead_t[x], lambda: pn[0, x])
            grad_t = jnp.where(last_t, 0.0, nxt - p)
            if x < rows_x - 1:
                grad_x = pc[0, x + 1] - p
            else:
                @pl.when(has_later_x)
                def _():
                    ahead_x_copy(t).wait_recv()
                grad_x = lax.cond(has_later_x, lambda: ahead_x[t] - p, lambda: jnp.zeros_like(p))
            grad_y = jnp.where(last_row, 0.0, pltpu.roll(p, width_y - 1, 0) - p)
            grad_z = jnp.where(last_col, 0.0, pltpu.roll(p, width_z - 1, 1) - p)
            grads = (grad_t, grad_x, grad_y, grad_z)
            mults = tuple(m[c, 0, x] for c in range(4))
            target = tuple(g + mu * (1.0 / RATE) for g, mu in zip(grads, mults))
            lead = target[0]
            wsq = target[1] * target[1] + target[2] * target[2] + target[3] * target[3]
            excess = lead + 0.5 * wsq
            shifted = lead + 1.0
            half_again = 1.5 * wsq
            stretch = jnp.maximum(1.0, shifted)
            for step in range(NEWTON):
                square = stretch * stretch
                cube = square * stretch
                stretch = jnp.maximum(1.0, stretch * (shifted * square + half_again) / (cube + wsq))
            inside = excess <= 0.0
            shrink = 1.0 / stretch
            proj = (jnp.where(inside, lead, lead - (stretch - 1.0)),) + tuple(
                jnp.where(inside, target[c], target[c] * shrink) for c in (1, 2, 3)
            )
            flux = []
            for c in range(4):
                nm = mults[c] + RATE * (grads[c] - proj[c])
                nm_out[c, 0, x] = nm
                flux.append(nm - RATE * proj[c])
            flow_y = jnp.where(first_row, 0.0, pltpu.roll(flux[2], 1, 0)) - jnp.where(last_row, 0.0, flux[2])
            flow_z = jnp.where(first_col, 0.0, pltpu.roll(flux[3], 1, 1)) - jnp.where(last_col, 0.0, flux[3])
            rest = PROX * p - (flow_y + flow_z)
            rest = rest + jnp.where(t_glob == 0, sd[x], 0.0) - jnp.where(last_t, fd[x], 0.0)
            has_prev = jnp.logical_and(t > 0, t < steps_t - 1)
            ft_prev = lax.cond(has_prev, lambda: ft_store[jnp.maximum(t - 1, 0), x], lambda: jnp.zeros_like(p))
            div_t = ft_prev - jnp.where(last_t, 0.0, flux[0])
            ft_store[t, x] = flux[0]

            @pl.when(t == steps_t - 1)
            def _():
                send_t[x] = flux[0]

                @pl.when(has_later_t)
                def _():
                    behind_t_copy(x).start()
            if x < rows_x - 1:
                fx_cur = flux[1]
            else:
                fx_cur = jnp.where(has_later_x, flux[1], 0.0)
                send_x[t] = flux[1]

                @pl.when(has_later_x)
                def _():
                    behind_x_copy(t).start()
            value = rest - div_t + fx_cur
            if x - 1 in fx_done:
                value = value - fx_done[x - 1]
            pay_out[t, x] = value
            if x + 1 in fx_done:
                pay_out[t, x + 1] = pay_out[t, x + 1] - flux[1]
            fx_done[x] = flux[1]

    @pl.when(s == steps_t - 1)
    def _():
        rows_in([rows_x - 1] + list(range(rows_x - 1)))

    @pl.when(s < steps_t - 1)
    def _():
        rows_in(list(range(rows_x)))

    @pl.when(s == steps_t - 1)
    def _():
        for x in range(rows_x):
            pay_out[steps_t - 1, x] = pay_out[steps_t - 1, x] - ft_store[steps_t - 2, x]

        @pl.when(has_earlier_t)
        def _():
            ahead_t_copy().wait_send()
            for x in range(rows_x):
                behind_t_copy(x).wait_recv()
                pay_out[0, x] = pay_out[0, x] - behind_t[x]

        @pl.when(has_earlier_x)
        def _():
            for r in range(steps_t):
                ahead_x_copy(r).wait_send()
                behind_x_copy(r).wait_recv()
                pay_out[r, 0] = pay_out[r, 0] - behind_x[r]

        @pl.when(has_later_x)
        def _():
            for r in range(steps_t):
                behind_x_copy(r).wait_send()

        @pl.when(has_later_t)
        def _():
            for x in range(rows_x):
                behind_t_copy(x).wait_send()


def cells(potential, multiplier, start_density, final_density, n_tm, n_sp):
    steps_t, rows_x, width_y, width_z = potential.shape
    idx = jnp.stack([lax.axis_index("tm"), lax.axis_index("space")]).astype(jnp.int32)
    slab = (1, rows_x, width_y, width_z)
    plane = (rows_x, width_y, width_z)
    f32 = jnp.float32
    grid_spec = pltpu.PrefetchScalarGridSpec(
        num_scalar_prefetch=1,
        grid=(steps_t,),
        in_specs=[
            pl.BlockSpec(slab, lambda i, s: (visit(i, steps_t), 0, 0, 0)),
            pl.BlockSpec(slab, lambda i, s: (jnp.minimum(visit(i, steps_t) + 1, steps_t - 1), 0, 0, 0)),
            pl.BlockSpec(memory_space=pl.ANY),
            pl.BlockSpec((4, 1, rows_x, width_y, width_z), lambda i, s: (0, visit(i, steps_t), 0, 0, 0)),
            pl.BlockSpec(plane, lambda t, s: (0, 0, 0)),
            pl.BlockSpec(plane, lambda t, s: (0, 0, 0)),
        ],
        out_specs=[
            pl.BlockSpec((4, 1, rows_x, width_y, width_z), lambda i, s: (0, visit(i, steps_t), 0, 0, 0)),
            pl.BlockSpec(potential.shape, lambda t, s: (0, 0, 0, 0)),
        ],
        scratch_shapes=[
            pltpu.VMEM((steps_t,) + plane, f32),
            pltpu.VMEM(plane, f32),
            pltpu.VMEM((steps_t, width_y, width_z), f32),
            pltpu.VMEM((steps_t, width_y, width_z), f32),
            pltpu.VMEM(plane, f32),
            pltpu.VMEM(plane, f32),
            pltpu.VMEM((steps_t, width_y, width_z), f32),
            pltpu.SemaphoreType.DMA((2,)),
            pltpu.SemaphoreType.DMA((2, steps_t)),
            pltpu.SemaphoreType.DMA((2, rows_x)),
            pltpu.SemaphoreType.DMA((2, steps_t)),
        ],
    )
    cells_n = potential.size
    return pl.pallas_call(
        functools.partial(cell_kernel, n_tm, n_sp),
        grid_spec=grid_spec,
        out_shape=[
            jax.ShapeDtypeStruct(multiplier.shape, f32),
            jax.ShapeDtypeStruct(potential.shape, f32),
        ],
        compiler_params=pltpu.CompilerParams(
            dimension_semantics=("arbitrary",), collective_id=0, has_side_effects=True
        ),
        cost_estimate=pl.CostEstimate(
            flops=cells_n * 200, transcendentals=cells_n * 11, bytes_accessed=cells_n * 4 * 12
        ),
    )(idx, potential, potential, potential, multiplier, start_density, final_density)

def body(potential, multiplier, start_density, final_density):
    high = lax.Precision.HIGH
    steps_t, rows_x, width_y, width_z = potential.shape
    n_tm = lax.axis_size("tm")
    n_sp = lax.axis_size("space")
    total_t = steps_t * n_tm
    total_x = rows_x * n_sp
    block_y = width_y // (n_tm * n_sp)
    time_at = lax.axis_index("tm") * steps_t + jnp.arange(steps_t)
    row_at = lax.axis_index("space") * rows_x + jnp.arange(rows_x)
    next_multiplier, partial = cells(
        potential, multiplier, start_density, final_density, n_tm, n_sp
    )
    cos_y = cosine_table(width_y)
    cos_z = cosine_table(width_z)
    payload = jnp.einsum("txyi,ki->txyk", partial, cos_z, precision=high)
    payload = jnp.einsum("txiz,ki->ktxz", payload, cos_y, precision=high)
    both = ("tm", "space")
    middle = lax.all_to_all(payload, both, split_axis=0, concat_axis=0, tiled=True)
    next_multiplier = jnp.where(next_multiplier == next_multiplier, next_multiplier, 0.0)
    middle, next_multiplier = lax.optimization_barrier((middle, next_multiplier))
    middle = middle.reshape(n_tm, n_sp, block_y, steps_t, rows_x, width_z)
    cos_t = cosine_table(total_t).reshape(total_t, n_tm, steps_t)
    cos_x = cosine_table(total_x).reshape(total_x, n_sp, rows_x)
    hat = jnp.einsum("kat,abytxz->kbxyz", cos_t, middle, precision=high)
    hat = jnp.einsum("jbx,kbxyz->kjyz", cos_x, hat, precision=high)
    freq_y = (
        (lax.axis_index("tm") * n_sp + lax.axis_index("space")) * block_y + jnp.arange(block_y)
    ).astype(jnp.float32)
    eig_t = eigen_at(total_t, jnp.arange(total_t, dtype=jnp.float32))
    eig_x = eigen_at(total_x, jnp.arange(total_x, dtype=jnp.float32))
    eig_y = eigen_at(width_y, freq_y)
    eig_z = eigen_at(width_z, jnp.arange(width_z, dtype=jnp.float32))
    denom = eig_t[:, None, None, None] + eig_x[None, :, None, None]
    denom = denom + eig_y[None, None, :, None] + eig_z[None, None, None, :]
    hat = hat / (RATE * denom + PROX)
    hat = jnp.einsum("atk,kjyz->atjyz", cos_t.reshape(n_tm, steps_t, total_t), hat, precision=high)
    solved = jnp.einsum("bxj,atjyz->abytxz", cos_x.reshape(n_sp, rows_x, total_x), hat, precision=high)
    solved = solved.reshape(n_tm * n_sp * block_y, steps_t, rows_x, width_z)
    local = lax.all_to_all(solved, both, split_axis=0, concat_axis=0, tiled=True)
    local = jnp.einsum("ik,ktxz->txiz", cos_y, local, precision=high)
    next_potential = jnp.einsum("ik,txyk->txyi", cos_z, local, precision=high)
    return (next_potential, next_multiplier)


def solution(mesh):
    in_specs = (
        P("tm", "space", None, None),
        P(None, "tm", "space", None, None),
        P("space", None, None),
        P("space", None, None),
    )
    out_specs = (P("tm", "space", None, None), P(None, "tm", "space", None, None))
    return jax.shard_map(body, mesh=mesh, in_specs=in_specs, out_specs=out_specs, check_vma=False)
```

```python
import functools

import jax
import jax.numpy as jnp
from jax import lax
from jax.sharding import PartitionSpec as P
from jax.experimental import pallas as pl
from jax.experimental.pallas import tpu as pltpu

NEWTON = 10


RATE = 4.0
PROX = 0.01


def from_behind(block, axis, distance):
    devices = range(lax.axis_size(axis))
    route = [(i - distance, i) for i in devices if i - distance in devices]
    return lax.ppermute(block, axis, route)


def cosine_table(length):
    freq = jnp.arange(length, dtype=jnp.float32)[:, None]
    place = jnp.arange(length, dtype=jnp.float32)[None, :]
    weight = jnp.where(freq == 0.0, jnp.sqrt(jnp.float32(0.5)), jnp.float32(1.0))
    return (
        jnp.sqrt(jnp.float32(2.0) / length)
        * weight
        * jnp.cos(jnp.pi * freq * (place + 0.5) / length)
    )


def eigen_at(length, freq):
    return 4.0 * jnp.square(jnp.sin(jnp.pi * freq / (2.0 * length)))


def adjoint(face, axis):
    size = face.shape[axis]
    inner = lax.slice_in_dim(face, 0, size - 1, axis=axis)
    edge = jnp.zeros_like(lax.slice_in_dim(face, 0, 1, axis=axis))
    return jnp.concatenate([edge, inner], axis=axis) - jnp.concatenate([inner, edge], axis=axis)


def local_diff(field, axis):
    size = field.shape[axis]
    upper = lax.slice_in_dim(field, 1, size, axis=axis)
    lower = lax.slice_in_dim(field, 0, size - 1, axis=axis)
    edge = jnp.zeros_like(lax.slice_in_dim(field, 0, 1, axis=axis))
    return jnp.concatenate([upper - lower, edge], axis=axis)


def project(target):
    lead = target[0]
    side = target[1:]
    wsq = jnp.sum(side * side, axis=0)
    excess = lead + 0.5 * wsq
    stretch = jnp.maximum(1.0, lead + 1.0)
    shifted = lead + 1.0
    half_again = 1.5 * wsq
    for step in range(NEWTON):
        square = stretch * stretch
        cube = square * stretch
        stretch = jnp.maximum(1.0, stretch * (shifted * square + half_again) / (cube + wsq))
    inside = excess <= 0.0
    new_lead = jnp.where(inside, lead, lead - (stretch - 1.0))
    shrink = 1.0 / stretch
    new_side = jnp.where(inside[None], side, side * shrink[None])
    return jnp.concatenate([new_lead[None], new_side], axis=0)


def visit(step, steps_t):
    return jnp.where(step < 1, step, jnp.where(step == 1, steps_t - 1, step - 1))


def cell_kernel(n_tm, n_sp, idx_ref, pc, pn, p_any, m, sd, fd, nm_out, pay_out,
                ft_store, ahead_t, ahead_x, send_x, send_t, behind_t, behind_x,
                at_sems, ax_sems, bt_sems, bx_sems):
    s = pl.program_id(0)
    steps_t = pl.num_programs(0)
    t = visit(s, steps_t)
    rows_x, width_y, width_z = pc.shape[1], pc.shape[2], pc.shape[3]
    tm = lax.axis_index("tm")
    sp = lax.axis_index("space")
    t_glob = tm * steps_t + t
    last_t = t_glob == n_tm * steps_t - 1
    has_later_t = tm < n_tm - 1
    has_earlier_t = tm > 0
    has_later_x = sp < n_sp - 1
    has_earlier_x = sp > 0
    mesh_id = pl.DeviceIdType.MESH

    def ahead_t_copy():
        return pltpu.make_async_remote_copy(
            p_any.at[0], ahead_t, at_sems.at[0], at_sems.at[1],
            device_id=(tm - 1, sp), device_id_type=mesh_id)

    def ahead_x_copy(row):
        return pltpu.make_async_remote_copy(
            p_any.at[row, 0], ahead_x.at[row], ax_sems.at[0, row], ax_sems.at[1, row],
            device_id=(tm, sp - 1), device_id_type=mesh_id)

    def behind_t_copy(x):
        return pltpu.make_async_remote_copy(
            send_t.at[x], behind_t.at[x], bt_sems.at[0, x], bt_sems.at[1, x],
            device_id=(tm + 1, sp), device_id_type=mesh_id)

    def behind_x_copy(row):
        return pltpu.make_async_remote_copy(
            send_x.at[row], behind_x.at[row], bx_sems.at[0, row], bx_sems.at[1, row],
            device_id=(tm, sp + 1), device_id_type=mesh_id)

    @pl.when(s == 0)
    def _():
        barrier = pltpu.get_barrier_semaphore()
        for cond, dev in ((has_earlier_t, (tm - 1, sp)), (has_later_t, (tm + 1, sp)),
                          (has_earlier_x, (tm, sp - 1)), (has_later_x, (tm, sp + 1))):
            @pl.when(cond)
            def _():
                pl.semaphore_signal(barrier, 1, device_id=dev, device_id_type=mesh_id)
        peers = (has_earlier_t.astype(jnp.int32) + has_later_t.astype(jnp.int32)
                 + has_earlier_x.astype(jnp.int32) + has_later_x.astype(jnp.int32))
        pl.semaphore_wait(barrier, peers)

        @pl.when(has_earlier_t)
        def _():
            ahead_t_copy().start()

        @pl.when(has_earlier_x)
        def _():
            rows = ahead_x.shape[0]
            for row in [0, rows - 1] + list(range(1, rows - 1)):
                ahead_x_copy(row).start()

    row = lax.broadcasted_iota(jnp.int32, (width_y, width_z), 0)
    col = lax.broadcasted_iota(jnp.int32, (width_y, width_z), 1)
    first_row = row == 0
    last_row = row == width_y - 1
    last_col = col == width_z - 1
    first_col = col == 0
    def rows_in(order):
        fx_done = {}
        for x in order:
            p = pc[0, x]
            if x == order[0]:
                @pl.when(jnp.logical_and(t == steps_t - 1, has_later_t))
                def _():
                    ahead_t_copy().wait_recv()
            nxt = lax.cond(t == steps_t - 1, lambda: ahead_t[x], lambda: pn[0, x])
            grad_t = jnp.where(last_t, 0.0, nxt - p)
            if x < rows_x - 1:
                grad_x = pc[0, x + 1] - p
            else:
                @pl.when(has_later_x)
                def _():
                    ahead_x_copy(t).wait_recv()
                grad_x = lax.cond(has_later_x, lambda: ahead_x[t] - p, lambda: jnp.zeros_like(p))
            grad_y = jnp.where(last_row, 0.0, pltpu.roll(p, width_y - 1, 0) - p)
            grad_z = jnp.where(last_col, 0.0, pltpu.roll(p, width_z - 1, 1) - p)
            grads = (grad_t, grad_x, grad_y, grad_z)
            mults = tuple(m[c, 0, x] for c in range(4))
            target = tuple(g + mu * (1.0 / RATE) for g, mu in zip(grads, mults))
            lead = target[0]
            wsq = target[1] * target[1] + target[2] * target[2] + target[3] * target[3]
            excess = lead + 0.5 * wsq
            shifted = lead + 1.0
            half_again = 1.5 * wsq
            stretch = jnp.maximum(1.0, shifted)
            for step in range(NEWTON):
                square = stretch * stretch
                cube = square * stretch
                stretch = jnp.maximum(1.0, stretch * (shifted * square + half_again) / (cube + wsq))
            inside = excess <= 0.0
            shrink = 1.0 / stretch
            proj = (jnp.where(inside, lead, lead - (stretch - 1.0)),) + tuple(
                jnp.where(inside, target[c], target[c] * shrink) for c in (1, 2, 3)
            )
            flux = []
            for c in range(4):
                nm = mults[c] + RATE * (grads[c] - proj[c])
                nm_out[c, 0, x] = nm
                flux.append(nm - RATE * proj[c])
            flow_y = jnp.where(first_row, 0.0, pltpu.roll(flux[2], 1, 0)) - jnp.where(last_row, 0.0, flux[2])
            flow_z = jnp.where(first_col, 0.0, pltpu.roll(flux[3], 1, 1)) - jnp.where(last_col, 0.0, flux[3])
            rest = PROX * p - (flow_y + flow_z)
            rest = rest + jnp.where(t_glob == 0, sd[x], 0.0) - jnp.where(last_t, fd[x], 0.0)
            has_prev = jnp.logical_and(t > 0, t < steps_t - 1)
            ft_prev = jnp.where(has_prev, ft_store[jnp.maximum(t - 1, 0), x], 0.0)
            div_t = ft_prev - jnp.where(last_t, 0.0, flux[0])
            ft_store[t, x] = flux[0]

            @pl.when(t == steps_t - 1)
            def _():
                send_t[x] = flux[0]

                @pl.when(has_later_t)
                def _():
                    behind_t_copy(x).start()
            if x < rows_x - 1:
                fx_cur = flux[1]
            else:
                fx_cur = jnp.where(has_later_x, flux[1], 0.0)
                send_x[t] = flux[1]

                @pl.when(has_later_x)
                def _():
                    behind_x_copy(t).start()
            value = rest - div_t + fx_cur
            if x - 1 in fx_done:
                value = value - fx_done[x - 1]
            pay_out[t, x] = value
            if x + 1 in fx_done:
                pay_out[t, x + 1] = pay_out[t, x + 1] - flux[1]
            fx_done[x] = flux[1]

    @pl.when(s == steps_t - 1)
    def _():
        rows_in([rows_x - 1] + list(range(rows_x - 1)))

    @pl.when(s < steps_t - 1)
    def _():
        rows_in(list(range(rows_x)))

    @pl.when(s == steps_t - 1)
    def _():
        for x in range(rows_x):
            pay_out[steps_t - 1, x] = pay_out[steps_t - 1, x] - ft_store[steps_t - 2, x]

        @pl.when(has_earlier_t)
        def _():
            ahead_t_copy().wait_send()
            for x in range(rows_x):
                behind_t_copy(x).wait_recv()
                pay_out[0, x] = pay_out[0, x] - behind_t[x]

        @pl.when(has_earlier_x)
        def _():
            for r in range(steps_t):
                ahead_x_copy(r).wait_send()
                behind_x_copy(r).wait_recv()
                pay_out[r, 0] = pay_out[r, 0] - behind_x[r]

        @pl.when(has_later_x)
        def _():
            for r in range(steps_t):
                behind_x_copy(r).wait_send()

        @pl.when(has_later_t)
        def _():
            for x in range(rows_x):
                behind_t_copy(x).wait_send()


def cells(potential, multiplier, start_density, final_density, n_tm, n_sp):
    steps_t, rows_x, width_y, width_z = potential.shape
    idx = jnp.stack([lax.axis_index("tm"), lax.axis_index("space")]).astype(jnp.int32)
    slab = (1, rows_x, width_y, width_z)
    plane = (rows_x, width_y, width_z)
    f32 = jnp.float32
    grid_spec = pltpu.PrefetchScalarGridSpec(
        num_scalar_prefetch=1,
        grid=(steps_t,),
        in_specs=[
            pl.BlockSpec(slab, lambda i, s: (visit(i, steps_t), 0, 0, 0)),
            pl.BlockSpec(slab, lambda i, s: (jnp.minimum(visit(i, steps_t) + 1, steps_t - 1), 0, 0, 0)),
            pl.BlockSpec(memory_space=pl.ANY),
            pl.BlockSpec((4, 1, rows_x, width_y, width_z), lambda i, s: (0, visit(i, steps_t), 0, 0, 0)),
            pl.BlockSpec(plane, lambda t, s: (0, 0, 0)),
            pl.BlockSpec(plane, lambda t, s: (0, 0, 0)),
        ],
        out_specs=[
            pl.BlockSpec((4, 1, rows_x, width_y, width_z), lambda i, s: (0, visit(i, steps_t), 0, 0, 0)),
            pl.BlockSpec(potential.shape, lambda t, s: (0, 0, 0, 0)),
        ],
        scratch_shapes=[
            pltpu.VMEM((steps_t,) + plane, f32),
            pltpu.VMEM(plane, f32),
            pltpu.VMEM((steps_t, width_y, width_z), f32),
            pltpu.VMEM((steps_t, width_y, width_z), f32),
            pltpu.VMEM(plane, f32),
            pltpu.VMEM(plane, f32),
            pltpu.VMEM((steps_t, width_y, width_z), f32),
            pltpu.SemaphoreType.DMA((2,)),
            pltpu.SemaphoreType.DMA((2, steps_t)),
            pltpu.SemaphoreType.DMA((2, rows_x)),
            pltpu.SemaphoreType.DMA((2, steps_t)),
        ],
    )
    cells_n = potential.size
    return pl.pallas_call(
        functools.partial(cell_kernel, n_tm, n_sp),
        grid_spec=grid_spec,
        out_shape=[
            jax.ShapeDtypeStruct(multiplier.shape, f32),
            jax.ShapeDtypeStruct(potential.shape, f32),
        ],
        compiler_params=pltpu.CompilerParams(
            dimension_semantics=("arbitrary",), collective_id=0, has_side_effects=True
        ),
        cost_estimate=pl.CostEstimate(
            flops=cells_n * 200, transcendentals=cells_n * 11, bytes_accessed=cells_n * 4 * 12
        ),
    )(idx, potential, potential, potential, multiplier, start_density, final_density)

def body(potential, multiplier, start_density, final_density):
    high = lax.Precision.HIGH
    steps_t, rows_x, width_y, width_z = potential.shape
    n_tm = lax.axis_size("tm")
    n_sp = lax.axis_size("space")
    total_t = steps_t * n_tm
    total_x = rows_x * n_sp
    block_y = width_y // (n_tm * n_sp)
    time_at = lax.axis_index("tm") * steps_t + jnp.arange(steps_t)
    row_at = lax.axis_index("space") * rows_x + jnp.arange(rows_x)
    next_multiplier, partial = cells(
        potential, multiplier, start_density, final_density, n_tm, n_sp
    )
    cos_y = cosine_table(width_y)
    cos_z = cosine_table(width_z)
    payload = jnp.einsum("txyi,ki->txyk", partial, cos_z, precision=high)
    payload = jnp.einsum("txiz,ki->ktxz", payload, cos_y, precision=high)
    both = ("tm", "space")
    middle = lax.all_to_all(payload, both, split_axis=0, concat_axis=0, tiled=True)
    next_multiplier = jnp.where(next_multiplier == next_multiplier, next_multiplier, 0.0)
    middle, next_multiplier = lax.optimization_barrier((middle, next_multiplier))
    middle = middle.reshape(n_tm, n_sp, block_y, steps_t, rows_x, width_z)
    cos_t = cosine_table(total_t).reshape(total_t, n_tm, steps_t)
    cos_x = cosine_table(total_x).reshape(total_x, n_sp, rows_x)
    hat = jnp.einsum("kat,abytxz->kbxyz", cos_t, middle, precision=high)
    hat = jnp.einsum("jbx,kbxyz->kjyz", cos_x, hat, precision=high)
    freq_y = (
        (lax.axis_index("tm") * n_sp + lax.axis_index("space")) * block_y + jnp.arange(block_y)
    ).astype(jnp.float32)
    eig_t = eigen_at(total_t, jnp.arange(total_t, dtype=jnp.float32))
    eig_x = eigen_at(total_x, jnp.arange(total_x, dtype=jnp.float32))
    eig_y = eigen_at(width_y, freq_y)
    eig_z = eigen_at(width_z, jnp.arange(width_z, dtype=jnp.float32))
    denom = eig_t[:, None, None, None] + eig_x[None, :, None, None]
    denom = denom + eig_y[None, None, :, None] + eig_z[None, None, None, :]
    hat = hat / (RATE * denom + PROX)
    hat = jnp.einsum("atk,kjyz->atjyz", cos_t.reshape(n_tm, steps_t, total_t), hat, precision=high)
    solved = jnp.einsum("bxj,atjyz->abytxz", cos_x.reshape(n_sp, rows_x, total_x), hat, precision=high)
    solved = solved.reshape(n_tm * n_sp * block_y, steps_t, rows_x, width_z)
    local = lax.all_to_all(solved, both, split_axis=0, concat_axis=0, tiled=True)
    local = jnp.einsum("ik,ktxz->txiz", cos_y, local, precision=high)
    next_potential = jnp.einsum("ik,txyk->txyi", cos_z, local, precision=high)
    return (next_potential, next_multiplier)


def solution(mesh):
    in_specs = (
        P("tm", "space", None, None),
        P(None, "tm", "space", None, None),
        P("space", None, None),
        P("space", None, None),
    )
    out_specs = (P("tm", "space", None, None), P(None, "tm", "space", None, None))
    return jax.shard_map(body, mesh=mesh, in_specs=in_specs, out_specs=out_specs, check_vma=False)
```

```python
import functools

import jax
import jax.numpy as jnp
from jax import lax
from jax.sharding import PartitionSpec as P
from jax.experimental import pallas as pl
from jax.experimental.pallas import tpu as pltpu

NEWTON = 10


RATE = 4.0
PROX = 0.01


def from_behind(block, axis, distance):
    devices = range(lax.axis_size(axis))
    route = [(i - distance, i) for i in devices if i - distance in devices]
    return lax.ppermute(block, axis, route)


def cosine_table(length):
    freq = jnp.arange(length, dtype=jnp.float32)[:, None]
    place = jnp.arange(length, dtype=jnp.float32)[None, :]
    weight = jnp.where(freq == 0.0, jnp.sqrt(jnp.float32(0.5)), jnp.float32(1.0))
    return (
        jnp.sqrt(jnp.float32(2.0) / length)
        * weight
        * jnp.cos(jnp.pi * freq * (place + 0.5) / length)
    )


def eigen_at(length, freq):
    return 4.0 * jnp.square(jnp.sin(jnp.pi * freq / (2.0 * length)))


def adjoint(face, axis):
    size = face.shape[axis]
    inner = lax.slice_in_dim(face, 0, size - 1, axis=axis)
    edge = jnp.zeros_like(lax.slice_in_dim(face, 0, 1, axis=axis))
    return jnp.concatenate([edge, inner], axis=axis) - jnp.concatenate([inner, edge], axis=axis)


def local_diff(field, axis):
    size = field.shape[axis]
    upper = lax.slice_in_dim(field, 1, size, axis=axis)
    lower = lax.slice_in_dim(field, 0, size - 1, axis=axis)
    edge = jnp.zeros_like(lax.slice_in_dim(field, 0, 1, axis=axis))
    return jnp.concatenate([upper - lower, edge], axis=axis)


def project(target):
    lead = target[0]
    side = target[1:]
    wsq = jnp.sum(side * side, axis=0)
    excess = lead + 0.5 * wsq
    stretch = jnp.maximum(1.0, lead + 1.0)
    shifted = lead + 1.0
    half_again = 1.5 * wsq
    for step in range(NEWTON):
        square = stretch * stretch
        cube = square * stretch
        stretch = jnp.maximum(1.0, stretch * (shifted * square + half_again) / (cube + wsq))
    inside = excess <= 0.0
    new_lead = jnp.where(inside, lead, lead - (stretch - 1.0))
    shrink = 1.0 / stretch
    new_side = jnp.where(inside[None], side, side * shrink[None])
    return jnp.concatenate([new_lead[None], new_side], axis=0)


def visit(step, steps_t):
    return jnp.where(step < 1, step, jnp.where(step == 1, steps_t - 1, step - 1))


def cell_kernel(n_tm, n_sp, idx_ref, pc, pn, p_any, m, sd, fd, nm_out, pay_out,
                ft_store, ahead_t, ahead_x, send_x, send_t, behind_t, behind_x,
                at_sems, ax_sems, bt_sems, bx_sems):
    s = pl.program_id(0)
    steps_t = pl.num_programs(0)
    t = visit(s, steps_t)
    rows_x, width_y, width_z = pc.shape[1], pc.shape[2], pc.shape[3]
    tm = lax.axis_index("tm")
    sp = lax.axis_index("space")
    t_glob = tm * steps_t + t
    last_t = t_glob == n_tm * steps_t - 1
    has_later_t = tm < n_tm - 1
    has_earlier_t = tm > 0
    has_later_x = sp < n_sp - 1
    has_earlier_x = sp > 0
    mesh_id = pl.DeviceIdType.MESH

    def ahead_t_copy():
        return pltpu.make_async_remote_copy(
            p_any.at[0], ahead_t, at_sems.at[0], at_sems.at[1],
            device_id=(tm - 1, sp), device_id_type=mesh_id)

    def ahead_x_copy(row):
        return pltpu.make_async_remote_copy(
            p_any.at[row, 0], ahead_x.at[row], ax_sems.at[0, row], ax_sems.at[1, row],
            device_id=(tm, sp - 1), device_id_type=mesh_id)

    def behind_t_copy(x):
        return pltpu.make_async_remote_copy(
            send_t.at[x], behind_t.at[x], bt_sems.at[0, x], bt_sems.at[1, x],
            device_id=(tm + 1, sp), device_id_type=mesh_id)

    def behind_x_copy(row):
        return pltpu.make_async_remote_copy(
            send_x.at[row], behind_x.at[row], bx_sems.at[0, row], bx_sems.at[1, row],
            device_id=(tm, sp + 1), device_id_type=mesh_id)

    @pl.when(s == 0)
    def _():
        barrier = pltpu.get_barrier_semaphore()
        for cond, dev in ((has_earlier_t, (tm - 1, sp)), (has_later_t, (tm + 1, sp)),
                          (has_earlier_x, (tm, sp - 1)), (has_later_x, (tm, sp + 1))):
            @pl.when(cond)
            def _():
                pl.semaphore_signal(barrier, 1, device_id=dev, device_id_type=mesh_id)
        peers = (has_earlier_t.astype(jnp.int32) + has_later_t.astype(jnp.int32)
                 + has_earlier_x.astype(jnp.int32) + has_later_x.astype(jnp.int32))
        pl.semaphore_wait(barrier, peers)

        @pl.when(has_earlier_t)
        def _():
            ahead_t_copy().start()

        @pl.when(has_earlier_x)
        def _():
            rows = ahead_x.shape[0]
            for row in [0, rows - 1] + list(range(1, rows - 1)):
                ahead_x_copy(row).start()

    row = lax.broadcasted_iota(jnp.int32, (width_y, width_z), 0)
    col = lax.broadcasted_iota(jnp.int32, (width_y, width_z), 1)
    first_row = row == 0
    last_row = row == width_y - 1
    last_col = col == width_z - 1
    first_col = col == 0
    def rows_in(order):
        fx_done = {}
        for x in order:
            p = pc[0, x]
            if x == order[0]:
                @pl.when(jnp.logical_and(t == steps_t - 1, has_later_t))
                def _():
                    ahead_t_copy().wait_recv()
            nxt = lax.cond(t == steps_t - 1, lambda: ahead_t[x], lambda: pn[0, x])
            grad_t = jnp.where(last_t, 0.0, nxt - p)
            if x < rows_x - 1:
                grad_x = pc[0, x + 1] - p
            else:
                @pl.when(has_later_x)
                def _():
                    ahead_x_copy(t).wait_recv()
                grad_x = lax.cond(has_later_x, lambda: ahead_x[t] - p, lambda: jnp.zeros_like(p))
            grad_y = jnp.where(last_row, 0.0, pltpu.roll(p, width_y - 1, 0) - p)
            grad_z = jnp.where(last_col, 0.0, pltpu.roll(p, width_z - 1, 1) - p)
            grads = (grad_t, grad_x, grad_y, grad_z)
            mults = tuple(m[c, 0, x] for c in range(4))
            target = tuple(g + mu * (1.0 / RATE) for g, mu in zip(grads, mults))
            lead = target[0]
            wsq = target[1] * target[1] + target[2] * target[2] + target[3] * target[3]
            excess = lead + 0.5 * wsq
            shifted = lead + 1.0
            half_again = 1.5 * wsq
            stretch = jnp.maximum(1.0, shifted)
            for step in range(NEWTON):
                square = stretch * stretch
                cube = square * stretch
                stretch = jnp.maximum(1.0, stretch * (shifted * square + half_again) / (cube + wsq))
            inside = excess <= 0.0
            shrink = 1.0 / stretch
            proj = (jnp.where(inside, lead, lead - (stretch - 1.0)),) + tuple(
                jnp.where(inside, target[c], target[c] * shrink) for c in (1, 2, 3)
            )
            flux = []
            for c in range(4):
                nm = mults[c] + RATE * (grads[c] - proj[c])
                nm_out[c, 0, x] = nm
                flux.append(nm - RATE * proj[c])
            if x == rows_x - 1:
                send_x[t] = flux[1]

                @pl.when(has_later_x)
                def _():
                    behind_x_copy(t).start()

            @pl.when(t == steps_t - 1)
            def _():
                send_t[x] = flux[0]

                @pl.when(has_later_t)
                def _():
                    behind_t_copy(x).start()
            flow_y = jnp.where(first_row, 0.0, pltpu.roll(flux[2], 1, 0)) - jnp.where(last_row, 0.0, flux[2])
            flow_z = jnp.where(first_col, 0.0, pltpu.roll(flux[3], 1, 1)) - jnp.where(last_col, 0.0, flux[3])
            rest = PROX * p - (flow_y + flow_z)
            rest = rest + jnp.where(t_glob == 0, sd[x], 0.0) - jnp.where(last_t, fd[x], 0.0)
            has_prev = jnp.logical_and(t > 0, t < steps_t - 1)
            ft_prev = lax.cond(has_prev, lambda: ft_store[jnp.maximum(t - 1, 0), x], lambda: jnp.zeros_like(p))
            div_t = ft_prev - jnp.where(last_t, 0.0, flux[0])
            ft_store[t, x] = flux[0]
            if x < rows_x - 1:
                fx_cur = flux[1]
            else:
                fx_cur = jnp.where(has_later_x, flux[1], 0.0)
            value = rest - div_t + fx_cur
            if x - 1 in fx_done:
                value = value - fx_done[x - 1]
            pay_out[t, x] = value
            if x + 1 in fx_done:
                pay_out[t, x + 1] = pay_out[t, x + 1] - flux[1]
            fx_done[x] = flux[1]

    @pl.when(s == steps_t - 1)
    def _():
        rows_in([rows_x - 1] + list(range(rows_x - 1)))

    @pl.when(s < steps_t - 1)
    def _():
        rows_in(list(range(rows_x)))

    @pl.when(s == steps_t - 1)
    def _():
        for x in range(rows_x):
            pay_out[steps_t - 1, x] = pay_out[steps_t - 1, x] - ft_store[steps_t - 2, x]

        @pl.when(has_earlier_t)
        def _():
            ahead_t_copy().wait_send()
            for x in range(rows_x):
                behind_t_copy(x).wait_recv()
                pay_out[0, x] = pay_out[0, x] - behind_t[x]

        @pl.when(has_earlier_x)
        def _():
            for r in range(steps_t):
                ahead_x_copy(r).wait_send()
                behind_x_copy(r).wait_recv()
                pay_out[r, 0] = pay_out[r, 0] - behind_x[r]

        @pl.when(has_later_x)
        def _():
            for r in range(steps_t):
                behind_x_copy(r).wait_send()

        @pl.when(has_later_t)
        def _():
            for x in range(rows_x):
                behind_t_copy(x).wait_send()


def cells(potential, multiplier, start_density, final_density, n_tm, n_sp):
    steps_t, rows_x, width_y, width_z = potential.shape
    idx = jnp.stack([lax.axis_index("tm"), lax.axis_index("space")]).astype(jnp.int32)
    slab = (1, rows_x, width_y, width_z)
    plane = (rows_x, width_y, width_z)
    f32 = jnp.float32
    grid_spec = pltpu.PrefetchScalarGridSpec(
        num_scalar_prefetch=1,
        grid=(steps_t,),
        in_specs=[
            pl.BlockSpec(slab, lambda i, s: (visit(i, steps_t), 0, 0, 0)),
            pl.BlockSpec(slab, lambda i, s: (jnp.minimum(visit(i, steps_t) + 1, steps_t - 1), 0, 0, 0)),
            pl.BlockSpec(memory_space=pl.ANY),
            pl.BlockSpec((4, 1, rows_x, width_y, width_z), lambda i, s: (0, visit(i, steps_t), 0, 0, 0)),
            pl.BlockSpec(plane, lambda t, s: (0, 0, 0)),
            pl.BlockSpec(plane, lambda t, s: (0, 0, 0)),
        ],
        out_specs=[
            pl.BlockSpec((4, 1, rows_x, width_y, width_z), lambda i, s: (0, visit(i, steps_t), 0, 0, 0)),
            pl.BlockSpec(potential.shape, lambda t, s: (0, 0, 0, 0)),
        ],
        scratch_shapes=[
            pltpu.VMEM((steps_t,) + plane, f32),
            pltpu.VMEM(plane, f32),
            pltpu.VMEM((steps_t, width_y, width_z), f32),
            pltpu.VMEM((steps_t, width_y, width_z), f32),
            pltpu.VMEM(plane, f32),
            pltpu.VMEM(plane, f32),
            pltpu.VMEM((steps_t, width_y, width_z), f32),
            pltpu.SemaphoreType.DMA((2,)),
            pltpu.SemaphoreType.DMA((2, steps_t)),
            pltpu.SemaphoreType.DMA((2, rows_x)),
            pltpu.SemaphoreType.DMA((2, steps_t)),
        ],
    )
    cells_n = potential.size
    return pl.pallas_call(
        functools.partial(cell_kernel, n_tm, n_sp),
        grid_spec=grid_spec,
        out_shape=[
            jax.ShapeDtypeStruct(multiplier.shape, f32),
            jax.ShapeDtypeStruct(potential.shape, f32),
        ],
        compiler_params=pltpu.CompilerParams(
            dimension_semantics=("arbitrary",), collective_id=0, has_side_effects=True
        ),
        cost_estimate=pl.CostEstimate(
            flops=cells_n * 200, transcendentals=cells_n * 11, bytes_accessed=cells_n * 4 * 12
        ),
    )(idx, potential, potential, potential, multiplier, start_density, final_density)

def body(potential, multiplier, start_density, final_density):
    high = lax.Precision.HIGH
    steps_t, rows_x, width_y, width_z = potential.shape
    n_tm = lax.axis_size("tm")
    n_sp = lax.axis_size("space")
    total_t = steps_t * n_tm
    total_x = rows_x * n_sp
    block_y = width_y // (n_tm * n_sp)
    time_at = lax.axis_index("tm") * steps_t + jnp.arange(steps_t)
    row_at = lax.axis_index("space") * rows_x + jnp.arange(rows_x)
    next_multiplier, partial = cells(
        potential, multiplier, start_density, final_density, n_tm, n_sp
    )
    cos_y = cosine_table(width_y)
    cos_z = cosine_table(width_z)
    payload = jnp.einsum("txyi,ki->txyk", partial, cos_z, precision=high)
    payload = jnp.einsum("txiz,ki->ktxz", payload, cos_y, precision=high)
    both = ("tm", "space")
    middle = lax.all_to_all(payload, both, split_axis=0, concat_axis=0, tiled=True)
    next_multiplier = jnp.where(next_multiplier == next_multiplier, next_multiplier, 0.0)
    middle, next_multiplier = lax.optimization_barrier((middle, next_multiplier))
    middle = middle.reshape(n_tm, n_sp, block_y, steps_t, rows_x, width_z)
    cos_t = cosine_table(total_t).reshape(total_t, n_tm, steps_t)
    cos_x = cosine_table(total_x).reshape(total_x, n_sp, rows_x)
    hat = jnp.einsum("kat,abytxz->kbxyz", cos_t, middle, precision=high)
    hat = jnp.einsum("jbx,kbxyz->kjyz", cos_x, hat, precision=high)
    freq_y = (
        (lax.axis_index("tm") * n_sp + lax.axis_index("space")) * block_y + jnp.arange(block_y)
    ).astype(jnp.float32)
    eig_t = eigen_at(total_t, jnp.arange(total_t, dtype=jnp.float32))
    eig_x = eigen_at(total_x, jnp.arange(total_x, dtype=jnp.float32))
    eig_y = eigen_at(width_y, freq_y)
    eig_z = eigen_at(width_z, jnp.arange(width_z, dtype=jnp.float32))
    denom = eig_t[:, None, None, None] + eig_x[None, :, None, None]
    denom = denom + eig_y[None, None, :, None] + eig_z[None, None, None, :]
    hat = hat / (RATE * denom + PROX)
    hat = jnp.einsum("atk,kjyz->atjyz", cos_t.reshape(n_tm, steps_t, total_t), hat, precision=high)
    solved = jnp.einsum("bxj,atjyz->abytxz", cos_x.reshape(n_sp, rows_x, total_x), hat, precision=high)
    solved = solved.reshape(n_tm * n_sp * block_y, steps_t, rows_x, width_z)
    local = lax.all_to_all(solved, both, split_axis=0, concat_axis=0, tiled=True)
    local = jnp.einsum("ik,ktxz->txiz", cos_y, local, precision=high)
    next_potential = jnp.einsum("ik,txyk->txyi", cos_z, local, precision=high)
    return (next_potential, next_multiplier)


def solution(mesh):
    in_specs = (
        P("tm", "space", None, None),
        P(None, "tm", "space", None, None),
        P("space", None, None),
        P("space", None, None),
    )
    out_specs = (P("tm", "space", None, None), P(None, "tm", "space", None, None))
    return jax.shard_map(body, mesh=mesh, in_specs=in_specs, out_specs=out_specs, check_vma=False)
```

```python
import functools

import jax
import jax.numpy as jnp
from jax import lax
from jax.sharding import PartitionSpec as P
from jax.experimental import pallas as pl
from jax.experimental.pallas import tpu as pltpu

NEWTON = 10


RATE = 4.0
PROX = 0.01


def from_behind(block, axis, distance):
    devices = range(lax.axis_size(axis))
    route = [(i - distance, i) for i in devices if i - distance in devices]
    return lax.ppermute(block, axis, route)


def cosine_table(length):
    freq = jnp.arange(length, dtype=jnp.float32)[:, None]
    place = jnp.arange(length, dtype=jnp.float32)[None, :]
    weight = jnp.where(freq == 0.0, jnp.sqrt(jnp.float32(0.5)), jnp.float32(1.0))
    return (
        jnp.sqrt(jnp.float32(2.0) / length)
        * weight
        * jnp.cos(jnp.pi * freq * (place + 0.5) / length)
    )


def eigen_at(length, freq):
    return 4.0 * jnp.square(jnp.sin(jnp.pi * freq / (2.0 * length)))


def adjoint(face, axis):
    size = face.shape[axis]
    inner = lax.slice_in_dim(face, 0, size - 1, axis=axis)
    edge = jnp.zeros_like(lax.slice_in_dim(face, 0, 1, axis=axis))
    return jnp.concatenate([edge, inner], axis=axis) - jnp.concatenate([inner, edge], axis=axis)


def local_diff(field, axis):
    size = field.shape[axis]
    upper = lax.slice_in_dim(field, 1, size, axis=axis)
    lower = lax.slice_in_dim(field, 0, size - 1, axis=axis)
    edge = jnp.zeros_like(lax.slice_in_dim(field, 0, 1, axis=axis))
    return jnp.concatenate([upper - lower, edge], axis=axis)


def project(target):
    lead = target[0]
    side = target[1:]
    wsq = jnp.sum(side * side, axis=0)
    excess = lead + 0.5 * wsq
    stretch = jnp.maximum(1.0, lead + 1.0)
    shifted = lead + 1.0
    half_again = 1.5 * wsq
    for step in range(NEWTON):
        square = stretch * stretch
        cube = square * stretch
        stretch = jnp.maximum(1.0, stretch * (shifted * square + half_again) / (cube + wsq))
    inside = excess <= 0.0
    new_lead = jnp.where(inside, lead, lead - (stretch - 1.0))
    shrink = 1.0 / stretch
    new_side = jnp.where(inside[None], side, side * shrink[None])
    return jnp.concatenate([new_lead[None], new_side], axis=0)


def visit(step, steps_t):
    return jnp.where(step < 1, step, jnp.where(step == 1, steps_t - 1, step - 1))


def cell_kernel(n_tm, n_sp, idx_ref, pc, pn, p_any, m, sd, fd, nm_out, pay_out,
                ft_store, ahead_t, ahead_x, send_x, send_t, behind_t, behind_x,
                at_sems, ax_sems, bt_sems, bx_sems):
    s = pl.program_id(0)
    steps_t = pl.num_programs(0)
    t = visit(s, steps_t)
    rows_x, width_y, width_z = pc.shape[1], pc.shape[2], pc.shape[3]
    tm = lax.axis_index("tm")
    sp = lax.axis_index("space")
    t_glob = tm * steps_t + t
    last_t = t_glob == n_tm * steps_t - 1
    has_later_t = tm < n_tm - 1
    has_earlier_t = tm > 0
    has_later_x = sp < n_sp - 1
    has_earlier_x = sp > 0
    mesh_id = pl.DeviceIdType.MESH

    def ahead_t_copy():
        return pltpu.make_async_remote_copy(
            p_any.at[0], ahead_t, at_sems.at[0], at_sems.at[1],
            device_id=(tm - 1, sp), device_id_type=mesh_id)

    def ahead_x_copy(row):
        return pltpu.make_async_remote_copy(
            p_any.at[row, 0], ahead_x.at[row], ax_sems.at[0, row], ax_sems.at[1, row],
            device_id=(tm, sp - 1), device_id_type=mesh_id)

    def behind_t_copy(x):
        return pltpu.make_async_remote_copy(
            send_t.at[x], behind_t.at[x], bt_sems.at[0, x], bt_sems.at[1, x],
            device_id=(tm + 1, sp), device_id_type=mesh_id)

    def behind_x_copy(row):
        return pltpu.make_async_remote_copy(
            send_x.at[row], behind_x.at[row], bx_sems.at[0, row], bx_sems.at[1, row],
            device_id=(tm, sp + 1), device_id_type=mesh_id)

    @pl.when(s == 0)
    def _():
        barrier = pltpu.get_barrier_semaphore()
        for cond, dev in ((has_earlier_t, (tm - 1, sp)), (has_later_t, (tm + 1, sp)),
                          (has_earlier_x, (tm, sp - 1)), (has_later_x, (tm, sp + 1))):
            @pl.when(cond)
            def _():
                pl.semaphore_signal(barrier, 1, device_id=dev, device_id_type=mesh_id)
        peers = (has_earlier_t.astype(jnp.int32) + has_later_t.astype(jnp.int32)
                 + has_earlier_x.astype(jnp.int32) + has_later_x.astype(jnp.int32))
        pl.semaphore_wait(barrier, peers)

        @pl.when(has_earlier_t)
        def _():
            ahead_t_copy().start()

        @pl.when(has_earlier_x)
        def _():
            rows = ahead_x.shape[0]
            for row in [0, rows - 1] + list(range(1, rows - 1)):
                ahead_x_copy(row).start()

    row = lax.broadcasted_iota(jnp.int32, (width_y, width_z), 0)
    col = lax.broadcasted_iota(jnp.int32, (width_y, width_z), 1)
    first_row = row == 0
    last_row = row == width_y - 1
    last_col = col == width_z - 1
    first_col = col == 0
    def rows_in(order):
        fx_done = {}
        for x in order:
            p = pc[0, x]
            if x == order[0]:
                @pl.when(jnp.logical_and(t == steps_t - 1, has_later_t))
                def _():
                    ahead_t_copy().wait_recv()
            nxt = lax.cond(t == steps_t - 1, lambda: ahead_t[x], lambda: pn[0, x])
            grad_t = jnp.where(last_t, 0.0, nxt - p)
            if x < rows_x - 1:
                grad_x = pc[0, x + 1] - p
            else:
                @pl.when(has_later_x)
                def _():
                    ahead_x_copy(t).wait_recv()
                grad_x = lax.cond(has_later_x, lambda: ahead_x[t] - p, lambda: jnp.zeros_like(p))
            grad_y = jnp.where(last_row, 0.0, pltpu.roll(p, width_y - 1, 0) - p)
            grad_z = jnp.where(last_col, 0.0, pltpu.roll(p, width_z - 1, 1) - p)
            grads = (grad_t, grad_x, grad_y, grad_z)
            mults = tuple(m[c, 0, x] for c in range(4))
            target = tuple(g + mu * (1.0 / RATE) for g, mu in zip(grads, mults))
            lead = target[0]
            wsq = target[1] * target[1] + target[2] * target[2] + target[3] * target[3]
            excess = lead + 0.5 * wsq
            shifted = lead + 1.0
            half_again = 1.5 * wsq
            stretch = jnp.maximum(1.0, shifted)
            for step in range(NEWTON):
                square = stretch * stretch
                cube = square * stretch
                stretch = jnp.maximum(1.0, stretch * (shifted * square + half_again) / (cube + wsq))
            inside = excess <= 0.0
            shrink = 1.0 / stretch
            proj = (jnp.where(inside, lead, lead - (stretch - 1.0)),) + tuple(
                jnp.where(inside, target[c], target[c] * shrink) for c in (1, 2, 3)
            )
            flux = []
            for c in range(4):
                nm = mults[c] + RATE * (grads[c] - proj[c])
                nm_out[c, 0, x] = nm
                flux.append(nm - RATE * proj[c])
            if x == rows_x - 1:
                send_x[t] = flux[1]

                @pl.when(has_later_x)
                def _():
                    behind_x_copy(t).start()

            @pl.when(t == steps_t - 1)
            def _():
                send_t[x] = flux[0]

                @pl.when(has_later_t)
                def _():
                    behind_t_copy(x).start()
            flow_y = jnp.where(first_row, 0.0, pltpu.roll(flux[2], 1, 0)) - jnp.where(last_row, 0.0, flux[2])
            flow_z = jnp.where(first_col, 0.0, pltpu.roll(flux[3], 1, 1)) - jnp.where(last_col, 0.0, flux[3])
            rest = PROX * p - (flow_y + flow_z)
            rest = rest + jnp.where(t_glob == 0, sd[x], 0.0) - jnp.where(last_t, fd[x], 0.0)
            has_prev = jnp.logical_and(t > 0, t < steps_t - 1)
            ft_prev = lax.cond(has_prev, lambda: ft_store[jnp.maximum(t - 1, 0), x], lambda: jnp.zeros_like(p))
            div_t = ft_prev - jnp.where(last_t, 0.0, flux[0])
            ft_store[t, x] = flux[0]
            if x < rows_x - 1:
                fx_cur = flux[1]
            else:
                fx_cur = jnp.where(has_later_x, flux[1], 0.0)
            value = rest - div_t + fx_cur
            if x - 1 in fx_done:
                value = value - fx_done[x - 1]
            pay_out[t, x] = value
            if x + 1 in fx_done:
                pay_out[t, x + 1] = pay_out[t, x + 1] - flux[1]
            fx_done[x] = flux[1]

    @pl.when(s == steps_t - 1)
    def _():
        rows_in([rows_x - 1] + list(range(rows_x - 1)))

    @pl.when(s < steps_t - 1)
    def _():
        rows_in(list(range(rows_x)))

    @pl.when(s == steps_t - 1)
    def _():
        for x in range(rows_x):
            pay_out[steps_t - 1, x] = pay_out[steps_t - 1, x] - ft_store[steps_t - 2, x]

        @pl.when(has_earlier_t)
        def _():
            ahead_t_copy().wait_send()
            for x in range(rows_x):
                behind_t_copy(x).wait_recv()
                pay_out[0, x] = pay_out[0, x] - behind_t[x]

        @pl.when(has_earlier_x)
        def _():
            for r in range(steps_t):
                ahead_x_copy(r).wait_send()
            for r in [steps_t - 1] + list(range(steps_t - 2)) + [steps_t - 2]:
                behind_x_copy(r).wait_recv()
                pay_out[r, 0] = pay_out[r, 0] - behind_x[r]

        @pl.when(has_later_x)
        def _():
            for r in range(steps_t):
                behind_x_copy(r).wait_send()

        @pl.when(has_later_t)
        def _():
            for x in range(rows_x):
                behind_t_copy(x).wait_send()


def cells(potential, multiplier, start_density, final_density, n_tm, n_sp):
    steps_t, rows_x, width_y, width_z = potential.shape
    idx = jnp.stack([lax.axis_index("tm"), lax.axis_index("space")]).astype(jnp.int32)
    slab = (1, rows_x, width_y, width_z)
    plane = (rows_x, width_y, width_z)
    f32 = jnp.float32
    grid_spec = pltpu.PrefetchScalarGridSpec(
        num_scalar_prefetch=1,
        grid=(steps_t,),
        in_specs=[
            pl.BlockSpec(slab, lambda i, s: (visit(i, steps_t), 0, 0, 0)),
            pl.BlockSpec(slab, lambda i, s: (jnp.minimum(visit(i, steps_t) + 1, steps_t - 1), 0, 0, 0)),
            pl.BlockSpec(memory_space=pl.ANY),
            pl.BlockSpec((4, 1, rows_x, width_y, width_z), lambda i, s: (0, visit(i, steps_t), 0, 0, 0)),
            pl.BlockSpec(plane, lambda t, s: (0, 0, 0)),
            pl.BlockSpec(plane, lambda t, s: (0, 0, 0)),
        ],
        out_specs=[
            pl.BlockSpec((4, 1, rows_x, width_y, width_z), lambda i, s: (0, visit(i, steps_t), 0, 0, 0)),
            pl.BlockSpec(potential.shape, lambda t, s: (0, 0, 0, 0)),
        ],
        scratch_shapes=[
            pltpu.VMEM((steps_t,) + plane, f32),
            pltpu.VMEM(plane, f32),
            pltpu.VMEM((steps_t, width_y, width_z), f32),
            pltpu.VMEM((steps_t, width_y, width_z), f32),
            pltpu.VMEM(plane, f32),
            pltpu.VMEM(plane, f32),
            pltpu.VMEM((steps_t, width_y, width_z), f32),
            pltpu.SemaphoreType.DMA((2,)),
            pltpu.SemaphoreType.DMA((2, steps_t)),
            pltpu.SemaphoreType.DMA((2, rows_x)),
            pltpu.SemaphoreType.DMA((2, steps_t)),
        ],
    )
    cells_n = potential.size
    return pl.pallas_call(
        functools.partial(cell_kernel, n_tm, n_sp),
        grid_spec=grid_spec,
        out_shape=[
            jax.ShapeDtypeStruct(multiplier.shape, f32),
            jax.ShapeDtypeStruct(potential.shape, f32),
        ],
        compiler_params=pltpu.CompilerParams(
            dimension_semantics=("arbitrary",), collective_id=0, has_side_effects=True
        ),
        cost_estimate=pl.CostEstimate(
            flops=cells_n * 200, transcendentals=cells_n * 11, bytes_accessed=cells_n * 4 * 12
        ),
    )(idx, potential, potential, potential, multiplier, start_density, final_density)

def body(potential, multiplier, start_density, final_density):
    high = lax.Precision.HIGH
    steps_t, rows_x, width_y, width_z = potential.shape
    n_tm = lax.axis_size("tm")
    n_sp = lax.axis_size("space")
    total_t = steps_t * n_tm
    total_x = rows_x * n_sp
    block_y = width_y // (n_tm * n_sp)
    time_at = lax.axis_index("tm") * steps_t + jnp.arange(steps_t)
    row_at = lax.axis_index("space") * rows_x + jnp.arange(rows_x)
    next_multiplier, partial = cells(
        potential, multiplier, start_density, final_density, n_tm, n_sp
    )
    cos_y = cosine_table(width_y)
    cos_z = cosine_table(width_z)
    payload = jnp.einsum("txyi,ki->txyk", partial, cos_z, precision=high)
    payload = jnp.einsum("txiz,ki->ktxz", payload, cos_y, precision=high)
    both = ("tm", "space")
    middle = lax.all_to_all(payload, both, split_axis=0, concat_axis=0, tiled=True)
    next_multiplier = jnp.where(next_multiplier == next_multiplier, next_multiplier, 0.0)
    middle, next_multiplier = lax.optimization_barrier((middle, next_multiplier))
    middle = middle.reshape(n_tm, n_sp, block_y, steps_t, rows_x, width_z)
    cos_t = cosine_table(total_t).reshape(total_t, n_tm, steps_t)
    cos_x = cosine_table(total_x).reshape(total_x, n_sp, rows_x)
    hat = jnp.einsum("kat,abytxz->kbxyz", cos_t, middle, precision=high)
    hat = jnp.einsum("jbx,kbxyz->kjyz", cos_x, hat, precision=high)
    freq_y = (
        (lax.axis_index("tm") * n_sp + lax.axis_index("space")) * block_y + jnp.arange(block_y)
    ).astype(jnp.float32)
    eig_t = eigen_at(total_t, jnp.arange(total_t, dtype=jnp.float32))
    eig_x = eigen_at(total_x, jnp.arange(total_x, dtype=jnp.float32))
    eig_y = eigen_at(width_y, freq_y)
    eig_z = eigen_at(width_z, jnp.arange(width_z, dtype=jnp.float32))
    denom = eig_t[:, None, None, None] + eig_x[None, :, None, None]
    denom = denom + eig_y[None, None, :, None] + eig_z[None, None, None, :]
    hat = hat / (RATE * denom + PROX)
    hat = jnp.einsum("atk,kjyz->atjyz", cos_t.reshape(n_tm, steps_t, total_t), hat, precision=high)
    solved = jnp.einsum("bxj,atjyz->abytxz", cos_x.reshape(n_sp, rows_x, total_x), hat, precision=high)
    solved = solved.reshape(n_tm * n_sp * block_y, steps_t, rows_x, width_z)
    local = lax.all_to_all(solved, both, split_axis=0, concat_axis=0, tiled=True)
    local = jnp.einsum("ik,ktxz->txiz", cos_y, local, precision=high)
    next_potential = jnp.einsum("ik,txyk->txyi", cos_z, local, precision=high)
    return (next_potential, next_multiplier)


def solution(mesh):
    in_specs = (
        P("tm", "space", None, None),
        P(None, "tm", "space", None, None),
        P("space", None, None),
        P("space", None, None),
    )
    out_specs = (P("tm", "space", None, None), P(None, "tm", "space", None, None))
    return jax.shard_map(body, mesh=mesh, in_specs=in_specs, out_specs=out_specs, check_vma=False)
```

```python
import functools

import jax
import jax.numpy as jnp
from jax import lax
from jax.sharding import PartitionSpec as P
from jax.experimental import pallas as pl
from jax.experimental.pallas import tpu as pltpu

NEWTON = 10


RATE = 4.0
PROX = 0.01


def from_behind(block, axis, distance):
    devices = range(lax.axis_size(axis))
    route = [(i - distance, i) for i in devices if i - distance in devices]
    return lax.ppermute(block, axis, route)


def cosine_table(length):
    freq = jnp.arange(length, dtype=jnp.float32)[:, None]
    place = jnp.arange(length, dtype=jnp.float32)[None, :]
    weight = jnp.where(freq == 0.0, jnp.sqrt(jnp.float32(0.5)), jnp.float32(1.0))
    return (
        jnp.sqrt(jnp.float32(2.0) / length)
        * weight
        * jnp.cos(jnp.pi * freq * (place + 0.5) / length)
    )


def eigen_at(length, freq):
    return 4.0 * jnp.square(jnp.sin(jnp.pi * freq / (2.0 * length)))


def adjoint(face, axis):
    size = face.shape[axis]
    inner = lax.slice_in_dim(face, 0, size - 1, axis=axis)
    edge = jnp.zeros_like(lax.slice_in_dim(face, 0, 1, axis=axis))
    return jnp.concatenate([edge, inner], axis=axis) - jnp.concatenate([inner, edge], axis=axis)


def local_diff(field, axis):
    size = field.shape[axis]
    upper = lax.slice_in_dim(field, 1, size, axis=axis)
    lower = lax.slice_in_dim(field, 0, size - 1, axis=axis)
    edge = jnp.zeros_like(lax.slice_in_dim(field, 0, 1, axis=axis))
    return jnp.concatenate([upper - lower, edge], axis=axis)


def project(target):
    lead = target[0]
    side = target[1:]
    wsq = jnp.sum(side * side, axis=0)
    excess = lead + 0.5 * wsq
    stretch = jnp.maximum(1.0, lead + 1.0)
    shifted = lead + 1.0
    half_again = 1.5 * wsq
    for step in range(NEWTON):
        square = stretch * stretch
        cube = square * stretch
        stretch = jnp.maximum(1.0, stretch * (shifted * square + half_again) / (cube + wsq))
    inside = excess <= 0.0
    new_lead = jnp.where(inside, lead, lead - (stretch - 1.0))
    shrink = 1.0 / stretch
    new_side = jnp.where(inside[None], side, side * shrink[None])
    return jnp.concatenate([new_lead[None], new_side], axis=0)


def visit(step, steps_t):
    return jnp.where(step < 1, step, jnp.where(step == 1, steps_t - 1, step - 1))


def cell_kernel(n_tm, n_sp, idx_ref, pc, pn, p_any, m, sd, fd, nm_out, pay_out,
                ft_store, ahead_t, ahead_x, send_x, send_t, behind_t, behind_x,
                at_sems, ax_sems, bt_sems, bx_sems):
    s = pl.program_id(0)
    steps_t = pl.num_programs(0)
    t = visit(s, steps_t)
    rows_x, width_y, width_z = pc.shape[1], pc.shape[2], pc.shape[3]
    tm = lax.axis_index("tm")
    sp = lax.axis_index("space")
    t_glob = tm * steps_t + t
    last_t = t_glob == n_tm * steps_t - 1
    has_later_t = tm < n_tm - 1
    has_earlier_t = tm > 0
    has_later_x = sp < n_sp - 1
    has_earlier_x = sp > 0
    mesh_id = pl.DeviceIdType.MESH

    def ahead_t_copy():
        return pltpu.make_async_remote_copy(
            p_any.at[0], ahead_t, at_sems.at[0], at_sems.at[1],
            device_id=(tm - 1, sp), device_id_type=mesh_id)

    def ahead_x_copy(row):
        return pltpu.make_async_remote_copy(
            p_any.at[row, 0], ahead_x.at[row], ax_sems.at[0, row], ax_sems.at[1, row],
            device_id=(tm, sp - 1), device_id_type=mesh_id)

    def behind_t_copy(x):
        return pltpu.make_async_remote_copy(
            send_t.at[x], behind_t.at[x], bt_sems.at[0, x], bt_sems.at[1, x],
            device_id=(tm + 1, sp), device_id_type=mesh_id)

    def behind_x_copy(row):
        return pltpu.make_async_remote_copy(
            send_x.at[row], behind_x.at[row], bx_sems.at[0, row], bx_sems.at[1, row],
            device_id=(tm, sp + 1), device_id_type=mesh_id)

    @pl.when(s == 0)
    def _():
        barrier = pltpu.get_barrier_semaphore()
        for cond, dev in ((has_earlier_t, (tm - 1, sp)), (has_later_t, (tm + 1, sp)),
                          (has_earlier_x, (tm, sp - 1)), (has_later_x, (tm, sp + 1))):
            @pl.when(cond)
            def _():
                pl.semaphore_signal(barrier, 1, device_id=dev, device_id_type=mesh_id)
        peers = (has_earlier_t.astype(jnp.int32) + has_later_t.astype(jnp.int32)
                 + has_earlier_x.astype(jnp.int32) + has_later_x.astype(jnp.int32))
        pl.semaphore_wait(barrier, peers)

        @pl.when(has_earlier_t)
        def _():
            ahead_t_copy().start()

        @pl.when(has_earlier_x)
        def _():
            rows = ahead_x.shape[0]
            for row in [0, rows - 1] + list(range(1, rows - 1)):
                ahead_x_copy(row).start()

    row = lax.broadcasted_iota(jnp.int32, (width_y, width_z), 0)
    col = lax.broadcasted_iota(jnp.int32, (width_y, width_z), 1)
    first_row = row == 0
    last_row = row == width_y - 1
    last_col = col == width_z - 1
    first_col = col == 0
    def rows_in(order):
        fx_done = {}
        for x in order:
            p = pc[0, x]
            if x == order[0]:
                @pl.when(jnp.logical_and(t == steps_t - 1, has_later_t))
                def _():
                    ahead_t_copy().wait_recv()
            nxt = lax.cond(t == steps_t - 1, lambda: ahead_t[x], lambda: pn[0, x])
            grad_t = jnp.where(last_t, 0.0, nxt - p)
            if x < rows_x - 1:
                grad_x = pc[0, x + 1] - p
            else:
                @pl.when(has_later_x)
                def _():
                    ahead_x_copy(t).wait_recv()
                grad_x = lax.cond(has_later_x, lambda: ahead_x[t] - p, lambda: jnp.zeros_like(p))
            grad_y = jnp.where(last_row, 0.0, pltpu.roll(p, width_y - 1, 0) - p)
            grad_z = jnp.where(last_col, 0.0, pltpu.roll(p, width_z - 1, 1) - p)
            grads = (grad_t, grad_x, grad_y, grad_z)
            mults = tuple(m[c, 0, x] for c in range(4))
            target = tuple(g + mu * (1.0 / RATE) for g, mu in zip(grads, mults))
            lead = target[0]
            wsq = target[1] * target[1] + target[2] * target[2] + target[3] * target[3]
            excess = lead + 0.5 * wsq
            shifted = lead + 1.0
            half_again = 1.5 * wsq
            stretch = jnp.maximum(1.0, shifted)
            for step in range(NEWTON):
                square = stretch * stretch
                cube = square * stretch
                stretch = jnp.maximum(1.0, stretch * (shifted * square + half_again) / (cube + wsq))
            inside = excess <= 0.0
            shrink = 1.0 / stretch
            proj = (jnp.where(inside, lead, lead - (stretch - 1.0)),) + tuple(
                jnp.where(inside, target[c], target[c] * shrink) for c in (1, 2, 3)
            )
            flux = []
            for c in range(4):
                nm = mults[c] + RATE * (grads[c] - proj[c])
                nm_out[c, 0, x] = nm
                flux.append(nm - RATE * proj[c])
            if x == rows_x - 1:
                send_x[t] = flux[1]

                @pl.when(has_later_x)
                def _():
                    behind_x_copy(t).start()

            @pl.when(t == steps_t - 1)
            def _():
                send_t[x] = flux[0]

                @pl.when(has_later_t)
                def _():
                    behind_t_copy(x).start()
            flow_y = jnp.where(first_row, 0.0, pltpu.roll(flux[2], 1, 0)) - jnp.where(last_row, 0.0, flux[2])
            flow_z = jnp.where(first_col, 0.0, pltpu.roll(flux[3], 1, 1)) - jnp.where(last_col, 0.0, flux[3])
            rest = PROX * p - (flow_y + flow_z)
            rest = rest + jnp.where(t_glob == 0, sd[x], 0.0) - jnp.where(last_t, fd[x], 0.0)
            has_prev = jnp.logical_and(t > 0, t < steps_t - 1)
            ft_prev = lax.cond(has_prev, lambda: ft_store[jnp.maximum(t - 1, 0), x], lambda: jnp.zeros_like(p))
            div_t = ft_prev - jnp.where(last_t, 0.0, flux[0])
            ft_store[t, x] = flux[0]
            if x < rows_x - 1:
                fx_cur = flux[1]
            else:
                fx_cur = jnp.where(has_later_x, flux[1], 0.0)
            value = rest - div_t + fx_cur
            if x - 1 in fx_done:
                value = value - fx_done[x - 1]
            pay_out[t, x] = value
            if x + 1 in fx_done:
                pay_out[t, x + 1] = pay_out[t, x + 1] - flux[1]
            fx_done[x] = flux[1]

    @pl.when(s == steps_t - 1)
    def _():
        rows_in([rows_x - 1] + list(range(rows_x - 1)))

    @pl.when(s < steps_t - 1)
    def _():
        rows_in(list(range(rows_x)))

    @pl.when(s == steps_t - 1)
    def _():
        for x in range(rows_x):
            pay_out[steps_t - 1, x] = pay_out[steps_t - 1, x] - ft_store[steps_t - 2, x]

        @pl.when(has_earlier_t)
        def _():
            for x in range(rows_x):
                behind_t_copy(x).wait_recv()
                pay_out[0, x] = pay_out[0, x] - behind_t[x]
            ahead_t_copy().wait_send()

        @pl.when(has_earlier_x)
        def _():
            for r in range(steps_t):
                ahead_x_copy(r).wait_send()
            for r in [steps_t - 1] + list(range(steps_t - 2)) + [steps_t - 2]:
                behind_x_copy(r).wait_recv()
                pay_out[r, 0] = pay_out[r, 0] - behind_x[r]

        @pl.when(has_later_x)
        def _():
            for r in range(steps_t):
                behind_x_copy(r).wait_send()

        @pl.when(has_later_t)
        def _():
            for x in range(rows_x):
                behind_t_copy(x).wait_send()


def cells(potential, multiplier, start_density, final_density, n_tm, n_sp):
    steps_t, rows_x, width_y, width_z = potential.shape
    idx = jnp.stack([lax.axis_index("tm"), lax.axis_index("space")]).astype(jnp.int32)
    slab = (1, rows_x, width_y, width_z)
    plane = (rows_x, width_y, width_z)
    f32 = jnp.float32
    grid_spec = pltpu.PrefetchScalarGridSpec(
        num_scalar_prefetch=1,
        grid=(steps_t,),
        in_specs=[
            pl.BlockSpec(slab, lambda i, s: (visit(i, steps_t), 0, 0, 0)),
            pl.BlockSpec(slab, lambda i, s: (jnp.minimum(visit(i, steps_t) + 1, steps_t - 1), 0, 0, 0)),
            pl.BlockSpec(memory_space=pl.ANY),
            pl.BlockSpec((4, 1, rows_x, width_y, width_z), lambda i, s: (0, visit(i, steps_t), 0, 0, 0)),
            pl.BlockSpec(plane, lambda t, s: (0, 0, 0)),
            pl.BlockSpec(plane, lambda t, s: (0, 0, 0)),
        ],
        out_specs=[
            pl.BlockSpec((4, 1, rows_x, width_y, width_z), lambda i, s: (0, visit(i, steps_t), 0, 0, 0)),
            pl.BlockSpec(potential.shape, lambda t, s: (0, 0, 0, 0)),
        ],
        scratch_shapes=[
            pltpu.VMEM((steps_t,) + plane, f32),
            pltpu.VMEM(plane, f32),
            pltpu.VMEM((steps_t, width_y, width_z), f32),
            pltpu.VMEM((steps_t, width_y, width_z), f32),
            pltpu.VMEM(plane, f32),
            pltpu.VMEM(plane, f32),
            pltpu.VMEM((steps_t, width_y, width_z), f32),
            pltpu.SemaphoreType.DMA((2,)),
            pltpu.SemaphoreType.DMA((2, steps_t)),
            pltpu.SemaphoreType.DMA((2, rows_x)),
            pltpu.SemaphoreType.DMA((2, steps_t)),
        ],
    )
    cells_n = potential.size
    return pl.pallas_call(
        functools.partial(cell_kernel, n_tm, n_sp),
        grid_spec=grid_spec,
        out_shape=[
            jax.ShapeDtypeStruct(multiplier.shape, f32),
            jax.ShapeDtypeStruct(potential.shape, f32),
        ],
        compiler_params=pltpu.CompilerParams(
            dimension_semantics=("arbitrary",), collective_id=0, has_side_effects=True
        ),
        cost_estimate=pl.CostEstimate(
            flops=cells_n * 200, transcendentals=cells_n * 11, bytes_accessed=cells_n * 4 * 12
        ),
    )(idx, potential, potential, potential, multiplier, start_density, final_density)

def body(potential, multiplier, start_density, final_density):
    high = lax.Precision.HIGH
    steps_t, rows_x, width_y, width_z = potential.shape
    n_tm = lax.axis_size("tm")
    n_sp = lax.axis_size("space")
    total_t = steps_t * n_tm
    total_x = rows_x * n_sp
    block_y = width_y // (n_tm * n_sp)
    time_at = lax.axis_index("tm") * steps_t + jnp.arange(steps_t)
    row_at = lax.axis_index("space") * rows_x + jnp.arange(rows_x)
    next_multiplier, partial = cells(
        potential, multiplier, start_density, final_density, n_tm, n_sp
    )
    cos_y = cosine_table(width_y)
    cos_z = cosine_table(width_z)
    payload = jnp.einsum("txyi,ki->txyk", partial, cos_z, precision=high)
    payload = jnp.einsum("txiz,ki->ktxz", payload, cos_y, precision=high)
    both = ("tm", "space")
    middle = lax.all_to_all(payload, both, split_axis=0, concat_axis=0, tiled=True)
    next_multiplier = jnp.where(next_multiplier == next_multiplier, next_multiplier, 0.0)
    middle, next_multiplier = lax.optimization_barrier((middle, next_multiplier))
    middle = middle.reshape(n_tm, n_sp, block_y, steps_t, rows_x, width_z)
    cos_t = cosine_table(total_t).reshape(total_t, n_tm, steps_t)
    cos_x = cosine_table(total_x).reshape(total_x, n_sp, rows_x)
    hat = jnp.einsum("kat,abytxz->kbxyz", cos_t, middle, precision=high)
    hat = jnp.einsum("jbx,kbxyz->kjyz", cos_x, hat, precision=high)
    freq_y = (
        (lax.axis_index("tm") * n_sp + lax.axis_index("space")) * block_y + jnp.arange(block_y)
    ).astype(jnp.float32)
    eig_t = eigen_at(total_t, jnp.arange(total_t, dtype=jnp.float32))
    eig_x = eigen_at(total_x, jnp.arange(total_x, dtype=jnp.float32))
    eig_y = eigen_at(width_y, freq_y)
    eig_z = eigen_at(width_z, jnp.arange(width_z, dtype=jnp.float32))
    denom = eig_t[:, None, None, None] + eig_x[None, :, None, None]
    denom = denom + eig_y[None, None, :, None] + eig_z[None, None, None, :]
    hat = hat / (RATE * denom + PROX)
    hat = jnp.einsum("atk,kjyz->atjyz", cos_t.reshape(n_tm, steps_t, total_t), hat, precision=high)
    solved = jnp.einsum("bxj,atjyz->abytxz", cos_x.reshape(n_sp, rows_x, total_x), hat, precision=high)
    solved = solved.reshape(n_tm * n_sp * block_y, steps_t, rows_x, width_z)
    local = lax.all_to_all(solved, both, split_axis=0, concat_axis=0, tiled=True)
    local = jnp.einsum("ik,ktxz->txiz", cos_y, local, precision=high)
    next_potential = jnp.einsum("ik,txyk->txyi", cos_z, local, precision=high)
    return (next_potential, next_multiplier)


def solution(mesh):
    in_specs = (
        P("tm", "space", None, None),
        P(None, "tm", "space", None, None),
        P("space", None, None),
        P("space", None, None),
    )
    out_specs = (P("tm", "space", None, None), P(None, "tm", "space", None, None))
    return jax.shard_map(body, mesh=mesh, in_specs=in_specs, out_specs=out_specs, check_vma=False)
```
